32 devices in a mesh: group: 4 (over z), seq: 4 (over x, core), tensor: 2 (over y).
Axes of the slice: x: 2, y: 2, z: 4, core: 2. Of those that a mesh axis runs over, the one named last changes fastest.
Arguments:
- queries: bfloat16 [4, 1024, 4096], P('group', 'seq', 'tensor'), as said below
- suffix_kv: bfloat16 [4, 1024, 2048], P('group', 'seq', 'tensor'), may hold values from -15 to 15
- suffix_seg: int32 [4, 1024], P('group', 'seq'), may hold values from 0 to 3, never falling along the last dimension, each value on 1 to 512 neighbouring positions
- prefix_pool: bfloat16 [4, 64, 128, 2048], P('group', 'seq', None, 'tensor'), as said below
- page_table: int32 [2, 32], P(None, 'seq'), may hold values from 0 to 15, as said below
- owner: int32 [2], replicated, may hold values from 0 to 3, as said below
- group_of: int32 [4], P('group'), may hold values from 0 to 1, as said below
Outputs:
- attention: bfloat16 [4, 1024, 4096], P('group', 'seq', 'tensor')
The draws below stay inside these ranges and needn't reach their ends.
Inputs may be any that keep to these rules, and one draw needn't show every extreme that they name: `queries`: of order one except in a few rows, which may be as large as 10 in every entry. `prefix_pool`: entries of order 2.5. `page_table`: within a row, the 8 entries of each index of seq are distinct. `owner`: Distinct. `group_of`: every request group is served by exactly two group indices.
All inputs are finite; a program needn't handle non-finite values.
Results may differ from the reference program's by a relative error of at most 0.0044.
Values may be sent and summed in bfloat16 or wider, within the bound.
A program may use at most 128 MiB of HBM per device.

```python
import math
import jax
import jax.numpy as jnp
import numpy as np
from jax import lax

Q_HEADS = 32
KV_HEADS = 8
HEAD = 128
PAGE = 128
REQS = 4
PG_DEV = 8
POOL = 16
PREFIX = 4096
SUF = 1024
MOST = 512
RG = 2
N_GROUP = 4
N_SEQ = 4


def draw_queries(key, part):
    shape = (N_GROUP, SUF, Q_HEADS * HEAD)
    values = jnp.clip(jax.random.normal(jax.random.fold_in(key, 11), shape, jnp.float32), -6.0, 6.0)
    return values.astype(jnp.bfloat16)


def draw_prefix_pool(key, part):
    shape = (N_GROUP, N_SEQ * POOL, PAGE, KV_HEADS * 2 * HEAD)
    values = 2.5 * jnp.clip(jax.random.normal(jax.random.fold_in(key, 13), shape, jnp.float32), -6.0, 6.0)
    return values.astype(jnp.bfloat16)


def draw_page_table(key, part):

    def one_row(row_key):
        return jax.random.permutation(row_key, POOL)[:PG_DEV].astype(jnp.int32)

    def ends_row(row_key):
        inner = (1 + jax.random.permutation(jax.random.fold_in(row_key, 1), POOL - 2)[:PG_DEV - 2]).astype(jnp.int32)
        full_row = jnp.concatenate([jnp.array([0, POOL - 1], jnp.int32), inner])
        order = jax.random.permutation(jax.random.fold_in(row_key, 2), PG_DEV)
        return full_row[order].astype(jnp.int32)
    row_keys = jax.random.split(jax.random.fold_in(key, 21), RG * N_SEQ)
    drawn_rows = jax.vmap(one_row)(row_keys)
    first_row = ends_row(jax.random.fold_in(key, 22))
    row_ids = jnp.arange(RG * N_SEQ, dtype=jnp.int32)
    rows_all = jnp.where((row_ids == 0)[:, None], first_row[None, :], drawn_rows)
    return rows_all.reshape(RG, N_SEQ * PG_DEV).astype(jnp.int32)


def draw_owner(key, part):
    return jax.random.permutation(jax.random.fold_in(key, 31), N_GROUP)[:RG].astype(jnp.int32)


def draw_group_of(key, part):
    return (jax.random.permutation(jax.random.fold_in(key, 41), N_GROUP) // 2).astype(jnp.int32)


def steps_of(own_key, dims, cuts, low, high):
    def one(axis_at, shards_of):
        draws = jax.random.uniform(jax.random.fold_in(jax.random.fold_in(own_key, 6), axis_at), (shards_of,), jnp.float32, low / len(cuts), high / len(cuts))
        return jnp.repeat(jnp.exp(draws), dims[axis_at] // shards_of).reshape((-1,) + (1,) * (len(dims) - axis_at - 1))

    gain = one(*cuts[0])
    for cut in cuts[1:]:
        gain = gain * one(*cut)
    return gain


def length_profile(amount, total, reach, lean):
    portions = [(1 << 20) // math.isqrt(rank ** lean) + 1 for rank in range(2, amount + 1)]
    surplus, given = total - reach - (amount - 1), [1] * (amount - 1)
    while surplus > 0:
        free = [i for i in range(amount - 1) if given[i] < reach]
        pool, budget = sum([portions[i] for i in free]), surplus
        for i in free:
            extra = min(reach - given[i], max(1, budget * portions[i] // pool), surplus)
            given[i] = given[i] + extra
            surplus = surplus - extra
    return np.array([reach] + given)


def ragged(stream_key, number_of, total, bound, lean):
    if number_of == 2:
        one = jax.random.randint(stream_key, (), max(1, total - bound), min(bound, total - 1) + 1)
        return jnp.stack([one, total - one])
    tallies = jnp.asarray(length_profile(number_of, total, bound, lean), jnp.int32)
    couples = (number_of - 1) // 2
    source_of, receiver = tallies[1:1 + 2 * couples:2], tallies[2:2 + 2 * couples:2]
    margin = jnp.minimum(source_of - 1, bound - receiver)
    moved = jax.random.randint(jax.random.fold_in(stream_key, 1), (couples,), 0, 1 << 20) % (margin + 1)
    tallies = tallies.at[1:1 + 2 * couples:2].set(source_of - moved).at[2:2 + 2 * couples:2].set(receiver + moved)
    return tallies[jax.random.permutation(jax.random.fold_in(stream_key, 2), number_of)]


def bell_draw(own_key, dims, deviation, limit, cuts=(), kind=jnp.bfloat16):
    values = jax.random.normal(own_key, dims, jnp.float32) * deviation
    if len(cuts) > 0:
        values = steps_of(own_key, dims, cuts, -0.22, 0.18) * values
    return jnp.clip(values, min=-limit, max=limit).astype(kind)


def setup_inputs(seed: int = 0) -> dict:
    streams_of = jax.random.split(jax.random.key(seed), 8)
    return {
        "queries": draw_queries(jax.random.fold_in(streams_of[7], 71), 0),
        "suffix_kv": bell_draw(streams_of[1], (N_GROUP, SUF, KV_HEADS * 2 * HEAD), 2.5, 15.0, ((0, 4), (1, 4), (2, 2))),
        "suffix_seg": jax.vmap(lambda own: jnp.searchsorted(jnp.cumsum(ragged(own, REQS, SUF, MOST, 2)), jnp.arange(SUF), side="right"))(jax.random.split(streams_of[2], N_GROUP)).reshape((N_GROUP, SUF)).astype(jnp.int32),
        "prefix_pool": draw_prefix_pool(jax.random.fold_in(streams_of[7], 71), 0),
        "page_table": draw_page_table(jax.random.fold_in(streams_of[7], 71), 0),
        "owner": draw_owner(jax.random.fold_in(streams_of[7], 71), 0),
        "group_of": draw_group_of(jax.random.fold_in(streams_of[7], 71), 0),
    }


NEG_FILL = -1e+30

def reference(queries, suffix_kv, suffix_seg, prefix_pool, page_table, owner, group_of):
    row_width = prefix_pool.shape[-1]
    head_count = row_width // (2 * HEAD)
    group_size = queries.shape[-1] // (head_count * HEAD)
    scale = 1.0 / math.sqrt(HEAD)
    pool_all = prefix_pool.reshape(N_GROUP, N_SEQ, POOL, PAGE, row_width)

    def one_group(group_index):
        request = group_of[group_index]
        source = owner[request]
        slot_ids = page_table[request].reshape(N_SEQ, PG_DEV)
        owner_pool = pool_all[source]
        pages = jax.vmap(lambda pool_rows, slot_row: pool_rows[slot_row])(owner_pool, slot_ids)
        prefix_rows = pages.reshape(PREFIX, row_width)
        kv_rows = jnp.concatenate([prefix_rows, suffix_kv[group_index]], 0).reshape(-1, head_count, 2, HEAD)
        query_rows = queries[group_index].reshape(SUF, head_count, group_size, HEAD)
        segment = suffix_seg[group_index]
        position = jnp.arange(SUF, dtype=jnp.int32)
        suffix_seen = (segment[None, :] == segment[:, None]) & (position[None, :] <= position[:, None])
        visible = jnp.concatenate([jnp.ones((SUF, PREFIX), dtype=bool), suffix_seen], 1)

        def one_head(head_index):
            query_head = query_rows[:, head_index].astype(jnp.float32)
            key_head = kv_rows[:, head_index, 0].astype(jnp.float32)
            value_head = kv_rows[:, head_index, 1].astype(jnp.float32)
            scores = jnp.einsum('tgd,kd->tgk', query_head, key_head) * scale
            scores = jnp.where(visible[:, None, :], scores, NEG_FILL)
            row_max = lax.optimization_barrier(jnp.max(scores, axis=-1, keepdims=True))
            weights = jnp.where(visible[:, None, :], jnp.exp(scores - row_max), 0.0)
            totals = lax.optimization_barrier(jnp.sum(weights, axis=-1, keepdims=True))
            weights_b = lax.optimization_barrier(weights.astype(jnp.bfloat16))
            context = jnp.einsum('tgk,kd->tgd', weights_b.astype(jnp.float32), value_head)
            return context / totals
        heads_out = lax.map(one_head, jnp.arange(head_count))
        return heads_out.transpose(1, 0, 2, 3).reshape(SUF, -1).astype(jnp.bfloat16)
    return lax.map(one_group, jnp.arange(N_GROUP))
```

```python
import functools
import math

import jax
import jax.numpy as jnp
from jax import lax
from jax.experimental import pallas as pl
from jax.experimental.pallas import tpu as pltpu
from jax.sharding import PartitionSpec as P

HEAD = 128


NEG_FILL = -1e30


def broadcast(value, axis, root):
    mine = lax.axis_index(axis) == root
    return lax.psum(jnp.where(mine, value, jnp.zeros_like(value)), axis)


def absorb(carried, query_rows, key_block, valid):
    running_max, running_sum, accumulator = carried
    scale = 1.0 / math.sqrt(HEAD)
    key_rows = key_block[:, :, 0, :]
    value_rows = key_block[:, :, 1, :]
    scores = (
        jnp.einsum("thgd,khd->htgk", query_rows, key_rows, preferred_element_type=jnp.float32)
        * scale
    )
    if valid is not None:
        scores = jnp.where(valid[None, :, None, :], scores, NEG_FILL)
    new_max = jnp.maximum(running_max, jnp.max(scores, axis=-1, keepdims=True))
    weight = jnp.exp(scores - new_max)
    if valid is not None:
        weight = jnp.where(valid[None, :, None, :], weight, 0.0)
    factor = jnp.exp(running_max - new_max)
    running_sum = running_sum * factor + jnp.sum(weight, axis=-1, keepdims=True)
    accumulator = accumulator * factor + jnp.einsum(
        "htgk,khd->htgd",
        weight.astype(jnp.bfloat16),
        value_rows,
        preferred_element_type=jnp.float32,
    )
    return (new_max, running_sum, accumulator)


def sweep(carried, query_rows, kv_rows, mask_for):
    row_count = kv_rows.shape[0]
    block_rows = math.gcd(row_count, 1024)
    head_count = kv_rows.shape[1] // (2 * HEAD)

    def absorb_block(block_index, state_now):
        offset = block_index * block_rows
        key_block = lax.dynamic_slice_in_dim(kv_rows, offset, block_rows, 0).reshape(
            block_rows, head_count, 2, HEAD
        )
        return absorb(state_now, query_rows, key_block, mask_for(offset, block_rows))

    if row_count == block_rows:
        return absorb_block(0, carried)
    return lax.fori_loop(0, row_count // block_rows, absorb_block, carried)


def combine(earlier, later):
    new_max = jnp.maximum(earlier[0], later[0])
    scale_first = jnp.exp(earlier[0] - new_max)
    scale_second = jnp.exp(later[0] - new_max)
    return (
        new_max,
        earlier[1] * scale_first + later[1] * scale_second,
        earlier[2] * scale_first + later[2] * scale_second,
    )


def no_mask(offset, block_rows):
    return None


def local(queries, suffix_kv, suffix_seg, prefix_pool, page_table, owner, group_of):
    tokens = queries.shape[1]
    row_width = suffix_kv.shape[-1]
    head_count = row_width // (2 * HEAD)
    group_size = queries.shape[-1] // (head_count * HEAD)
    query_rows = queries[0].reshape(tokens, head_count, group_size, HEAD)
    page_pool = prefix_pool[0]
    my_group = group_of[0]
    held_shape = (page_table.shape[1] * page_pool.shape[1], row_width)

    def compact(slot_ids):
        def put(j, rows):
            page = lax.dynamic_slice_in_dim(page_pool, slot_ids[j], 1, 0)
            return lax.dynamic_update_slice_in_dim(rows, page, j, 0)

        count = slot_ids.shape[0]
        rows = jnp.zeros((count,) + page_pool.shape[1:], page_pool.dtype)
        return lax.fori_loop(0, count, put, rows).reshape(-1, row_width)

    def visit_group(request, held_pages):
        moved_pages = broadcast(compact(page_table[request]), "group", owner[request])
        return jnp.where(request == my_group, moved_pages, held_pages)

    prefix_rows = lax.fori_loop(
        0, page_table.shape[0], visit_group, jnp.zeros(held_shape, jnp.bfloat16)
    )
    fresh_state = (
        jnp.full((head_count, tokens, group_size, 1), NEG_FILL, jnp.float32),
        jnp.zeros((head_count, tokens, group_size, 1), jnp.float32),
        jnp.zeros((head_count, tokens, group_size, HEAD), jnp.float32),
    )
    before = sweep(
        fresh_state, query_rows, lax.all_gather(prefix_rows, "seq", axis=0, tiled=True), no_mask
    )
    first_row = lax.axis_index("seq") * tokens
    query_pos = first_row + jnp.arange(tokens, dtype=jnp.int32)
    query_seg = suffix_seg[0]
    first_index = jnp.int32(0)
    kv_rows = lax.all_gather(suffix_kv[0], "seq", axis=0, tiled=True)
    key_segments = lax.all_gather(suffix_seg[0], "seq", axis=0, tiled=True)

    def mask_for(offset, block_rows):
        block_seg = lax.dynamic_slice_in_dim(key_segments, offset, block_rows, 0)
        key_pos = first_index + offset + jnp.arange(block_rows, dtype=jnp.int32)
        return (block_seg[None, :] == query_seg[:, None]) & (key_pos[None, :] <= query_pos[:, None])

    combined = sweep(fresh_state, query_rows, kv_rows, mask_for)
    final_state = combine(before, combined)
    outcome = final_state[2] / final_state[1]
    return outcome.transpose(1, 0, 2, 3).reshape(1, tokens, -1).astype(jnp.bfloat16)

MESH = pl.DeviceIdType.MESH
EXP2_SCALE = math.log2(math.e) / math.sqrt(HEAD)


def choose(flag, first, second):
    return lax.select(flag != 0, first, second)


def fused_kernel(
    lanes, heads, group_size,
    owner, group_of, pages, queries, suffix, seg_row, pool,
    out,
    own, mate, sg, qseg, wants, wanted,
    right_in, left_in, right_out, left_out, kv, skv, qs, bias,
    score_0, score_1, weight_0, weight_1, factor_0, factor_1,
    m_ref, l_ref, acc, spare,
    sem_right_s, sem_right_r, sem_left_s, sem_left_r, sem_x_s, sem_x_r,
    sem_mate_s, sem_mate_r, sem_q_s, sem_q_r, sem_skv_s, sem_skv_r,
    sem_xskv_s, sem_xskv_r, sem_sg_s, sem_sg_r, sem_want_s, sem_want_r,
    sem_out_s, sem_out_r,
):
    z = lax.axis_index("group")
    s = lax.axis_index("seq")
    x = s // 2
    c = lax.rem(s, 2)
    chunks, rows = own.shape[:2]
    mine = heads // 2
    tokens = queries.shape[0]
    width = mine * group_size * HEAD
    pair = 2 * HEAD
    partner = s + 1 - 2 * c
    across = lax.rem(s + 2, 4)
    mid = (z == 1) | (z == 2)
    per_head = chunks // mine
    half = per_head // 2

    owner_0, owner_1, want = owner[0], owner[1], group_of[0]
    owner_mine = jnp.where(want == 1, owner_1, owner_0)

    wanted[...] = jnp.zeros_like(wanted)
    barrier = pltpu.get_barrier_semaphore()
    for there in (partner, across):
        pl.semaphore_signal(barrier, inc=1, device_id={"seq": there}, device_id_type=MESH)

    @pl.when(z > 0)
    def _():
        pl.semaphore_signal(barrier, inc=1, device_id={"group": z - 1}, device_id_type=MESH)

    @pl.when(z < 3)
    def _():
        pl.semaphore_signal(barrier, inc=1, device_id={"group": z + 1}, device_id_type=MESH)

    wants[...] = jnp.broadcast_to(want, wants.shape)
    sg[0, c] = jnp.broadcast_to(seg_row[...], sg.shape[2:])
    qs[c] = queries[:, pl.ds(pl.multiple_of(c * width, HEAD), width)]

    owned = jnp.where(owner_1 == z, 1, 0)
    page = pool.shape[1]
    in_part = rows // page

    def columns(core, h):
        return pl.ds(pl.multiple_of((core * mine + h) * pair, pair), pair)

    @pl.loop(0, pages.shape[1])
    def _(j):
        slot = pages[owned, j]
        place = pl.ds(pl.multiple_of(lax.rem(j, in_part) * page, page), page)
        for h in range(mine):
            own[h * per_head + j // in_part, place, :] = pool[slot, :, columns(c, h)]
            mate[h * half + j // in_part, place, :] = pool[slot, :, columns(1 - c, h)]

    for h in range(mine):
        skv[0, h, c] = suffix[:, columns(c, h)]

    pl.semaphore_wait(barrier, jnp.where(mid, 4, 3))

    def move(src, dst, send, recv, axis, there):
        return pltpu.make_async_remote_copy(
            src_ref=src, dst_ref=dst, send_sem=send, recv_sem=recv,
            device_id={axis: there}, device_id_type=MESH,
        )

    def right(lane, k, src=None):
        return move(
            right_out.at[lane, k] if src is None else src, right_in.at[lane, k],
            sem_right_s.at[lane, k], sem_right_r.at[lane, k], "group", lax.rem(z + 1, 4),
        )

    def left(lane, k, src=None):
        return move(
            left_out.at[lane, k] if src is None else src, left_in.at[lane, k],
            sem_left_s.at[lane, k], sem_left_r.at[lane, k], "group", lax.rem(z + 3, 4),
        )

    def cross(k):
        return move(kv.at[k, 0], kv.at[k, 1], sem_x_s.at[k], sem_x_r.at[k], "seq", across)

    def mate_copy(e):
        to = e // half * per_head + half + lax.rem(e, half)
        return move(
            mate.at[e], own.at[to], sem_mate_s.at[e], sem_mate_r.at[e], "seq", partner
        )

    def query_copy():
        cols = pl.ds(pl.multiple_of((1 - c) * width, HEAD), width)
        return move(queries.at[:, cols], qs.at[c], sem_q_s, sem_q_r, "seq", partner)

    def suffix_copy(h):
        return move(
            suffix.at[:, columns(1 - c, h)], skv.at[0, h, c],
            sem_skv_s.at[h], sem_skv_r.at[h], "seq", partner,
        )

    def suffix_cross(h):
        return move(
            skv.at[0, h], skv.at[1, h], sem_xskv_s.at[h], sem_xskv_r.at[h], "seq", across
        )

    def seg_copy():
        return move(sg.at[0, c], sg.at[0, c], sem_sg_s.at[0], sem_sg_r.at[0], "seq", partner)

    def seg_cross():
        return move(sg.at[0], sg.at[1], sem_sg_s.at[1], sem_sg_r.at[1], "seq", across)

    def want_copy(there):
        return move(wants, wanted, sem_want_s, sem_want_r, "group", there)

    def out_copy(h):
        cols = pl.ds(
            pl.multiple_of((c * mine + h) * group_size * HEAD, HEAD), group_size * HEAD
        )
        return move(
            spare.at[h], out.at[:, cols], sem_out_s.at[h], sem_out_r.at[h], "seq", partner
        )

    def from_edge(first, last):
        @pl.when(z == 0)
        def _():
            @pl.loop(first, last)
            def _(k):
                right(0, k, own.at[k]).start()

        @pl.when(z == 3)
        def _():
            @pl.loop(first, last)
            def _(k):
                left(0, k, own.at[k]).start()

    @pl.when((z == 0) | (z == 3))
    def _():
        want_copy(jnp.where(z == 0, 1, 2)).start()

    from_edge(0, half)
    seg_copy().start()
    for h in range(mine):
        suffix_copy(h).start()
    query_copy().start()

    @pl.loop(0, mine * half)
    def _(e):
        mate_copy(e).start()

    seg_copy().wait_recv()
    for h in range(mine):
        suffix_copy(h).wait_recv()

    @pl.when(x == 0)
    def _():
        seg_cross().start()
        for h in range(mine):
            suffix_cross(h).start()

    @pl.loop(0, mine * half)
    def _(e):
        mate_copy(e).wait_recv()

    from_edge(half, chunks)
    for a in range(2):
        qseg[a] = jnp.broadcast_to(sg[0, a, :1, :], (HEAD, tokens)).T
    query_copy().wait_recv()

    scores, weights, factors = (
        (score_0, score_1), (weight_0, weight_1), (factor_0, factor_1)
    )

    def attend(h, tiles, count, block, init, masks):
        def place(tile):
            return (h * 2 + tile[0]) * group_size + tile[1]

        def multiply(t):
            a, i = tiles[t]
            col = pl.multiple_of((h * group_size + i) * HEAD, HEAD)
            scores[t % 2][:, :count] = lax.dot_general(
                qs[a, :, pl.ds(col, HEAD)], block()[:, :HEAD],
                (((1,), (1,)), ((), ())), preferred_element_type=jnp.float32,
            )

        def soften(t):
            sc = scores[t % 2][:, :count]
            if masks is not None:
                sc = jnp.minimum(sc, masks[tiles[t][0]])
            at = place(tiles[t])
            top = jnp.broadcast_to(jnp.max(sc, axis=1, keepdims=True), (tokens, HEAD))
            if not init:
                old = m_ref[at]
                top = jnp.maximum(old, top)
                factors[t % 2][...] = jnp.exp2((old - top) * EXP2_SCALE)
            m_ref[at] = top
            w = jnp.exp2((sc - top[:, :1]) * EXP2_SCALE)
            weights[t % 2][:, :count] = w.astype(jnp.bfloat16)

        def gather(t):
            at = place(tiles[t])
            values = jnp.concatenate(
                [block()[:, HEAD:], jnp.ones((count, HEAD), jnp.bfloat16)], axis=1
            )
            add = jnp.dot(
                weights[t % 2][:, :count], values, preferred_element_type=jnp.float32
            )
            if init:
                acc[at] = add[:, :HEAD]
                l_ref[at] = add[:, HEAD:]
            else:
                factor = factors[t % 2][...]
                acc[at] = acc[at] * factor + add[:, :HEAD]
                l_ref[at] = l_ref[at] * factor + add[:, HEAD:]

        multiply(0)
        for t in range(len(tiles)):
            if t + 1 < len(tiles):
                multiply(t + 1)
            if t > 0:
                gather(t - 1)
            soften(t)
        gather(len(tiles) - 1)

    def set_bias(side):
        for a in range(2):
            k_seg = jnp.concatenate([sg[side, b, :1, :] for b in range(2)], axis=1)
            seen = k_seg == qseg[a][:, :1]
            if side == 0:
                q_off = a * tokens + lax.broadcasted_iota(jnp.int32, seen.shape, 0)
                seen = seen & (lax.broadcasted_iota(jnp.int32, seen.shape, 1) <= q_off)
            bias[a] = jnp.where(seen, jnp.inf, NEG_FILL)

    def attend_suffix(side, h):
        attend(
            h, [(a, i) for a in range(2) for i in range(group_size)], 2 * tokens,
            lambda: skv[side, h].reshape(2 * tokens, pair), side == 0, (bias[0], bias[1]),
        )

    def attend_prefix(part):
        unit = part // 2
        h = unit // (per_head // 2)
        a = lax.rem(part + 1 + c, 2)
        attend(
            h, [(a, i) for i in range(group_size)], 4 * rows,
            lambda: kv[pl.ds(2 * unit, 2)].reshape(4 * rows, pair), False, None,
        )

        @pl.when(lax.rem(unit, per_head // 2) == per_head // 2 - 1)
        def _():
            def ratio(i):
                at = (h * 2 + a) * group_size + i
                return (acc[at] / l_ref[at]).astype(out.dtype)

            @pl.when(a != c)
            def _():
                for i in range(group_size):
                    spare[h, :, i * HEAD : (i + 1) * HEAD] = ratio(i)
                out_copy(h).start()

            @pl.when(a == c)
            def _():
                for i in range(group_size):
                    col = ((c * mine + h) * group_size + i) * HEAD
                    out[:, pl.ds(pl.multiple_of(col, HEAD), HEAD)] = ratio(i)

    depth = jnp.maximum(z, 3 - z)
    lag = 2 + 4 * x
    is_mine = (owner_mine == z).astype(jnp.int32)
    from_left = (owner_mine < z).astype(jnp.int32)
    in_lane_1 = (want == 1).astype(jnp.int32)

    def sent_on(lane):
        if lanes == 1:
            return ((owner_0 == z) | (owner_1 == z)).astype(jnp.int32)
        return ((owner_0, owner_1)[lane] == z).astype(jnp.int32)

    @pl.when(mid)
    def _():
        want_copy(jnp.where(z == 1, 0, 3)).wait_recv()

    edge_want = jnp.max(wanted[...])
    edge_owned = (jnp.where(edge_want == 1, owner_1, owner_0) == z).astype(jnp.int32)

    set_bias(0)

    def step(i, carry):
        k_right = i - z

        @pl.when(mid & (k_right >= 0) & (k_right < chunks))
        def _():
            k = k_right

            @pl.when(z == 1)
            def _():
                right(0, k).wait_recv()
                for lane in range(lanes):
                    right_out[lane, k] = choose(sent_on(lane), own[k], right_in[0, k])
                    right(lane, k).start()

            @pl.when(z == 2)
            def _():
                for lane in range(lanes):
                    right(lane, k).wait_recv()
                got = right_in[0, k]
                if lanes > 1:
                    got = choose(edge_want, right_in[1, k], got)
                right_out[0, k] = choose(edge_owned, own[k], got)
                right(0, k).start()

        k_left = i - (3 - z)

        @pl.when(mid & (k_left >= 0) & (k_left < chunks))
        def _():
            k = k_left

            @pl.when(z == 2)
            def _():
                left(0, k).wait_recv()
                for lane in range(lanes):
                    left_out[lane, k] = choose(sent_on(lane), own[k], left_in[0, k])
                    left(lane, k).start()

            @pl.when(z == 1)
            def _():
                for lane in range(lanes):
                    left(lane, k).wait_recv()
                got = left_in[0, k]
                if lanes > 1:
                    got = choose(edge_want, left_in[1, k], got)
                left_out[0, k] = choose(edge_owned, own[k], got)
                left(0, k).start()

        k_mine = i - depth

        @pl.when((k_mine >= 0) & (k_mine < chunks))
        def _():
            k = k_mine

            @pl.when(z == 0)
            def _():
                left(0, k).wait_recv()
                kv[k, 0] = choose(is_mine, own[k], left_in[0, k])

            @pl.when(z == 3)
            def _():
                right(0, k).wait_recv()
                kv[k, 0] = choose(is_mine, own[k], right_in[0, k])

            @pl.when(z == 1)
            def _():
                came = left_in[0, k]
                if lanes > 1:
                    came = choose(in_lane_1, left_in[1, k], came)
                came = choose(from_left, right_in[0, k], came)
                kv[k, 0] = choose(is_mine, own[k], came)

            @pl.when(z == 2)
            def _():
                came = right_in[0, k]
                if lanes > 1:
                    came = choose(in_lane_1, right_in[1, k], came)
                came = choose(from_left, came, left_in[0, k])
                kv[k, 0] = choose(is_mine, own[k], came)

            cross(k).start()

        @pl.when(i < mine)
        def _():
            attend_suffix(0, i)

        h_far = i - 6

        @pl.when((x == 1) & (h_far == 0))
        def _():
            seg_cross().wait_recv()
            set_bias(1)

        @pl.when((x == 1) & (h_far >= 0) & (h_far < mine))
        def _():
            suffix_cross(h_far).wait_recv()
            attend_suffix(1, h_far)

        part = i - depth - lag

        @pl.when((part >= 0) & (part < chunks))
        def _():
            @pl.when(lax.rem(part, 2) == 0)
            def _():
                cross(part).wait_recv()
                cross(part + 1).wait_recv()

            attend_prefix(part)

        return carry

    lax.fori_loop(0, chunks + depth + lag, step, 0)

    for h in range(mine):
        out_copy(h).wait_recv()
        out_copy(h).wait_send()
        suffix_copy(h).wait_send()
    seg_copy().wait_send()
    query_copy().wait_send()

    @pl.when(x == 0)
    def _():
        seg_cross().wait_send()
        for h in range(mine):
            suffix_cross(h).wait_send()

    @pl.loop(0, mine * half)
    def _(e):
        mate_copy(e).wait_send()

    @pl.when((z == 0) | (z == 3))
    def _():
        want_copy(jnp.where(z == 0, 1, 2)).wait_send()

    @pl.loop(0, chunks)
    def _(k):
        cross(k).wait_send()

        @pl.when(z < 3)
        def _():
            right(0, k).wait_send()

        @pl.when(z > 0)
        def _():
            left(0, k).wait_send()

        if lanes > 1:
            @pl.when(z == 1)
            def _():
                right(1, k).wait_send()

            @pl.when(z == 2)
            def _():
                left(1, k).wait_send()


def fused(lanes, owner, group_of, pages, queries, suffix, seg_row, pool):
    tokens, width = queries.shape
    heads = suffix.shape[1] // (2 * HEAD)
    mine = heads // 2
    q_heads = width // HEAD
    chunks = 2 * pages.shape[1] * pool.shape[1] // tokens * mine
    piece = (tokens, 2 * HEAD)
    count = 4 * tokens
    vmem, smem = pl.BlockSpec(memory_space=pltpu.VMEM), pl.BlockSpec(memory_space=pltpu.SMEM)
    dma = pltpu.SemaphoreType.DMA
    bf16, f32, i32 = jnp.bfloat16, jnp.float32, jnp.int32
    return pl.pallas_call(
        functools.partial(fused_kernel, lanes, heads, q_heads // heads),
        out_shape=jax.ShapeDtypeStruct((tokens, width), bf16),
        in_specs=[smem] * 3 + [vmem] * 4,
        out_specs=vmem,
        scratch_shapes=[
            pltpu.VMEM((chunks,) + piece, bf16),
            pltpu.VMEM((chunks // 2,) + piece, bf16),
            pltpu.VMEM((2, 2, 8, tokens), i32),
            pltpu.VMEM((2, tokens, HEAD), i32),
            pltpu.VMEM((8, HEAD), i32),
            pltpu.VMEM((8, HEAD), i32),
        ]
        + [pltpu.VMEM((lanes, chunks) + piece, bf16)] * 4
        + [
            pltpu.VMEM((chunks, 2) + piece, bf16),
            pltpu.VMEM((2, mine, 2) + piece, bf16),
            pltpu.VMEM((2, tokens, width // 2), bf16),
            pltpu.VMEM((2, tokens, 2 * tokens), f32),
        ]
        + [pltpu.VMEM((tokens, count), f32)] * 2
        + [pltpu.VMEM((tokens, count), bf16)] * 2
        + [pltpu.VMEM((tokens, HEAD), f32)] * 2
        + [pltpu.VMEM((q_heads, tokens, HEAD), f32)] * 3
        + [pltpu.VMEM((mine, tokens, width // heads), bf16)]
        + [dma((lanes, chunks))] * 4
        + [dma((chunks,))] * 2
        + [dma((chunks // 2,))] * 2
        + [dma] * 2
        + [dma((mine,))] * 4
        + [dma((2,))] * 2
        + [dma] * 2
        + [dma((mine,))] * 2,
        compiler_params=pltpu.CompilerParams(
            collective_id=lanes, has_side_effects=True, vmem_limit_bytes=58 << 20
        ),
    )(owner, group_of, pages, queries, suffix, seg_row, pool)


def local_fused(queries, suffix_kv, suffix_seg, prefix_pool, page_table, owner, group_of):
    args = (owner, group_of, page_table, queries[0], suffix_kv[0], suffix_seg, prefix_pool[0])
    apart = (owner[0] < 2) != (owner[1] < 2)
    return lax.cond(
        apart, functools.partial(fused, 1), functools.partial(fused, 2), *args
    )[None]


def fits(mesh):
    return dict(mesh.shape) == {"group": 4, "seq": 4, "tensor": 2}


def solution(mesh):
    return jax.shard_map(
        local_fused if fits(mesh) else local,
        mesh=mesh,
        in_specs=(
            P("group", "seq", "tensor"),
            P("group", "seq", "tensor"),
            P("group", "seq"),
            P("group", "seq", None, "tensor"),
            P(None, "seq"),
            P(),
            P("group"),
        ),
        out_specs=P("group", "seq", "tensor"),
        check_vma=False,
    )
```

```python
import functools
import math

import jax
import jax.numpy as jnp
from jax import lax
from jax.experimental import pallas as pl
from jax.experimental.pallas import tpu as pltpu
from jax.sharding import PartitionSpec as P

HEAD = 128


NEG_FILL = -1e30


def broadcast(value, axis, root):
    mine = lax.axis_index(axis) == root
    return lax.psum(jnp.where(mine, value, jnp.zeros_like(value)), axis)


def absorb(carried, query_rows, key_block, valid):
    running_max, running_sum, accumulator = carried
    scale = 1.0 / math.sqrt(HEAD)
    key_rows = key_block[:, :, 0, :]
    value_rows = key_block[:, :, 1, :]
    scores = (
        jnp.einsum("thgd,khd->htgk", query_rows, key_rows, preferred_element_type=jnp.float32)
        * scale
    )
    if valid is not None:
        scores = jnp.where(valid[None, :, None, :], scores, NEG_FILL)
    new_max = jnp.maximum(running_max, jnp.max(scores, axis=-1, keepdims=True))
    weight = jnp.exp(scores - new_max)
    if valid is not None:
        weight = jnp.where(valid[None, :, None, :], weight, 0.0)
    factor = jnp.exp(running_max - new_max)
    running_sum = running_sum * factor + jnp.sum(weight, axis=-1, keepdims=True)
    accumulator = accumulator * factor + jnp.einsum(
        "htgk,khd->htgd",
        weight.astype(jnp.bfloat16),
        value_rows,
        preferred_element_type=jnp.float32,
    )
    return (new_max, running_sum, accumulator)


def sweep(carried, query_rows, kv_rows, mask_for):
    row_count = kv_rows.shape[0]
    block_rows = math.gcd(row_count, 1024)
    head_count = kv_rows.shape[1] // (2 * HEAD)

    def absorb_block(block_index, state_now):
        offset = block_index * block_rows
        key_block = lax.dynamic_slice_in_dim(kv_rows, offset, block_rows, 0).reshape(
            block_rows, head_count, 2, HEAD
        )
        return absorb(state_now, query_rows, key_block, mask_for(offset, block_rows))

    if row_count == block_rows:
        return absorb_block(0, carried)
    return lax.fori_loop(0, row_count // block_rows, absorb_block, carried)


def combine(earlier, later):
    new_max = jnp.maximum(earlier[0], later[0])
    scale_first = jnp.exp(earlier[0] - new_max)
    scale_second = jnp.exp(later[0] - new_max)
    return (
        new_max,
        earlier[1] * scale_first + later[1] * scale_second,
        earlier[2] * scale_first + later[2] * scale_second,
    )


def no_mask(offset, block_rows):
    return None


def local(queries, suffix_kv, suffix_seg, prefix_pool, page_table, owner, group_of):
    tokens = queries.shape[1]
    row_width = suffix_kv.shape[-1]
    head_count = row_width // (2 * HEAD)
    group_size = queries.shape[-1] // (head_count * HEAD)
    query_rows = queries[0].reshape(tokens, head_count, group_size, HEAD)
    page_pool = prefix_pool[0]
    my_group = group_of[0]
    held_shape = (page_table.shape[1] * page_pool.shape[1], row_width)

    def compact(slot_ids):
        def put(j, rows):
            page = lax.dynamic_slice_in_dim(page_pool, slot_ids[j], 1, 0)
            return lax.dynamic_update_slice_in_dim(rows, page, j, 0)

        count = slot_ids.shape[0]
        rows = jnp.zeros((count,) + page_pool.shape[1:], page_pool.dtype)
        return lax.fori_loop(0, count, put, rows).reshape(-1, row_width)

    def visit_group(request, held_pages):
        moved_pages = broadcast(compact(page_table[request]), "group", owner[request])
        return jnp.where(request == my_group, moved_pages, held_pages)

    prefix_rows = lax.fori_loop(
        0, page_table.shape[0], visit_group, jnp.zeros(held_shape, jnp.bfloat16)
    )
    fresh_state = (
        jnp.full((head_count, tokens, group_size, 1), NEG_FILL, jnp.float32),
        jnp.zeros((head_count, tokens, group_size, 1), jnp.float32),
        jnp.zeros((head_count, tokens, group_size, HEAD), jnp.float32),
    )
    before = sweep(
        fresh_state, query_rows, lax.all_gather(prefix_rows, "seq", axis=0, tiled=True), no_mask
    )
    first_row = lax.axis_index("seq") * tokens
    query_pos = first_row + jnp.arange(tokens, dtype=jnp.int32)
    query_seg = suffix_seg[0]
    first_index = jnp.int32(0)
    kv_rows = lax.all_gather(suffix_kv[0], "seq", axis=0, tiled=True)
    key_segments = lax.all_gather(suffix_seg[0], "seq", axis=0, tiled=True)

    def mask_for(offset, block_rows):
        block_seg = lax.dynamic_slice_in_dim(key_segments, offset, block_rows, 0)
        key_pos = first_index + offset + jnp.arange(block_rows, dtype=jnp.int32)
        return (block_seg[None, :] == query_seg[:, None]) & (key_pos[None, :] <= query_pos[:, None])

    combined = sweep(fresh_state, query_rows, kv_rows, mask_for)
    final_state = combine(before, combined)
    outcome = final_state[2] / final_state[1]
    return outcome.transpose(1, 0, 2, 3).reshape(1, tokens, -1).astype(jnp.bfloat16)

MESH = pl.DeviceIdType.MESH
SKEW = 2
EXP2_SCALE = math.log2(math.e) / math.sqrt(HEAD)


def choose(flag, first, second):
    return lax.select(flag != 0, first, second)


def fused_kernel(
    lanes, heads, group_size,
    owner, group_of, pages, queries, suffix, seg_row, pool,
    out,
    own, mate, sg, qseg, wants, wanted,
    right_in, left_in, right_out, left_out, kv, skv, qs, bias,
    score_0, score_1, weight_0, weight_1, factor_0, factor_1,
    m_ref, l_ref, acc, spare,
    sem_right_s, sem_right_r, sem_left_s, sem_left_r, sem_x_s, sem_x_r,
    sem_mate_s, sem_mate_r, sem_q_s, sem_q_r, sem_skv_s, sem_skv_r,
    sem_xskv_s, sem_xskv_r, sem_sg_s, sem_sg_r, sem_want_s, sem_want_r,
    sem_out_s, sem_out_r,
):
    z = lax.axis_index("group")
    s = lax.axis_index("seq")
    x = s // 2
    c = lax.rem(s, 2)
    chunks, rows = own.shape[:2]
    mine = heads // 2
    tokens = queries.shape[0]
    width = mine * group_size * HEAD
    pair = 2 * HEAD
    partner = s + 1 - 2 * c
    across = lax.rem(s + 2, 4)
    mid = (z == 1) | (z == 2)
    per_head = chunks // mine
    half = per_head // 2

    owner_0, owner_1, want = owner[0], owner[1], group_of[0]
    owner_mine = jnp.where(want == 1, owner_1, owner_0)

    wanted[...] = jnp.zeros_like(wanted)
    barrier = pltpu.get_barrier_semaphore()
    for there in (partner, across):
        pl.semaphore_signal(barrier, inc=1, device_id={"seq": there}, device_id_type=MESH)

    @pl.when(z > 0)
    def _():
        pl.semaphore_signal(barrier, inc=1, device_id={"group": z - 1}, device_id_type=MESH)

    @pl.when(z < 3)
    def _():
        pl.semaphore_signal(barrier, inc=1, device_id={"group": z + 1}, device_id_type=MESH)

    wants[...] = jnp.broadcast_to(want, wants.shape)
    sg[0, c] = jnp.broadcast_to(seg_row[...], sg.shape[2:])
    qs[c] = queries[:, pl.ds(pl.multiple_of(c * width, HEAD), width)]

    owned = jnp.where(owner_1 == z, 1, 0)
    page = pool.shape[1]
    in_part = rows // page

    def columns(core, h):
        return pl.ds(pl.multiple_of((core * mine + h) * pair, pair), pair)

    @pl.loop(0, pages.shape[1])
    def _(j):
        slot = pages[owned, j]
        place = pl.ds(pl.multiple_of(lax.rem(j, in_part) * page, page), page)
        for h in range(mine):
            own[h * per_head + j // in_part, place, :] = pool[slot, :, columns(c, h)]
            mate[h * half + j // in_part, place, :] = pool[slot, :, columns(1 - c, h)]

    for h in range(mine):
        skv[0, h, c] = suffix[:, columns(c, h)]

    pl.semaphore_wait(barrier, jnp.where(mid, 4, 3))

    def move(src, dst, send, recv, axis, there):
        return pltpu.make_async_remote_copy(
            src_ref=src, dst_ref=dst, send_sem=send, recv_sem=recv,
            device_id={axis: there}, device_id_type=MESH,
        )

    def right(lane, k, src=None):
        return move(
            right_out.at[lane, k] if src is None else src, right_in.at[lane, k],
            sem_right_s.at[lane, k], sem_right_r.at[lane, k], "group", lax.rem(z + 1, 4),
        )

    def left(lane, k, src=None):
        return move(
            left_out.at[lane, k] if src is None else src, left_in.at[lane, k],
            sem_left_s.at[lane, k], sem_left_r.at[lane, k], "group", lax.rem(z + 3, 4),
        )

    def cross(k):
        return move(kv.at[k, 0], kv.at[k, 1], sem_x_s.at[k], sem_x_r.at[k], "seq", across)

    def mate_copy(e):
        to = e // half * per_head + half + lax.rem(e, half)
        return move(
            mate.at[e], own.at[to], sem_mate_s.at[e], sem_mate_r.at[e], "seq", partner
        )

    def query_copy():
        cols = pl.ds(pl.multiple_of((1 - c) * width, HEAD), width)
        return move(queries.at[:, cols], qs.at[c], sem_q_s, sem_q_r, "seq", partner)

    def suffix_copy(h):
        return move(
            suffix.at[:, columns(1 - c, h)], skv.at[0, h, c],
            sem_skv_s.at[h], sem_skv_r.at[h], "seq", partner,
        )

    def suffix_cross(h):
        return move(
            skv.at[0, h], skv.at[1, h], sem_xskv_s.at[h], sem_xskv_r.at[h], "seq", across
        )

    def seg_copy():
        return move(sg.at[0, c], sg.at[0, c], sem_sg_s.at[0], sem_sg_r.at[0], "seq", partner)

    def seg_cross():
        return move(sg.at[0], sg.at[1], sem_sg_s.at[1], sem_sg_r.at[1], "seq", across)

    def want_copy(there):
        return move(wants, wanted, sem_want_s, sem_want_r, "group", there)

    def out_copy(h):
        cols = pl.ds(
            pl.multiple_of((c * mine + h) * group_size * HEAD, HEAD), group_size * HEAD
        )
        return move(
            spare.at[h], out.at[:, cols], sem_out_s.at[h], sem_out_r.at[h], "seq", partner
        )

    def from_edge(first, last):
        @pl.when(z == 0)
        def _():
            @pl.loop(first, last)
            def _(k):
                right(0, k, own.at[k]).start()

        @pl.when(z == 3)
        def _():
            @pl.loop(first, last)
            def _(k):
                left(0, k, own.at[k]).start()

    @pl.when((z == 0) | (z == 3))
    def _():
        want_copy(jnp.where(z == 0, 1, 2)).start()

    from_edge(0, half)
    seg_copy().start()
    for h in range(mine):
        suffix_copy(h).start()
    query_copy().start()

    @pl.loop(0, mine * half)
    def _(e):
        mate_copy(e).start()

    seg_copy().wait_recv()
    for h in range(mine):
        suffix_copy(h).wait_recv()

    @pl.when(x == 0)
    def _():
        seg_cross().start()
        for h in range(mine):
            suffix_cross(h).start()

    @pl.loop(0, mine * half)
    def _(e):
        mate_copy(e).wait_recv()

    from_edge(half, chunks)
    for a in range(2):
        qseg[a] = jnp.broadcast_to(sg[0, a, :1, :], (HEAD, tokens)).T
    query_copy().wait_recv()

    scores, weights, factors = (
        (score_0, score_1), (weight_0, weight_1), (factor_0, factor_1)
    )

    def attend(h, tiles, count, block, init, masks):
        def place(tile):
            return (h * 2 + tile[0]) * group_size + tile[1]

        def multiply(t):
            a, i = tiles[t]
            col = pl.multiple_of((h * group_size + i) * HEAD, HEAD)
            scores[t % 2][:, :count] = lax.dot_general(
                qs[a, :, pl.ds(col, HEAD)], block()[:, :HEAD],
                (((1,), (1,)), ((), ())), preferred_element_type=jnp.float32,
            )

        def soften(t):
            sc = scores[t % 2][:, :count]
            if masks is not None:
                sc = jnp.minimum(sc, masks[tiles[t][0]])
            at = place(tiles[t])
            top = jnp.broadcast_to(jnp.max(sc, axis=1, keepdims=True), (tokens, HEAD))
            if not init:
                old = m_ref[at]
                top = jnp.maximum(old, top)
                factors[t % 2][...] = jnp.exp2((old - top) * EXP2_SCALE)
            m_ref[at] = top
            w = jnp.exp2((sc - top[:, :1]) * EXP2_SCALE)
            weights[t % 2][:, :count] = w.astype(jnp.bfloat16)

        def gather(t):
            at = place(tiles[t])
            values = jnp.concatenate(
                [block()[:, HEAD:], jnp.ones((count, HEAD), jnp.bfloat16)], axis=1
            )
            add = jnp.dot(
                weights[t % 2][:, :count], values, preferred_element_type=jnp.float32
            )
            if init:
                acc[at] = add[:, :HEAD]
                l_ref[at] = add[:, HEAD:]
            else:
                factor = factors[t % 2][...]
                acc[at] = acc[at] * factor + add[:, :HEAD]
                l_ref[at] = l_ref[at] * factor + add[:, HEAD:]

        multiply(0)
        for t in range(len(tiles)):
            if t + 1 < len(tiles):
                multiply(t + 1)
            if t > 0:
                gather(t - 1)
            soften(t)
        gather(len(tiles) - 1)

    def set_bias(side):
        for a in range(2):
            k_seg = jnp.concatenate([sg[side, b, :1, :] for b in range(2)], axis=1)
            seen = k_seg == qseg[a][:, :1]
            if side == 0:
                q_off = a * tokens + lax.broadcasted_iota(jnp.int32, seen.shape, 0)
                seen = seen & (lax.broadcasted_iota(jnp.int32, seen.shape, 1) <= q_off)
            bias[a] = jnp.where(seen, jnp.inf, NEG_FILL)

    def attend_suffix(side, h):
        attend(
            h, [(a, i) for a in range(2) for i in range(group_size)], 2 * tokens,
            lambda: skv[side, h].reshape(2 * tokens, pair), side == 0, (bias[0], bias[1]),
        )

    def attend_prefix(part):
        unit = part // 2
        h = unit // (per_head // 2)
        a = lax.rem(part + 1 + c, 2)
        attend(
            h, [(a, i) for i in range(group_size)], 4 * rows,
            lambda: kv[pl.ds(2 * unit, 2)].reshape(4 * rows, pair), False, None,
        )

        @pl.when(lax.rem(unit, per_head // 2) == per_head // 2 - 1)
        def _():
            def ratio(i):
                at = (h * 2 + a) * group_size + i
                return (acc[at] / l_ref[at]).astype(out.dtype)

            @pl.when(a != c)
            def _():
                for i in range(group_size):
                    spare[h, :, i * HEAD : (i + 1) * HEAD] = ratio(i)
                out_copy(h).start()

            @pl.when(a == c)
            def _():
                for i in range(group_size):
                    col = ((c * mine + h) * group_size + i) * HEAD
                    out[:, pl.ds(pl.multiple_of(col, HEAD), HEAD)] = ratio(i)

    depth = SKEW * jnp.maximum(z, 3 - z)
    lag = 2 + 2 * x
    is_mine = (owner_mine == z).astype(jnp.int32)
    from_left = (owner_mine < z).astype(jnp.int32)
    in_lane_1 = (want == 1).astype(jnp.int32)

    def sent_on(lane):
        if lanes == 1:
            return ((owner_0 == z) | (owner_1 == z)).astype(jnp.int32)
        return ((owner_0, owner_1)[lane] == z).astype(jnp.int32)

    @pl.when(mid)
    def _():
        want_copy(jnp.where(z == 1, 0, 3)).wait_recv()

    edge_want = jnp.max(wanted[...])
    edge_owned = (jnp.where(edge_want == 1, owner_1, owner_0) == z).astype(jnp.int32)

    set_bias(0)

    def step(i, carry):
        k_right = i - SKEW * z

        @pl.when(mid & (k_right >= 0) & (k_right < chunks))
        def _():
            k = k_right

            @pl.when(z == 1)
            def _():
                right(0, k).wait_recv()
                for lane in range(lanes):
                    right_out[lane, k] = choose(sent_on(lane), own[k], right_in[0, k])
                    right(lane, k).start()

            @pl.when(z == 2)
            def _():
                for lane in range(lanes):
                    right(lane, k).wait_recv()
                got = right_in[0, k]
                if lanes > 1:
                    got = choose(edge_want, right_in[1, k], got)
                right_out[0, k] = choose(edge_owned, own[k], got)
                right(0, k).start()

        k_left = i - SKEW * (3 - z)

        @pl.when(mid & (k_left >= 0) & (k_left < chunks))
        def _():
            k = k_left

            @pl.when(z == 2)
            def _():
                left(0, k).wait_recv()
                for lane in range(lanes):
                    left_out[lane, k] = choose(sent_on(lane), own[k], left_in[0, k])
                    left(lane, k).start()

            @pl.when(z == 1)
            def _():
                for lane in range(lanes):
                    left(lane, k).wait_recv()
                got = left_in[0, k]
                if lanes > 1:
                    got = choose(edge_want, left_in[1, k], got)
                left_out[0, k] = choose(edge_owned, own[k], got)
                left(0, k).start()

        k_mine = i - depth

        @pl.when((k_mine >= 0) & (k_mine < chunks))
        def _():
            k = k_mine

            @pl.when(z == 0)
            def _():
                left(0, k).wait_recv()
                kv[k, 0] = choose(is_mine, own[k], left_in[0, k])

            @pl.when(z == 3)
            def _():
                right(0, k).wait_recv()
                kv[k, 0] = choose(is_mine, own[k], right_in[0, k])

            @pl.when(z == 1)
            def _():
                came = left_in[0, k]
                if lanes > 1:
                    came = choose(in_lane_1, left_in[1, k], came)
                came = choose(from_left, right_in[0, k], came)
                kv[k, 0] = choose(is_mine, own[k], came)

            @pl.when(z == 2)
            def _():
                came = right_in[0, k]
                if lanes > 1:
                    came = choose(in_lane_1, right_in[1, k], came)
                came = choose(from_left, came, left_in[0, k])
                kv[k, 0] = choose(is_mine, own[k], came)

            cross(k).start()

        @pl.when(i < mine)
        def _():
            attend_suffix(0, i)

        h_far = i - 5

        @pl.when((x == 1) & (h_far == 0))
        def _():
            seg_cross().wait_recv()
            set_bias(1)

        @pl.when((x == 1) & (h_far >= 0) & (h_far < mine))
        def _():
            suffix_cross(h_far).wait_recv()
            attend_suffix(1, h_far)

        part = i - depth - lag

        @pl.when((part >= 0) & (part < chunks))
        def _():
            @pl.when(lax.rem(part, 2) == 0)
            def _():
                cross(part).wait_recv()
                cross(part + 1).wait_recv()

            attend_prefix(part)

        return carry

    lax.fori_loop(0, chunks + depth + lag, step, 0)

    for h in range(mine):
        out_copy(h).wait_recv()
        out_copy(h).wait_send()
        suffix_copy(h).wait_send()
    seg_copy().wait_send()
    query_copy().wait_send()

    @pl.when(x == 0)
    def _():
        seg_cross().wait_send()
        for h in range(mine):
            suffix_cross(h).wait_send()

    @pl.loop(0, mine * half)
    def _(e):
        mate_copy(e).wait_send()

    @pl.when((z == 0) | (z == 3))
    def _():
        want_copy(jnp.where(z == 0, 1, 2)).wait_send()

    @pl.loop(0, chunks)
    def _(k):
        cross(k).wait_send()

        @pl.when(z < 3)
        def _():
            right(0, k).wait_send()

        @pl.when(z > 0)
        def _():
            left(0, k).wait_send()

        if lanes > 1:
            @pl.when(z == 1)
            def _():
                right(1, k).wait_send()

            @pl.when(z == 2)
            def _():
                left(1, k).wait_send()


def fused(lanes, owner, group_of, pages, queries, suffix, seg_row, pool):
    tokens, width = queries.shape
    heads = suffix.shape[1] // (2 * HEAD)
    mine = heads // 2
    q_heads = width // HEAD
    chunks = 2 * pages.shape[1] * pool.shape[1] // tokens * mine
    piece = (tokens, 2 * HEAD)
    count = 4 * tokens
    vmem, smem = pl.BlockSpec(memory_space=pltpu.VMEM), pl.BlockSpec(memory_space=pltpu.SMEM)
    dma = pltpu.SemaphoreType.DMA
    bf16, f32, i32 = jnp.bfloat16, jnp.float32, jnp.int32
    return pl.pallas_call(
        functools.partial(fused_kernel, lanes, heads, q_heads // heads),
        out_shape=jax.ShapeDtypeStruct((tokens, width), bf16),
        in_specs=[smem] * 3 + [vmem] * 4,
        out_specs=vmem,
        scratch_shapes=[
            pltpu.VMEM((chunks,) + piece, bf16),
            pltpu.VMEM((chunks // 2,) + piece, bf16),
            pltpu.VMEM((2, 2, 8, tokens), i32),
            pltpu.VMEM((2, tokens, HEAD), i32),
            pltpu.VMEM((8, HEAD), i32),
            pltpu.VMEM((8, HEAD), i32),
        ]
        + [pltpu.VMEM((lanes, chunks) + piece, bf16)] * 4
        + [
            pltpu.VMEM((chunks, 2) + piece, bf16),
            pltpu.VMEM((2, mine, 2) + piece, bf16),
            pltpu.VMEM((2, tokens, width // 2), bf16),
            pltpu.VMEM((2, tokens, 2 * tokens), f32),
        ]
        + [pltpu.VMEM((tokens, count), f32)] * 2
        + [pltpu.VMEM((tokens, count), bf16)] * 2
        + [pltpu.VMEM((tokens, HEAD), f32)] * 2
        + [pltpu.VMEM((q_heads, tokens, HEAD), f32)] * 3
        + [pltpu.VMEM((mine, tokens, width // heads), bf16)]
        + [dma((lanes, chunks))] * 4
        + [dma((chunks,))] * 2
        + [dma((chunks // 2,))] * 2
        + [dma] * 2
        + [dma((mine,))] * 4
        + [dma((2,))] * 2
        + [dma] * 2
        + [dma((mine,))] * 2,
        compiler_params=pltpu.CompilerParams(
            collective_id=lanes, has_side_effects=True, vmem_limit_bytes=58 << 20
        ),
    )(owner, group_of, pages, queries, suffix, seg_row, pool)


def local_fused(queries, suffix_kv, suffix_seg, prefix_pool, page_table, owner, group_of):
    args = (owner, group_of, page_table, queries[0], suffix_kv[0], suffix_seg, prefix_pool[0])
    apart = (owner[0] < 2) != (owner[1] < 2)
    return lax.cond(
        apart, functools.partial(fused, 1), functools.partial(fused, 2), *args
    )[None]


def fits(mesh):
    return dict(mesh.shape) == {"group": 4, "seq": 4, "tensor": 2}


def solution(mesh):
    return jax.shard_map(
        local_fused if fits(mesh) else local,
        mesh=mesh,
        in_specs=(
            P("group", "seq", "tensor"),
            P("group", "seq", "tensor"),
            P("group", "seq"),
            P("group", "seq", None, "tensor"),
            P(None, "seq"),
            P(),
            P("group"),
        ),
        out_specs=P("group", "seq", "tensor"),
        check_vma=False,
    )
```

```python
import functools
import math

import jax
import jax.numpy as jnp
from jax import lax
from jax.experimental import pallas as pl
from jax.experimental.pallas import tpu as pltpu
from jax.sharding import PartitionSpec as P

HEAD = 128


NEG_FILL = -1e30


def broadcast(value, axis, root):
    mine = lax.axis_index(axis) == root
    return lax.psum(jnp.where(mine, value, jnp.zeros_like(value)), axis)


def absorb(carried, query_rows, key_block, valid):
    running_max, running_sum, accumulator = carried
    scale = 1.0 / math.sqrt(HEAD)
    key_rows = key_block[:, :, 0, :]
    value_rows = key_block[:, :, 1, :]
    scores = (
        jnp.einsum("thgd,khd->htgk", query_rows, key_rows, preferred_element_type=jnp.float32)
        * scale
    )
    if valid is not None:
        scores = jnp.where(valid[None, :, None, :], scores, NEG_FILL)
    new_max = jnp.maximum(running_max, jnp.max(scores, axis=-1, keepdims=True))
    weight = jnp.exp(scores - new_max)
    if valid is not None:
        weight = jnp.where(valid[None, :, None, :], weight, 0.0)
    factor = jnp.exp(running_max - new_max)
    running_sum = running_sum * factor + jnp.sum(weight, axis=-1, keepdims=True)
    accumulator = accumulator * factor + jnp.einsum(
        "htgk,khd->htgd",
        weight.astype(jnp.bfloat16),
        value_rows,
        preferred_element_type=jnp.float32,
    )
    return (new_max, running_sum, accumulator)


def sweep(carried, query_rows, kv_rows, mask_for):
    row_count = kv_rows.shape[0]
    block_rows = math.gcd(row_count, 1024)
    head_count = kv_rows.shape[1] // (2 * HEAD)

    def absorb_block(block_index, state_now):
        offset = block_index * block_rows
        key_block = lax.dynamic_slice_in_dim(kv_rows, offset, block_rows, 0).reshape(
            block_rows, head_count, 2, HEAD
        )
        return absorb(state_now, query_rows, key_block, mask_for(offset, block_rows))

    if row_count == block_rows:
        return absorb_block(0, carried)
    return lax.fori_loop(0, row_count // block_rows, absorb_block, carried)


def combine(earlier, later):
    new_max = jnp.maximum(earlier[0], later[0])
    scale_first = jnp.exp(earlier[0] - new_max)
    scale_second = jnp.exp(later[0] - new_max)
    return (
        new_max,
        earlier[1] * scale_first + later[1] * scale_second,
        earlier[2] * scale_first + later[2] * scale_second,
    )


def no_mask(offset, block_rows):
    return None


def local(queries, suffix_kv, suffix_seg, prefix_pool, page_table, owner, group_of):
    tokens = queries.shape[1]
    row_width = suffix_kv.shape[-1]
    head_count = row_width // (2 * HEAD)
    group_size = queries.shape[-1] // (head_count * HEAD)
    query_rows = queries[0].reshape(tokens, head_count, group_size, HEAD)
    page_pool = prefix_pool[0]
    my_group = group_of[0]
    held_shape = (page_table.shape[1] * page_pool.shape[1], row_width)

    def compact(slot_ids):
        def put(j, rows):
            page = lax.dynamic_slice_in_dim(page_pool, slot_ids[j], 1, 0)
            return lax.dynamic_update_slice_in_dim(rows, page, j, 0)

        count = slot_ids.shape[0]
        rows = jnp.zeros((count,) + page_pool.shape[1:], page_pool.dtype)
        return lax.fori_loop(0, count, put, rows).reshape(-1, row_width)

    def visit_group(request, held_pages):
        moved_pages = broadcast(compact(page_table[request]), "group", owner[request])
        return jnp.where(request == my_group, moved_pages, held_pages)

    prefix_rows = lax.fori_loop(
        0, page_table.shape[0], visit_group, jnp.zeros(held_shape, jnp.bfloat16)
    )
    fresh_state = (
        jnp.full((head_count, tokens, group_size, 1), NEG_FILL, jnp.float32),
        jnp.zeros((head_count, tokens, group_size, 1), jnp.float32),
        jnp.zeros((head_count, tokens, group_size, HEAD), jnp.float32),
    )
    before = sweep(
        fresh_state, query_rows, lax.all_gather(prefix_rows, "seq", axis=0, tiled=True), no_mask
    )
    first_row = lax.axis_index("seq") * tokens
    query_pos = first_row + jnp.arange(tokens, dtype=jnp.int32)
    query_seg = suffix_seg[0]
    first_index = jnp.int32(0)
    kv_rows = lax.all_gather(suffix_kv[0], "seq", axis=0, tiled=True)
    key_segments = lax.all_gather(suffix_seg[0], "seq", axis=0, tiled=True)

    def mask_for(offset, block_rows):
        block_seg = lax.dynamic_slice_in_dim(key_segments, offset, block_rows, 0)
        key_pos = first_index + offset + jnp.arange(block_rows, dtype=jnp.int32)
        return (block_seg[None, :] == query_seg[:, None]) & (key_pos[None, :] <= query_pos[:, None])

    combined = sweep(fresh_state, query_rows, kv_rows, mask_for)
    final_state = combine(before, combined)
    outcome = final_state[2] / final_state[1]
    return outcome.transpose(1, 0, 2, 3).reshape(1, tokens, -1).astype(jnp.bfloat16)

MESH = pl.DeviceIdType.MESH
SKEW = 2
EXP2_SCALE = math.log2(math.e) / math.sqrt(HEAD)


def choose(flag, first, second):
    return lax.select(flag != 0, first, second)


def fused_kernel(
    lanes, heads, group_size,
    owner, group_of, pages, queries, suffix, seg_row, pool,
    out,
    own, mate, sg, qseg, wants, wanted,
    right_in, left_in, right_out, left_out, kv, skv, qs, bias,
    score_0, score_1, weight_0, weight_1, factor_0, factor_1,
    m_ref, l_ref, acc, spare,
    sem_right_s, sem_right_r, sem_left_s, sem_left_r, sem_x_s, sem_x_r,
    sem_mate_s, sem_mate_r, sem_q_s, sem_q_r, sem_skv_s, sem_skv_r,
    sem_xskv_s, sem_xskv_r, sem_sg_s, sem_sg_r, sem_want_s, sem_want_r,
    sem_out_s, sem_out_r,
):
    z = lax.axis_index("group")
    s = lax.axis_index("seq")
    x = s // 2
    c = lax.rem(s, 2)
    chunks, rows = own.shape[:2]
    mine = heads // 2
    tokens = queries.shape[0]
    width = mine * group_size * HEAD
    pair = 2 * HEAD
    partner = s + 1 - 2 * c
    across = lax.rem(s + 2, 4)
    mid = (z == 1) | (z == 2)
    per_head = chunks // mine
    half = per_head // 2

    owner_0, owner_1, want = owner[0], owner[1], group_of[0]
    owner_mine = jnp.where(want == 1, owner_1, owner_0)

    wanted[...] = jnp.zeros_like(wanted)
    barrier = pltpu.get_barrier_semaphore()
    for there in (partner, across):
        pl.semaphore_signal(barrier, inc=1, device_id={"seq": there}, device_id_type=MESH)

    @pl.when(z > 0)
    def _():
        pl.semaphore_signal(barrier, inc=1, device_id={"group": z - 1}, device_id_type=MESH)

    @pl.when(z < 3)
    def _():
        pl.semaphore_signal(barrier, inc=1, device_id={"group": z + 1}, device_id_type=MESH)

    wants[...] = jnp.broadcast_to(want, wants.shape)
    sg[0, c] = jnp.broadcast_to(seg_row[...], sg.shape[2:])
    qs[c] = queries[:, pl.ds(pl.multiple_of(c * width, HEAD), width)]

    owned = jnp.where(owner_1 == z, 1, 0)
    page = pool.shape[1]
    in_part = rows // page

    def columns(core, h):
        return pl.ds(pl.multiple_of((core * mine + h) * pair, pair), pair)

    @pl.loop(0, pages.shape[1])
    def _(j):
        slot = pages[owned, j]
        place = pl.ds(pl.multiple_of(lax.rem(j, in_part) * page, page), page)
        for h in range(mine):
            own[h * per_head + j // in_part, place, :] = pool[slot, :, columns(c, h)]
            mate[h * half + j // in_part, place, :] = pool[slot, :, columns(1 - c, h)]

    for h in range(mine):
        skv[0, h, c] = suffix[:, columns(c, h)]

    pl.semaphore_wait(barrier, jnp.where(mid, 4, 3))

    def move(src, dst, send, recv, axis, there):
        return pltpu.make_async_remote_copy(
            src_ref=src, dst_ref=dst, send_sem=send, recv_sem=recv,
            device_id={axis: there}, device_id_type=MESH,
        )

    def right(lane, k, src=None):
        return move(
            right_out.at[lane, k] if src is None else src, right_in.at[lane, k],
            sem_right_s.at[lane, k], sem_right_r.at[lane, k], "group", lax.rem(z + 1, 4),
        )

    def left(lane, k, src=None):
        return move(
            left_out.at[lane, k] if src is None else src, left_in.at[lane, k],
            sem_left_s.at[lane, k], sem_left_r.at[lane, k], "group", lax.rem(z + 3, 4),
        )

    def cross(k):
        return move(kv.at[k, 0], kv.at[k, 1], sem_x_s.at[k], sem_x_r.at[k], "seq", across)

    def mate_copy(e):
        to = e // half * per_head + half + lax.rem(e, half)
        return move(
            mate.at[e], own.at[to], sem_mate_s.at[e], sem_mate_r.at[e], "seq", partner
        )

    def query_copy():
        cols = pl.ds(pl.multiple_of((1 - c) * width, HEAD), width)
        return move(queries.at[:, cols], qs.at[c], sem_q_s, sem_q_r, "seq", partner)

    def suffix_copy(h):
        return move(
            suffix.at[:, columns(1 - c, h)], skv.at[0, h, c],
            sem_skv_s.at[h], sem_skv_r.at[h], "seq", partner,
        )

    def suffix_cross(h):
        return move(
            skv.at[0, h], skv.at[1, h], sem_xskv_s.at[h], sem_xskv_r.at[h], "seq", across
        )

    def seg_copy():
        return move(sg.at[0, c], sg.at[0, c], sem_sg_s.at[0], sem_sg_r.at[0], "seq", partner)

    def seg_cross():
        return move(sg.at[0], sg.at[1], sem_sg_s.at[1], sem_sg_r.at[1], "seq", across)

    def want_copy(there):
        return move(wants, wanted, sem_want_s, sem_want_r, "group", there)

    def out_copy(h):
        cols = pl.ds(
            pl.multiple_of((c * mine + h) * group_size * HEAD, HEAD), group_size * HEAD
        )
        return move(
            spare.at[h], out.at[:, cols], sem_out_s.at[h], sem_out_r.at[h], "seq", partner
        )

    def from_edge(first, last):
        @pl.when(z == 0)
        def _():
            @pl.loop(first, last)
            def _(k):
                right(0, k, own.at[k]).start()

        @pl.when(z == 3)
        def _():
            @pl.loop(first, last)
            def _(k):
                left(0, k, own.at[k]).start()

    @pl.when((z == 0) | (z == 3))
    def _():
        want_copy(jnp.where(z == 0, 1, 2)).start()

    from_edge(0, half)
    seg_copy().start()
    for h in range(mine):
        suffix_copy(h).start()
    query_copy().start()

    @pl.loop(0, mine * half)
    def _(e):
        mate_copy(e).start()

    seg_copy().wait_recv()
    for h in range(mine):
        suffix_copy(h).wait_recv()

    @pl.when(x == 0)
    def _():
        seg_cross().start()
        for h in range(mine):
            suffix_cross(h).start()

    @pl.loop(0, mine * half)
    def _(e):
        mate_copy(e).wait_recv()

    from_edge(half, chunks)
    for a in range(2):
        qseg[a] = jnp.broadcast_to(sg[0, a, :1, :], (HEAD, tokens)).T
    query_copy().wait_recv()

    scores, weights, factors = (
        (score_0, score_1), (weight_0, weight_1), (factor_0, factor_1)
    )

    def attend(h, tiles, count, block, init, masks):
        def place(tile):
            return (h * 2 + tile[0]) * group_size + tile[1]

        def multiply(t):
            a, i = tiles[t]
            col = pl.multiple_of((h * group_size + i) * HEAD, HEAD)
            scores[t % 2][:, :count] = lax.dot_general(
                qs[a, :, pl.ds(col, HEAD)], block()[:, :HEAD],
                (((1,), (1,)), ((), ())), preferred_element_type=jnp.float32,
            )

        def soften(t):
            sc = scores[t % 2][:, :count]
            if masks is not None:
                sc = jnp.minimum(sc, masks[tiles[t][0]])
            at = place(tiles[t])
            top = jnp.broadcast_to(jnp.max(sc, axis=1, keepdims=True), (tokens, HEAD))
            if not init:
                old = m_ref[at]
                top = jnp.maximum(old, top)
                factors[t % 2][...] = jnp.exp2((old - top) * EXP2_SCALE)
            m_ref[at] = top
            w = jnp.exp2((sc - top[:, :1]) * EXP2_SCALE)
            weights[t % 2][:, :count] = w.astype(jnp.bfloat16)

        def gather(t):
            at = place(tiles[t])
            values = jnp.concatenate(
                [block()[:, HEAD:], jnp.ones((count, HEAD), jnp.bfloat16)], axis=1
            )
            add = jnp.dot(
                weights[t % 2][:, :count], values, preferred_element_type=jnp.float32
            )
            if init:
                acc[at] = add[:, :HEAD]
                l_ref[at] = add[:, HEAD:]
            else:
                factor = factors[t % 2][...]
                acc[at] = acc[at] * factor + add[:, :HEAD]
                l_ref[at] = l_ref[at] * factor + add[:, HEAD:]

        multiply(0)
        for t in range(len(tiles)):
            if t + 1 < len(tiles):
                multiply(t + 1)
            if t > 0:
                gather(t - 1)
            soften(t)
        gather(len(tiles) - 1)

    def set_bias(side):
        for a in range(2):
            k_seg = jnp.concatenate([sg[side, b, :1, :] for b in range(2)], axis=1)
            seen = k_seg == qseg[a][:, :1]
            if side == 0:
                q_off = a * tokens + lax.broadcasted_iota(jnp.int32, seen.shape, 0)
                seen = seen & (lax.broadcasted_iota(jnp.int32, seen.shape, 1) <= q_off)
            bias[a] = jnp.where(seen, jnp.inf, NEG_FILL)

    def attend_suffix(side, h):
        attend(
            h, [(a, i) for a in range(2) for i in range(group_size)], 2 * tokens,
            lambda: skv[side, h].reshape(2 * tokens, pair), side == 0, (bias[0], bias[1]),
        )

    def attend_prefix(part):
        unit = part // 2
        h = unit // (per_head // 2)
        a = lax.rem(part + 1 + c, 2)
        attend(
            h, [(a, i) for i in range(group_size)], 4 * rows,
            lambda: kv[pl.ds(2 * unit, 2)].reshape(4 * rows, pair), False, None,
        )

        @pl.when(lax.rem(unit, per_head // 2) == per_head // 2 - 1)
        def _():
            def ratio(i):
                at = (h * 2 + a) * group_size + i
                return (acc[at] / l_ref[at]).astype(out.dtype)

            @pl.when(a != c)
            def _():
                for i in range(group_size):
                    spare[h, :, i * HEAD : (i + 1) * HEAD] = ratio(i)
                out_copy(h).start()

            @pl.when(a == c)
            def _():
                for i in range(group_size):
                    col = ((c * mine + h) * group_size + i) * HEAD
                    out[:, pl.ds(pl.multiple_of(col, HEAD), HEAD)] = ratio(i)

    depth = SKEW * jnp.maximum(z, 3 - z)
    lag = 2 + 2 * x
    is_mine = (owner_mine == z).astype(jnp.int32)
    from_left = (owner_mine < z).astype(jnp.int32)
    in_lane_1 = (want == 1).astype(jnp.int32)

    def sent_on(lane):
        if lanes == 1:
            return ((owner_0 == z) | (owner_1 == z)).astype(jnp.int32)
        return ((owner_0, owner_1)[lane] == z).astype(jnp.int32)

    @pl.when(mid)
    def _():
        want_copy(jnp.where(z == 1, 0, 3)).wait_recv()

    edge_want = jnp.max(wanted[...])
    edge_owned = (jnp.where(edge_want == 1, owner_1, owner_0) == z).astype(jnp.int32)

    set_bias(0)

    def step(i, carry):
        k_right = i - SKEW * z

        @pl.when(mid & (k_right >= 0) & (k_right < chunks))
        def _():
            k = k_right

            @pl.when(z == 1)
            def _():
                right(0, k).wait_recv()
                for lane in range(lanes):
                    right_out[lane, k] = choose(sent_on(lane), own[k], right_in[0, k])
                    right(lane, k).start()

            @pl.when(z == 2)
            def _():
                for lane in range(lanes):
                    right(lane, k).wait_recv()
                got = right_in[0, k]
                if lanes > 1:
                    got = choose(edge_want, right_in[1, k], got)
                right_out[0, k] = choose(edge_owned, own[k], got)
                right(0, k).start()

        k_left = i - SKEW * (3 - z)

        @pl.when(mid & (k_left >= 0) & (k_left < chunks))
        def _():
            k = k_left

            @pl.when(z == 2)
            def _():
                left(0, k).wait_recv()
                for lane in range(lanes):
                    left_out[lane, k] = choose(sent_on(lane), own[k], left_in[0, k])
                    left(lane, k).start()

            @pl.when(z == 1)
            def _():
                for lane in range(lanes):
                    left(lane, k).wait_recv()
                got = left_in[0, k]
                if lanes > 1:
                    got = choose(edge_want, left_in[1, k], got)
                left_out[0, k] = choose(edge_owned, own[k], got)
                left(0, k).start()

        k_mine = i - depth

        @pl.when((k_mine >= 0) & (k_mine < chunks))
        def _():
            k = k_mine

            @pl.when(z == 0)
            def _():
                left(0, k).wait_recv()
                kv[k, 0] = choose(is_mine, own[k], left_in[0, k])

            @pl.when(z == 3)
            def _():
                right(0, k).wait_recv()
                kv[k, 0] = choose(is_mine, own[k], right_in[0, k])

            @pl.when(z == 1)
            def _():
                came = left_in[0, k]
                if lanes > 1:
                    came = choose(in_lane_1, left_in[1, k], came)
                came = choose(from_left, right_in[0, k], came)
                kv[k, 0] = choose(is_mine, own[k], came)

            @pl.when(z == 2)
            def _():
                came = right_in[0, k]
                if lanes > 1:
                    came = choose(in_lane_1, right_in[1, k], came)
                came = choose(from_left, came, left_in[0, k])
                kv[k, 0] = choose(is_mine, own[k], came)

            cross(k).start()

        @pl.when(i < mine)
        def _():
            attend_suffix(0, i)

        h_far = i - 5

        @pl.when((x == 1) & (h_far == 0))
        def _():
            seg_cross().wait_recv()
            set_bias(1)

        @pl.when((x == 1) & (h_far >= 0) & (h_far < mine))
        def _():
            suffix_cross(h_far).wait_recv()
            attend_suffix(1, h_far)

        part = i - depth - lag

        @pl.when((part >= 0) & (part < chunks))
        def _():
            @pl.when(lax.rem(part, 2) == 0)
            def _():
                cross(part).wait_recv()
                cross(part + 1).wait_recv()

            attend_prefix(part)

        return carry

    lax.fori_loop(0, chunks + depth + lag, step, 0)

    for h in range(mine):
        out_copy(h).wait_recv()
        out_copy(h).wait_send()
        suffix_copy(h).wait_send()
    seg_copy().wait_send()
    query_copy().wait_send()

    @pl.when(x == 0)
    def _():
        seg_cross().wait_send()
        for h in range(mine):
            suffix_cross(h).wait_send()

    @pl.loop(0, mine * half)
    def _(e):
        mate_copy(e).wait_send()

    @pl.when((z == 0) | (z == 3))
    def _():
        want_copy(jnp.where(z == 0, 1, 2)).wait_send()

    @pl.loop(0, chunks)
    def _(k):
        cross(k).wait_send()

        @pl.when(z < 3)
        def _():
            right(0, k).wait_send()

        @pl.when(z > 0)
        def _():
            left(0, k).wait_send()

        if lanes > 1:
            @pl.when(z == 1)
            def _():
                right(1, k).wait_send()

            @pl.when(z == 2)
            def _():
                left(1, k).wait_send()


def fused(lanes, owner, group_of, pages, queries, suffix, seg_row, pool):
    tokens, width = queries.shape
    heads = suffix.shape[1] // (2 * HEAD)
    mine = heads // 2
    q_heads = width // HEAD
    chunks = 2 * pages.shape[1] * pool.shape[1] // tokens * mine
    piece = (tokens, 2 * HEAD)
    count = 4 * tokens
    vmem, smem = pl.BlockSpec(memory_space=pltpu.VMEM), pl.BlockSpec(memory_space=pltpu.SMEM)
    dma = pltpu.SemaphoreType.DMA
    bf16, f32, i32 = jnp.bfloat16, jnp.float32, jnp.int32
    return pl.pallas_call(
        functools.partial(fused_kernel, lanes, heads, q_heads // heads),
        out_shape=jax.ShapeDtypeStruct((tokens, width), bf16),
        in_specs=[smem] * 3 + [vmem] * 4,
        out_specs=vmem,
        scratch_shapes=[
            pltpu.VMEM((chunks,) + piece, bf16),
            pltpu.VMEM((chunks // 2,) + piece, bf16),
            pltpu.VMEM((2, 2, 8, tokens), i32),
            pltpu.VMEM((2, tokens, HEAD), i32),
            pltpu.VMEM((8, HEAD), i32),
            pltpu.VMEM((8, HEAD), i32),
        ]
        + [pltpu.VMEM((lanes, chunks) + piece, bf16)] * 4
        + [
            pltpu.VMEM((chunks, 2) + piece, bf16),
            pltpu.VMEM((2, mine, 2) + piece, bf16),
            pltpu.VMEM((2, tokens, width // 2), bf16),
            pltpu.VMEM((2, tokens, 2 * tokens), f32),
        ]
        + [pltpu.VMEM((tokens, count), f32)] * 2
        + [pltpu.VMEM((tokens, count), bf16)] * 2
        + [pltpu.VMEM((tokens, HEAD), f32)] * 2
        + [pltpu.VMEM((q_heads, tokens, HEAD), f32)] * 3
        + [pltpu.VMEM((mine, tokens, width // heads), bf16)]
        + [dma((lanes, chunks))] * 4
        + [dma((chunks,))] * 2
        + [dma((chunks // 2,))] * 2
        + [dma] * 2
        + [dma((mine,))] * 4
        + [dma((2,))] * 2
        + [dma] * 2
        + [dma((mine,))] * 2,
        compiler_params=pltpu.CompilerParams(
            collective_id=lanes, has_side_effects=True, vmem_limit_bytes=58 << 20
        ),
    )(owner, group_of, pages, queries, suffix, seg_row, pool)


def pipeline(tiles, count, query, block, mask, place, state, buffers, init):
    m_ref, l_ref, acc = state
    scores, weights, factors = buffers
    rows = factors[0].shape[0]

    def multiply(t):
        scores[t % 2][:, :count] = lax.dot_general(
            query(tiles[t]), block(tiles[t])[:, :HEAD],
            (((1,), (1,)), ((), ())), preferred_element_type=jnp.float32,
        )

    def soften(t):
        sc = scores[t % 2][:, :count]
        if mask is not None:
            sc = jnp.minimum(sc, mask(tiles[t]))
        at = place(tiles[t])
        top = jnp.broadcast_to(jnp.max(sc, axis=1, keepdims=True), (rows, HEAD))
        if not init:
            old = m_ref[at]
            top = jnp.maximum(old, top)
            factors[t % 2][...] = jnp.exp2((old - top) * EXP2_SCALE)
        m_ref[at] = top
        w = jnp.exp2((sc - top[:, :1]) * EXP2_SCALE)
        weights[t % 2][:, :count] = w.astype(jnp.bfloat16)

    def gather(t):
        at = place(tiles[t])
        values = jnp.concatenate(
            [block(tiles[t])[:, HEAD:], jnp.ones((count, HEAD), jnp.bfloat16)], axis=1
        )
        add = jnp.dot(weights[t % 2][:, :count], values, preferred_element_type=jnp.float32)
        if init:
            acc[at] = add[:, :HEAD]
            l_ref[at] = add[:, HEAD:]
        else:
            factor = factors[t % 2][...]
            acc[at] = acc[at] * factor + add[:, :HEAD]
            l_ref[at] = l_ref[at] * factor + add[:, HEAD:]

    multiply(0)
    for t in range(len(tiles)):
        if t + 1 < len(tiles):
            multiply(t + 1)
        if t > 0:
            gather(t - 1)
        soften(t)
    gather(len(tiles) - 1)


def moved_kernel(
    flip, heads, group_size,
    owner, group_of, pages, queries, suffix, seg_row, pool,
    out,
    kv, mate, sg, qseg, wants, wanted, skv, qs, bias,
    down_in, down_out, up_q, slots, made, up_in, up_out, back, fin,
    made_ml, up_in_ml, up_out_ml, back_ml, fin_ml,
    score_0, score_1, weight_0, weight_1, factor_0, factor_1,
    m_ref, l_ref, acc, m_job, l_job, acc_job, spare,
    sem_x_s, sem_x_r, sem_mate_s, sem_mate_r, sem_q_s, sem_q_r, sem_skv_s, sem_skv_r,
    sem_xskv_s, sem_xskv_r, sem_sg_s, sem_sg_r, sem_want_s, sem_want_r,
    sem_out_s, sem_out_r, sem_down_s, sem_down_r, sem_upq_s, sem_upq_r,
    sem_up_s, sem_up_r, sem_upml_s, sem_upml_r, sem_back_s, sem_back_r,
    sem_backml_s, sem_backml_r,
):
    z = lax.axis_index("group")
    s = lax.axis_index("seq")
    x = s // 2
    c = lax.rem(s, 2)
    p = 3 - z if flip else z
    toward = -1 if flip else 1
    up = lax.rem(z + toward + 4, 4)
    down = lax.rem(z - toward + 4, 4)
    serves = p < 2
    chunks = kv.shape[0]
    rows = kv.shape[2]
    mine = heads // 2
    tokens = queries.shape[0]
    wide = group_size * HEAD
    pair = 2 * HEAD
    partner = s + 1 - 2 * c
    across = lax.rem(s + 2, 4)
    per_head = chunks // mine
    half = per_head // 2
    quarter = per_head // 2
    jobs = 4 * mine

    owner_0, owner_1, want = owner[0], owner[1], group_of[0]

    barrier = pltpu.get_barrier_semaphore()
    for there in (partner, across):
        pl.semaphore_signal(barrier, inc=1, device_id={"seq": there}, device_id_type=MESH)
    for k in range(1, 4):
        pl.semaphore_signal(
            barrier, inc=1, device_id={"group": lax.rem(z + k, 4)}, device_id_type=MESH
        )

    wants[...] = jnp.broadcast_to(want, wants.shape)
    wanted[z] = jnp.broadcast_to(want, wants.shape)
    sg[0, c] = jnp.broadcast_to(seg_row[...], sg.shape[2:])

    def query_columns(core, h):
        return pl.ds(pl.multiple_of((core * mine + h) * wide, HEAD), wide)

    def columns(core, h):
        return pl.ds(pl.multiple_of((core * mine + h) * pair, pair), pair)

    for h in range(mine):
        qs[h * 2 + c] = queries[:, query_columns(c, h)]
        skv[0, h, c] = suffix[:, columns(c, h)]

    owned = jnp.where(owner_1 == z, 1, 0)
    page = pool.shape[1]
    in_part = rows // page

    @pl.when(serves)
    def _():
        @pl.loop(0, pages.shape[1])
        def _(j):
            slot = pages[owned, j]
            place = pl.ds(pl.multiple_of(lax.rem(j, in_part) * page, page), page)
            for h in range(mine):
                kv[h * per_head + j // in_part, 0, place, :] = pool[slot, :, columns(c, h)]
                mate[h * half + j // in_part, place, :] = pool[slot, :, columns(1 - c, h)]

    pl.semaphore_wait(barrier, 5)

    def move(src, dst, send, recv, axis, there):
        return pltpu.make_async_remote_copy(
            src_ref=src, dst_ref=dst, send_sem=send, recv_sem=recv,
            device_id={axis: there}, device_id_type=MESH,
        )

    def cross(k):
        return move(kv.at[k, 0], kv.at[k, 1], sem_x_s.at[k], sem_x_r.at[k], "seq", across)

    def mate_copy(e):
        to = e // half * per_head + half + lax.rem(e, half)
        return move(
            mate.at[e], kv.at[to, 0], sem_mate_s.at[e], sem_mate_r.at[e], "seq", partner
        )

    def query_copy(h):
        return move(
            queries.at[:, query_columns(1 - c, h)], qs.at[h * 2 + c],
            sem_q_s.at[h], sem_q_r.at[h], "seq", partner,
        )

    def suffix_copy(h):
        return move(
            suffix.at[:, columns(1 - c, h)], skv.at[0, h, c],
            sem_skv_s.at[h], sem_skv_r.at[h], "seq", partner,
        )

    def suffix_cross(h):
        return move(
            skv.at[0, h], skv.at[1, h], sem_xskv_s.at[h], sem_xskv_r.at[h], "seq", across
        )

    def seg_copy():
        return move(sg.at[0, c], sg.at[0, c], sem_sg_s.at[0], sem_sg_r.at[0], "seq", partner)

    def seg_cross():
        return move(sg.at[0], sg.at[1], sem_sg_s.at[1], sem_sg_r.at[1], "seq", across)

    def want_copy(k, origin):
        return move(
            wants, wanted.at[origin], sem_want_s.at[k - 1], sem_want_r.at[origin],
            "group", lax.rem(z + k, 4),
        )

    def out_copy(h):
        return move(
            spare.at[h], out.at[:, query_columns(c, h)],
            sem_out_s.at[h], sem_out_r.at[h], "seq", partner,
        )

    def send_down(lane, e, src):
        return move(
            src, down_in.at[lane, e], sem_down_s.at[lane, e], sem_down_r.at[lane, e],
            "group", down,
        )

    def send_up_q(e):
        return move(qs.at[e], up_q.at[e], sem_upq_s.at[e], sem_upq_r.at[e], "group", up)

    def send_up(lane, f, src):
        return move(
            src.at[lane, f], up_in.at[lane, f], sem_up_s.at[lane, f], sem_up_r.at[lane, f],
            "group", up,
        )

    def send_up_ml(lane, e, src):
        return move(
            src.at[lane, e], up_in_ml.at[lane, e], sem_upml_s.at[lane, e],
            sem_upml_r.at[lane, e], "group", up,
        )

    def send_back(f):
        return move(made.at[0, f], back.at[f], sem_back_s.at[f], sem_back_r.at[f], "group", down)

    def send_back_ml(e):
        return move(
            made_ml.at[0, e], back_ml.at[e], sem_backml_s.at[e], sem_backml_r.at[e],
            "group", down,
        )

    for k in range(1, 4):
        want_copy(k, z).start()
    seg_copy().start()
    for h in range(mine):
        query_copy(h).start()
    for h in range(mine):
        suffix_copy(h).start()

    @pl.when(serves)
    def _():
        @pl.loop(0, half)
        def _(k):
            cross(k).start()

        @pl.loop(0, mine * half)
        def _(e):
            mate_copy(e).start()

    for h in range(mine):
        query_copy(h).wait_recv()

    @pl.when(p == 3)
    def _():
        for e in range(2 * mine):
            send_down(1, e, qs.at[e]).start()

    @pl.when(p == 2)
    def _():
        for e in range(2):
            send_down(0, e, qs.at[e]).start()

    @pl.when(p == 0)
    def _():
        for e in range(2 * mine):
            send_up_q(e).start()

    seg_copy().wait_recv()
    for h in range(mine):
        suffix_copy(h).wait_recv()

    @pl.when(serves)
    def _():
        @pl.loop(0, mine * half)
        def _(e):
            mate_copy(e).wait_recv()

        @pl.loop(half, chunks)
        def _(k):
            cross(k).start()

    @pl.when(x == 0)
    def _():
        seg_cross().start()
        for h in range(mine):
            suffix_cross(h).start()

    for a in range(2):
        qseg[a] = jnp.broadcast_to(sg[0, a, :1, :], (HEAD, tokens)).T

    for k in range(1, 4):
        want_copy(k, lax.rem(z + k, 4)).wait_recv()
    at_0, at_1 = (3 - owner_0, 3 - owner_1) if flip else (owner_0, owner_1)
    served = [
        jnp.where(jnp.max(wanted[3 - q if flip else q]) == 1, at_1, at_0) for q in range(4)
    ]

    def by(server, q):
        return (served[q] == server).astype(jnp.int32)

    split = (served[2] != served[3]).astype(jnp.int32)

    buffers = ((score_0, score_1), (weight_0, weight_1), (factor_0, factor_1))

    def set_bias(side):
        for a in range(2):
            k_seg = jnp.concatenate([sg[side, b, :1, :] for b in range(2)], axis=1)
            seen = k_seg == qseg[a][:, :1]
            if side == 0:
                q_off = a * tokens + lax.broadcasted_iota(jnp.int32, seen.shape, 0)
                seen = seen & (lax.broadcasted_iota(jnp.int32, seen.shape, 1) <= q_off)
            bias[a] = jnp.where(seen, jnp.inf, NEG_FILL)

    def attend_suffix(side, h):
        pipeline(
            [(a, i) for a in range(2) for i in range(group_size)], 2 * tokens,
            lambda t: qs[h * 2 + t[0], :, t[1] * HEAD : (t[1] + 1) * HEAD],
            lambda t: skv[side, h].reshape(2 * tokens, pair),
            lambda t: bias[t[0]],
            lambda t: (h * 2 + t[0]) * group_size + t[1],
            (m_ref, l_ref, acc), buffers, side == 0,
        )

    def event_1(b):
        e = b // 4 * 2 + lax.rem(b, 2)

        @pl.when(lax.rem(b // 2, 2) == 0)
        def _():
            send_down(0, e, down_out.at[0, e]).wait_recv()
            send_up_q(e).wait_recv()
            down_out[0, e] = choose(by(0, 1), qs[e], down_in[0, e])
            send_down(0, e, down_out.at[0, e]).start()
            rest = choose(by(1, 1), qs[e], down_in[0, e])
            slots[0, e] = choose(by(1, 0), up_q[e], rest)

        @pl.when(lax.rem(b // 2, 2) == 1)
        def _():
            send_down(1, e, down_out.at[1, e]).wait_recv()
            rest = choose(by(0, 2), down_in[0, e], qs[e])
            down_out[1, e] = choose(by(0, 3), down_in[1, e], rest)
            send_down(1, e, down_out.at[1, e]).start()
            rest = choose(by(1, 2), down_in[0, e], qs[e])
            slots[1, e] = choose(by(1, 3), down_in[1, e], rest)

    def event_0(b):
        e = b // 4 * 2 + lax.rem(b, 2)

        @pl.when(lax.rem(b // 2, 2) == 0)
        def _():
            send_down(0, e, down_out.at[0, e]).wait_recv()
            slots[0, e] = choose(by(0, 0), qs[e], down_in[0, e])

        @pl.when(lax.rem(b // 2, 2) == 1)
        def _():
            send_down(1, e, down_out.at[1, e]).wait_recv()
            slots[1, e] = down_in[1, e]

    def relay_q(e):
        send_down(1, e, down_in.at[1, e]).wait_recv()
        send_down(1, e, down_in.at[1, e]).start()

    def relay_1(e):
        for f in range(2):
            send_up(0, 2 * e + f, up_out).wait_recv()
        send_up_ml(0, e, up_out_ml).wait_recv()
        for f in range(2):
            rest = choose(by(1, 2), made[0, 2 * e + f], up_in[0, 2 * e + f])
            up_out[0, 2 * e + f] = choose(split, made[1, 2 * e + f], rest)
            send_up(0, 2 * e + f, up_out).start()
        rest = choose(by(1, 2), made_ml[0, e], up_in_ml[0, e])
        up_out_ml[0, e] = choose(split, made_ml[1, e], rest)
        send_up_ml(0, e, up_out_ml).start()

    local_3 = (1 - split) * by(1, 3)

    def relay_2(e):
        for f in range(2):
            send_up(1, 2 * e + f, up_out).wait_recv()
            up_out[1, 2 * e + f] = choose(local_3, made[1, 2 * e + f], up_in[1, 2 * e + f])
            send_up(1, 2 * e + f, up_out).start()
        send_up_ml(1, e, up_out_ml).wait_recv()
        up_out_ml[1, e] = choose(local_3, made_ml[1, e], up_in_ml[1, e])
        send_up_ml(1, e, up_out_ml).start()

    def finish(b, h, j, a):
        e = h * 2 + a
        lane = lax.broadcasted_iota(jnp.int32, (tokens, HEAD), 1)
        packed = jnp.zeros((tokens, HEAD), jnp.float32)
        for i in range(group_size):
            at = i % 2 * HEAD
            made[j, 2 * e + i // 2, :, at : at + HEAD] = (acc_job[i] / l_job[i]).astype(
                made.dtype
            )
            packed = jnp.where(lane == i, m_job[i], packed)
            packed = jnp.where(lane == group_size + i, l_job[i], packed)
        made_ml[j, e] = packed.T[:8]

        @pl.when(p == 0)
        def _():
            for f in range(2):
                send_up(j, 2 * e + f, made).start()
            send_up_ml(j, e, made_ml).start()

        @pl.when((p == 1) & (j == 0))
        def _():
            for f in range(2):
                send_back(2 * e + f).start()
            send_back_ml(e).start()

        @pl.when((p == 1) & (j == 1))
        def _():
            relay_1(e)

        @pl.when((p == 1) & (h == 1) & (j == 0))
        def _():
            relay_2(a)

    def serve(n, carry):
        b, v = n // 2, lax.rem(n, 2)
        h, j, a = b // 4, lax.rem(b // 2, 2), lax.rem(b, 2)
        e = h * 2 + a

        @pl.when((p == 0) & (v == 0))
        def _():
            event_0(b)

        @pl.when((p == 1) & (v == 1) & (b < jobs - 1))
        def _():
            event_1(b + 1)

        @pl.when((j == 0) & (a == 0))
        def _():
            for k in range(quarter):
                cross(h * per_head + v * quarter + k).wait_recv()

        @pl.when(v == 0)
        def _():
            m_job[...] = jnp.full(m_job.shape, NEG_FILL, jnp.float32)
            l_job[...] = jnp.zeros(l_job.shape, jnp.float32)
            acc_job[...] = jnp.zeros(acc_job.shape, jnp.float32)

        joined = quarter // 2
        first = h * per_head + v * quarter
        pipeline(
            [(g, i) for g in range(2) for i in range(group_size)], 2 * joined * rows,
            lambda t: slots[j, e, :, t[1] * HEAD : (t[1] + 1) * HEAD],
            lambda t: kv[pl.ds(first + t[0] * joined, joined)].reshape(2 * joined * rows, pair),
            None, lambda t: t[1], (m_job, l_job, acc_job), buffers, False,
        )

        @pl.when(v == 1)
        def _():
            finish(b, h, j, a)

        return carry

    def merge(e):
        h, a = e // 2, e % 2
        ml = jnp.concatenate([fin_ml[e]] * (HEAD // 8), axis=0).T

        def ratio(i):
            at = e * group_size + i
            lane = i % 2 * HEAD
            near = m_ref[at]
            far = jnp.broadcast_to(ml[:, i : i + 1], (tokens, HEAD))
            top = jnp.maximum(near, far)
            keep = jnp.exp2((near - top) * EXP2_SCALE)
            total = jnp.broadcast_to(
                ml[:, group_size + i : group_size + i + 1], (tokens, HEAD)
            ) * jnp.exp2((far - top) * EXP2_SCALE)
            context = fin[2 * e + i // 2, :, lane : lane + HEAD].astype(jnp.float32)
            both = context * total + acc[at] * keep
            return (both / (total + l_ref[at] * keep)).astype(out.dtype)

        @pl.when(a != c)
        def _():
            for i in range(group_size):
                spare[h, :, i * HEAD : (i + 1) * HEAD] = ratio(i)
            out_copy(h).start()

        @pl.when(a == c)
        def _():
            for i in range(group_size):
                col = ((c * mine + h) * group_size + i) * HEAD
                out[:, pl.ds(pl.multiple_of(col, HEAD), HEAD)] = ratio(i)

    set_bias(0)

    @pl.loop(0, mine)
    def _(h):
        attend_suffix(0, h)

        @pl.when(p == 2)
        def _():
            relay_q(h)

    @pl.when(p == 2)
    def _():
        for e in range(2, 2 * mine):
            send_down(0, e, qs.at[e]).start()

    @pl.when(p == 1)
    def _():
        event_1(jnp.int32(0))

    lax.fori_loop(0, jnp.where(serves, 2 * jobs, 0), serve, 0)

    @pl.when(p == 1)
    def _():
        relay_2(2)

    @pl.when(x == 1)
    def _():
        seg_cross().wait_recv()
        set_bias(1)

    @pl.loop(0, mine)
    def _(h):
        @pl.when(x == 1)
        def _():
            suffix_cross(h).wait_recv()
            attend_suffix(1, h)

        @pl.when(p == 2)
        def _():
            relay_q(2 + h)

    @pl.when(p == 1)
    def _():
        relay_2(3)

    for e in range(2 * mine):
        both = (2 * e, 2 * e + 1)

        @pl.when(p == 0)
        def _():
            for f in both:
                send_back(f).wait_recv()
                fin[f] = choose(by(0, 0), made[0, f], back[f])
            send_back_ml(e).wait_recv()
            fin_ml[e] = choose(by(0, 0), made_ml[0, e], back_ml[e])

        @pl.when(p == 1)
        def _():
            def pick(have, came, at):
                here = choose(by(1, 0), have[1, at], have[0, at])
                there = choose(by(0, 0), came[1, at], came[0, at])
                return choose(by(1, 1), here, there)

            for f in both:
                fin[f] = pick(made, up_in, f)
            fin_ml[e] = pick(made_ml, up_in_ml, e)

        @pl.when(p == 2)
        def _():
            late_2 = split * by(0, 2)
            early_3 = split * by(1, 3)
            for f in both:
                send_up(0, f, up_out).wait_recv()
                send_up(1, f, up_out).wait_recv()
                up_out[1, f] = choose(early_3, up_in[0, f], up_in[1, f])
                send_up(1, f, up_out).start()
                fin[f] = choose(late_2, up_in[1, f], up_in[0, f])
            send_up_ml(0, e, up_out_ml).wait_recv()
            send_up_ml(1, e, up_out_ml).wait_recv()
            up_out_ml[1, e] = choose(early_3, up_in_ml[0, e], up_in_ml[1, e])
            send_up_ml(1, e, up_out_ml).start()
            fin_ml[e] = choose(late_2, up_in_ml[1, e], up_in_ml[0, e])

        @pl.when(p == 3)
        def _():
            for f in both:
                send_up(1, f, up_out).wait_recv()
                fin[f] = up_in[1, f]
            send_up_ml(1, e, up_out_ml).wait_recv()
            fin_ml[e] = up_in_ml[1, e]

        merge(e)

    for k in range(1, 4):
        want_copy(k, z).wait_send()
    for h in range(mine):
        out_copy(h).wait_recv()
        out_copy(h).wait_send()
        suffix_copy(h).wait_send()
        query_copy(h).wait_send()
    seg_copy().wait_send()

    @pl.when(x == 0)
    def _():
        seg_cross().wait_send()
        for h in range(mine):
            suffix_cross(h).wait_send()

    @pl.when(serves)
    def _():
        @pl.loop(0, mine * half)
        def _(e):
            mate_copy(e).wait_send()

        @pl.loop(0, chunks)
        def _(k):
            cross(k).wait_send()

    for e in range(2 * mine):
        @pl.when((p == 1) | (p == 2))
        def _():
            send_down(0, e, qs.at[e]).wait_send()

        @pl.when(p > 0)
        def _():
            send_down(1, e, qs.at[e]).wait_send()

        @pl.when(p < 2)
        def _():
            send_up_ml(0, e, up_out_ml).wait_send()
            for f in range(2):
                send_up(0, 2 * e + f, up_out).wait_send()

        @pl.when(p < 3)
        def _():
            send_up_ml(1, e, up_out_ml).wait_send()
            for f in range(2):
                send_up(1, 2 * e + f, up_out).wait_send()

        @pl.when(p == 0)
        def _():
            send_up_q(e).wait_send()

        @pl.when(p == 1)
        def _():
            send_back_ml(e).wait_send()
            for f in range(2):
                send_back(2 * e + f).wait_send()


def moved(flip, owner, group_of, pages, queries, suffix, seg_row, pool):
    tokens, width = queries.shape
    heads = suffix.shape[1] // (2 * HEAD)
    mine = heads // 2
    q_heads = width // HEAD
    group_size = q_heads // heads
    chunks = 2 * pages.shape[1] * pool.shape[1] // tokens * mine
    piece = (tokens, 2 * HEAD)
    query = (tokens, group_size * HEAD)
    count = 4 * tokens
    vmem, smem = pl.BlockSpec(memory_space=pltpu.VMEM), pl.BlockSpec(memory_space=pltpu.SMEM)
    dma = pltpu.SemaphoreType.DMA
    bf16, f32, i32 = jnp.bfloat16, jnp.float32, jnp.int32
    parts = 2 * mine
    return pl.pallas_call(
        functools.partial(moved_kernel, flip, heads, group_size),
        out_shape=jax.ShapeDtypeStruct((tokens, width), bf16),
        in_specs=[smem] * 3 + [vmem] * 4,
        out_specs=vmem,
        scratch_shapes=[
            pltpu.VMEM((chunks, 2) + piece, bf16),
            pltpu.VMEM((chunks // 2,) + piece, bf16),
            pltpu.VMEM((2, 2, 8, tokens), i32),
            pltpu.VMEM((2, tokens, HEAD), i32),
            pltpu.VMEM((8, HEAD), i32),
            pltpu.VMEM((4, 8, HEAD), i32),
            pltpu.VMEM((2, mine, 2) + piece, bf16),
            pltpu.VMEM((parts,) + query, bf16),
            pltpu.VMEM((2, tokens, 2 * tokens), f32),
        ]
        + [pltpu.VMEM((2, parts) + query, bf16)] * 2
        + [
            pltpu.VMEM((parts,) + query, bf16),
            pltpu.VMEM((2, parts) + query, bf16),
        ]
        + [pltpu.VMEM((2, 2 * parts) + piece, bf16)] * 3
        + [pltpu.VMEM((2 * parts,) + piece, bf16)] * 2
        + [pltpu.VMEM((2, parts, 8, tokens), f32)] * 3
        + [pltpu.VMEM((parts, 8, tokens), f32)] * 2
        + [pltpu.VMEM((tokens, count), f32)] * 2
        + [pltpu.VMEM((tokens, count), bf16)] * 2
        + [pltpu.VMEM((tokens, HEAD), f32)] * 2
        + [pltpu.VMEM((q_heads, tokens, HEAD), f32)] * 3
        + [pltpu.VMEM((group_size, tokens, HEAD), f32)] * 3
        + [pltpu.VMEM((mine,) + query, bf16)]
        + [dma((chunks,))] * 2
        + [dma((chunks // 2,))] * 2
        + [dma((mine,))] * 6
        + [dma((2,))] * 2
        + [dma((3,)), dma((4,))]
        + [dma((mine,))] * 2
        + [dma((2, parts))] * 2
        + [dma((parts,))] * 2
        + [dma((2, 2 * parts))] * 2
        + [dma((2, parts))] * 2
        + [dma((2 * parts,))] * 2
        + [dma((parts,))] * 2,
        compiler_params=pltpu.CompilerParams(
            collective_id=2 + flip, has_side_effects=True, vmem_limit_bytes=58 << 20
        ),
    )(owner, group_of, pages, queries, suffix, seg_row, pool)


def local_fused(queries, suffix_kv, suffix_seg, prefix_pool, page_table, owner, group_of):
    args = (owner, group_of, page_table, queries[0], suffix_kv[0], suffix_seg, prefix_pool[0])
    low = (owner < 2).astype(jnp.int32)
    plans = [
        functools.partial(moved, 1), functools.partial(fused, 1), functools.partial(moved, 0)
    ]
    return lax.switch(low[0] + low[1], plans, *args)[None]


def fits(mesh):
    return dict(mesh.shape) == {"group": 4, "seq": 4, "tensor": 2}


def solution(mesh):
    return jax.shard_map(
        local_fused if fits(mesh) else local,
        mesh=mesh,
        in_specs=(
            P("group", "seq", "tensor"),
            P("group", "seq", "tensor"),
            P("group", "seq"),
            P("group", "seq", None, "tensor"),
            P(None, "seq"),
            P(),
            P("group"),
        ),
        out_specs=P("group", "seq", "tensor"),
        check_vma=False,
    )
```

```python
import functools
import math

import jax
import jax.numpy as jnp
from jax import lax
from jax.experimental import pallas as pl
from jax.experimental.pallas import tpu as pltpu
from jax.sharding import PartitionSpec as P

HEAD = 128


NEG_FILL = -1e30


def broadcast(value, axis, root):
    mine = lax.axis_index(axis) == root
    return lax.psum(jnp.where(mine, value, jnp.zeros_like(value)), axis)


def absorb(carried, query_rows, key_block, valid):
    running_max, running_sum, accumulator = carried
    scale = 1.0 / math.sqrt(HEAD)
    key_rows = key_block[:, :, 0, :]
    value_rows = key_block[:, :, 1, :]
    scores = (
        jnp.einsum("thgd,khd->htgk", query_rows, key_rows, preferred_element_type=jnp.float32)
        * scale
    )
    if valid is not None:
        scores = jnp.where(valid[None, :, None, :], scores, NEG_FILL)
    new_max = jnp.maximum(running_max, jnp.max(scores, axis=-1, keepdims=True))
    weight = jnp.exp(scores - new_max)
    if valid is not None:
        weight = jnp.where(valid[None, :, None, :], weight, 0.0)
    factor = jnp.exp(running_max - new_max)
    running_sum = running_sum * factor + jnp.sum(weight, axis=-1, keepdims=True)
    accumulator = accumulator * factor + jnp.einsum(
        "htgk,khd->htgd",
        weight.astype(jnp.bfloat16),
        value_rows,
        preferred_element_type=jnp.float32,
    )
    return (new_max, running_sum, accumulator)


def sweep(carried, query_rows, kv_rows, mask_for):
    row_count = kv_rows.shape[0]
    block_rows = math.gcd(row_count, 1024)
    head_count = kv_rows.shape[1] // (2 * HEAD)

    def absorb_block(block_index, state_now):
        offset = block_index * block_rows
        key_block = lax.dynamic_slice_in_dim(kv_rows, offset, block_rows, 0).reshape(
            block_rows, head_count, 2, HEAD
        )
        return absorb(state_now, query_rows, key_block, mask_for(offset, block_rows))

    if row_count == block_rows:
        return absorb_block(0, carried)
    return lax.fori_loop(0, row_count // block_rows, absorb_block, carried)


def combine(earlier, later):
    new_max = jnp.maximum(earlier[0], later[0])
    scale_first = jnp.exp(earlier[0] - new_max)
    scale_second = jnp.exp(later[0] - new_max)
    return (
        new_max,
        earlier[1] * scale_first + later[1] * scale_second,
        earlier[2] * scale_first + later[2] * scale_second,
    )


def no_mask(offset, block_rows):
    return None


def local(queries, suffix_kv, suffix_seg, prefix_pool, page_table, owner, group_of):
    tokens = queries.shape[1]
    row_width = suffix_kv.shape[-1]
    head_count = row_width // (2 * HEAD)
    group_size = queries.shape[-1] // (head_count * HEAD)
    query_rows = queries[0].reshape(tokens, head_count, group_size, HEAD)
    page_pool = prefix_pool[0]
    my_group = group_of[0]
    held_shape = (page_table.shape[1] * page_pool.shape[1], row_width)

    def compact(slot_ids):
        def put(j, rows):
            page = lax.dynamic_slice_in_dim(page_pool, slot_ids[j], 1, 0)
            return lax.dynamic_update_slice_in_dim(rows, page, j, 0)

        count = slot_ids.shape[0]
        rows = jnp.zeros((count,) + page_pool.shape[1:], page_pool.dtype)
        return lax.fori_loop(0, count, put, rows).reshape(-1, row_width)

    def visit_group(request, held_pages):
        moved_pages = broadcast(compact(page_table[request]), "group", owner[request])
        return jnp.where(request == my_group, moved_pages, held_pages)

    prefix_rows = lax.fori_loop(
        0, page_table.shape[0], visit_group, jnp.zeros(held_shape, jnp.bfloat16)
    )
    fresh_state = (
        jnp.full((head_count, tokens, group_size, 1), NEG_FILL, jnp.float32),
        jnp.zeros((head_count, tokens, group_size, 1), jnp.float32),
        jnp.zeros((head_count, tokens, group_size, HEAD), jnp.float32),
    )
    before = sweep(
        fresh_state, query_rows, lax.all_gather(prefix_rows, "seq", axis=0, tiled=True), no_mask
    )
    first_row = lax.axis_index("seq") * tokens
    query_pos = first_row + jnp.arange(tokens, dtype=jnp.int32)
    query_seg = suffix_seg[0]
    first_index = jnp.int32(0)
    kv_rows = lax.all_gather(suffix_kv[0], "seq", axis=0, tiled=True)
    key_segments = lax.all_gather(suffix_seg[0], "seq", axis=0, tiled=True)

    def mask_for(offset, block_rows):
        block_seg = lax.dynamic_slice_in_dim(key_segments, offset, block_rows, 0)
        key_pos = first_index + offset + jnp.arange(block_rows, dtype=jnp.int32)
        return (block_seg[None, :] == query_seg[:, None]) & (key_pos[None, :] <= query_pos[:, None])

    combined = sweep(fresh_state, query_rows, kv_rows, mask_for)
    final_state = combine(before, combined)
    outcome = final_state[2] / final_state[1]
    return outcome.transpose(1, 0, 2, 3).reshape(1, tokens, -1).astype(jnp.bfloat16)

MESH = pl.DeviceIdType.MESH
SKEW = 2
EXP2_SCALE = math.log2(math.e) / math.sqrt(HEAD)


def choose(flag, first, second):
    return lax.select(flag != 0, first, second)


def fused_kernel(
    lanes, heads, group_size,
    owner, group_of, pages, queries, suffix, seg_row, pool,
    out,
    own, mate, sg, qseg, wants, wanted,
    right_in, left_in, right_out, left_out, kv, skv, qs, bias,
    score_0, score_1, weight_0, weight_1, factor_0, factor_1,
    m_ref, l_ref, acc, spare,
    pages_0, pages_1, pages_2, pages_3, sem_load,
    sem_right_s, sem_right_r, sem_left_s, sem_left_r, sem_x_s, sem_x_r,
    sem_mate_s, sem_mate_r, sem_q_s, sem_q_r, sem_skv_s, sem_skv_r,
    sem_xskv_s, sem_xskv_r, sem_sg_s, sem_sg_r, sem_want_s, sem_want_r,
    sem_out_s, sem_out_r,
):
    z = lax.axis_index("group")
    s = lax.axis_index("seq")
    x = s // 2
    c = lax.rem(s, 2)
    chunks, rows = own.shape[:2]
    mine = heads // 2
    tokens = queries.shape[0]
    width = mine * group_size * HEAD
    pair = 2 * HEAD
    partner = s + 1 - 2 * c
    across = lax.rem(s + 2, 4)
    mid = (z == 1) | (z == 2)
    per_head = chunks // mine
    half = per_head // 2

    owner_0, owner_1, want = owner[0], owner[1], group_of[0]
    owner_mine = jnp.where(want == 1, owner_1, owner_0)

    wanted[...] = jnp.zeros_like(wanted)
    pages_in = (pages_0, pages_1, pages_2, pages_3)
    barrier = pltpu.get_barrier_semaphore()
    for there in (partner, across):
        pl.semaphore_signal(barrier, inc=1, device_id={"seq": there}, device_id_type=MESH)

    @pl.when(z > 0)
    def _():
        pl.semaphore_signal(barrier, inc=1, device_id={"group": z - 1}, device_id_type=MESH)

    @pl.when(z < 3)
    def _():
        pl.semaphore_signal(barrier, inc=1, device_id={"group": z + 1}, device_id_type=MESH)

    wants[...] = jnp.broadcast_to(want, wants.shape)
    sg[0, c] = jnp.broadcast_to(seg_row[...], sg.shape[2:])

    owned = jnp.where(owner_1 == z, 1, 0)
    page = pool.shape[1]
    in_part = rows // page

    def columns(core, h):
        return pl.ds(pl.multiple_of((core * mine + h) * pair, pair), pair)

    def load_pages(e):
        core = c if e < mine else 1 - c
        return pltpu.make_async_copy(
            pool.at[:, :, columns(core, e % mine)], pages_in[e], sem_load.at[e]
        )

    def load_suffix(h):
        return pltpu.make_async_copy(
            suffix.at[:, columns(c, h)], skv.at[0, h, c], sem_load.at[2 * mine + h]
        )

    def load_queries():
        cols = pl.ds(pl.multiple_of(c * width, HEAD), width)
        return pltpu.make_async_copy(queries.at[:, cols], qs.at[c], sem_load.at[3 * mine])

    def place_pages(e):
        load_pages(e).wait()
        first = e * per_head if e < mine else (e - mine) * half
        into = own if e < mine else mate

        @pl.loop(0, pages.shape[1])
        def _(j):
            place = pl.ds(pl.multiple_of(lax.rem(j, in_part) * page, page), page)
            into[first + j // in_part, place, :] = pages_in[e][pages[owned, j]]

    load_pages(0).start()
    for h in range(mine):
        load_suffix(h).start()
    load_queries().start()
    for h in range(mine):
        load_pages(mine + h).start()
        if h + 1 < mine:
            load_pages(h + 1).start()
    place_pages(0)

    pl.semaphore_wait(barrier, jnp.where(mid, 4, 3))

    def move(src, dst, send, recv, axis, there):
        return pltpu.make_async_remote_copy(
            src_ref=src, dst_ref=dst, send_sem=send, recv_sem=recv,
            device_id={axis: there}, device_id_type=MESH,
        )

    def right(lane, k, src=None):
        return move(
            right_out.at[lane, k] if src is None else src, right_in.at[lane, k],
            sem_right_s.at[lane, k], sem_right_r.at[lane, k], "group", lax.rem(z + 1, 4),
        )

    def left(lane, k, src=None):
        return move(
            left_out.at[lane, k] if src is None else src, left_in.at[lane, k],
            sem_left_s.at[lane, k], sem_left_r.at[lane, k], "group", lax.rem(z + 3, 4),
        )

    def cross(k):
        return move(kv.at[k, 0], kv.at[k, 1], sem_x_s.at[k], sem_x_r.at[k], "seq", across)

    def mate_copy(e):
        to = e // half * per_head + half + lax.rem(e, half)
        return move(
            mate.at[e], own.at[to], sem_mate_s.at[e], sem_mate_r.at[e], "seq", partner
        )

    def query_copy():
        cols = pl.ds(pl.multiple_of((1 - c) * width, HEAD), width)
        return move(queries.at[:, cols], qs.at[c], sem_q_s, sem_q_r, "seq", partner)

    def suffix_copy(h):
        return move(
            suffix.at[:, columns(1 - c, h)], skv.at[0, h, c],
            sem_skv_s.at[h], sem_skv_r.at[h], "seq", partner,
        )

    def suffix_cross(h):
        return move(
            skv.at[0, h], skv.at[1, h], sem_xskv_s.at[h], sem_xskv_r.at[h], "seq", across
        )

    def seg_copy():
        return move(sg.at[0, c], sg.at[0, c], sem_sg_s.at[0], sem_sg_r.at[0], "seq", partner)

    def seg_cross():
        return move(sg.at[0], sg.at[1], sem_sg_s.at[1], sem_sg_r.at[1], "seq", across)

    def want_copy(there):
        return move(wants, wanted, sem_want_s, sem_want_r, "group", there)

    def out_copy(h):
        cols = pl.ds(
            pl.multiple_of((c * mine + h) * group_size * HEAD, HEAD), group_size * HEAD
        )
        return move(
            spare.at[h], out.at[:, cols], sem_out_s.at[h], sem_out_r.at[h], "seq", partner
        )

    def from_edge(first, last):
        @pl.when(z == 0)
        def _():
            @pl.loop(first, last)
            def _(k):
                right(0, k, own.at[k]).start()

        @pl.when(z == 3)
        def _():
            @pl.loop(first, last)
            def _(k):
                left(0, k, own.at[k]).start()

    @pl.when((z == 0) | (z == 3))
    def _():
        want_copy(jnp.where(z == 0, 1, 2)).start()

    from_edge(0, half)
    seg_copy().start()
    for h in range(mine):
        suffix_copy(h).start()
    query_copy().start()

    for h in range(mine):
        place_pages(mine + h)

        @pl.loop(h * half, (h + 1) * half)
        def _(e):
            mate_copy(e).start()

    seg_copy().wait_recv()
    for h in range(mine):
        load_suffix(h).wait()
        suffix_copy(h).wait_recv()

    @pl.when(x == 0)
    def _():
        seg_cross().start()
        for h in range(mine):
            suffix_cross(h).start()

    for h in range(1, mine):
        place_pages(h)

    @pl.loop(0, mine * half)
    def _(e):
        mate_copy(e).wait_recv()

    from_edge(half, chunks)
    for a in range(2):
        qseg[a] = jnp.broadcast_to(sg[0, a, :1, :], (HEAD, tokens)).T
    load_queries().wait()
    query_copy().wait_recv()

    scores, weights, factors = (
        (score_0, score_1), (weight_0, weight_1), (factor_0, factor_1)
    )

    def attend(h, tiles, count, block, init, masks):
        def place(tile):
            return (h * 2 + tile[0]) * group_size + tile[1]

        def multiply(t):
            a, i = tiles[t]
            col = pl.multiple_of((h * group_size + i) * HEAD, HEAD)
            scores[t % 2][:, :count] = lax.dot_general(
                qs[a, :, pl.ds(col, HEAD)], block()[:, :HEAD],
                (((1,), (1,)), ((), ())), preferred_element_type=jnp.float32,
            )

        def soften(t):
            sc = scores[t % 2][:, :count]
            if masks is not None:
                sc = jnp.minimum(sc, masks[tiles[t][0]])
            at = place(tiles[t])
            top = jnp.broadcast_to(jnp.max(sc, axis=1, keepdims=True), (tokens, HEAD))
            if not init:
                old = m_ref[at]
                top = jnp.maximum(old, top)
                factors[t % 2][...] = jnp.exp2((old - top) * EXP2_SCALE)
            m_ref[at] = top
            w = jnp.exp2((sc - top[:, :1]) * EXP2_SCALE)
            weights[t % 2][:, :count] = w.astype(jnp.bfloat16)

        def gather(t):
            at = place(tiles[t])
            values = jnp.concatenate(
                [block()[:, HEAD:], jnp.ones((count, HEAD), jnp.bfloat16)], axis=1
            )
            add = jnp.dot(
                weights[t % 2][:, :count], values, preferred_element_type=jnp.float32
            )
            if init:
                acc[at] = add[:, :HEAD]
                l_ref[at] = add[:, HEAD:]
            else:
                factor = factors[t % 2][...]
                acc[at] = acc[at] * factor + add[:, :HEAD]
                l_ref[at] = l_ref[at] * factor + add[:, HEAD:]

        multiply(0)
        for t in range(len(tiles)):
            if t + 1 < len(tiles):
                multiply(t + 1)
            if t > 0:
                gather(t - 1)
            soften(t)
        gather(len(tiles) - 1)

    def set_bias(side):
        for a in range(2):
            k_seg = jnp.concatenate([sg[side, b, :1, :] for b in range(2)], axis=1)
            seen = k_seg == qseg[a][:, :1]
            if side == 0:
                q_off = a * tokens + lax.broadcasted_iota(jnp.int32, seen.shape, 0)
                seen = seen & (lax.broadcasted_iota(jnp.int32, seen.shape, 1) <= q_off)
            bias[a] = jnp.where(seen, jnp.inf, NEG_FILL)

    def attend_suffix(side, h):
        attend(
            h, [(a, i) for a in range(2) for i in range(group_size)], 2 * tokens,
            lambda: skv[side, h].reshape(2 * tokens, pair), side == 0, (bias[0], bias[1]),
        )

    def attend_prefix(part):
        unit = part // 2
        h = unit // (per_head // 2)
        a = lax.rem(part + 1 + c, 2)
        attend(
            h, [(a, i) for i in range(group_size)], 4 * rows,
            lambda: kv[pl.ds(2 * unit, 2)].reshape(4 * rows, pair), False, None,
        )

        @pl.when(lax.rem(unit, per_head // 2) == per_head // 2 - 1)
        def _():
            def ratio(i):
                at = (h * 2 + a) * group_size + i
                return (acc[at] / l_ref[at]).astype(out.dtype)

            @pl.when(a != c)
            def _():
                for i in range(group_size):
                    spare[h, :, i * HEAD : (i + 1) * HEAD] = ratio(i)
                out_copy(h).start()

            @pl.when(a == c)
            def _():
                for i in range(group_size):
                    col = ((c * mine + h) * group_size + i) * HEAD
                    out[:, pl.ds(pl.multiple_of(col, HEAD), HEAD)] = ratio(i)

    depth = SKEW * jnp.maximum(z, 3 - z)
    lag = 2 + 2 * x
    is_mine = (owner_mine == z).astype(jnp.int32)
    from_left = (owner_mine < z).astype(jnp.int32)
    in_lane_1 = (want == 1).astype(jnp.int32)

    def sent_on(lane):
        if lanes == 1:
            return ((owner_0 == z) | (owner_1 == z)).astype(jnp.int32)
        return ((owner_0, owner_1)[lane] == z).astype(jnp.int32)

    @pl.when(mid)
    def _():
        want_copy(jnp.where(z == 1, 0, 3)).wait_recv()

    edge_want = jnp.max(wanted[...])
    edge_owned = (jnp.where(edge_want == 1, owner_1, owner_0) == z).astype(jnp.int32)

    set_bias(0)

    def step(i, carry):
        k_right = i - SKEW * z

        @pl.when(mid & (k_right >= 0) & (k_right < chunks))
        def _():
            k = k_right

            @pl.when(z == 1)
            def _():
                right(0, k).wait_recv()
                for lane in range(lanes):
                    right_out[lane, k] = choose(sent_on(lane), own[k], right_in[0, k])
                    right(lane, k).start()

            @pl.when(z == 2)
            def _():
                for lane in range(lanes):
                    right(lane, k).wait_recv()
                got = right_in[0, k]
                if lanes > 1:
                    got = choose(edge_want, right_in[1, k], got)
                right_out[0, k] = choose(edge_owned, own[k], got)
                right(0, k).start()

        k_left = i - SKEW * (3 - z)

        @pl.when(mid & (k_left >= 0) & (k_left < chunks))
        def _():
            k = k_left

            @pl.when(z == 2)
            def _():
                left(0, k).wait_recv()
                for lane in range(lanes):
                    left_out[lane, k] = choose(sent_on(lane), own[k], left_in[0, k])
                    left(lane, k).start()

            @pl.when(z == 1)
            def _():
                for lane in range(lanes):
                    left(lane, k).wait_recv()
                got = left_in[0, k]
                if lanes > 1:
                    got = choose(edge_want, left_in[1, k], got)
                left_out[0, k] = choose(edge_owned, own[k], got)
                left(0, k).start()

        k_mine = i - depth

        @pl.when((k_mine >= 0) & (k_mine < chunks))
        def _():
            k = k_mine

            @pl.when(z == 0)
            def _():
                left(0, k).wait_recv()
                kv[k, 0] = choose(is_mine, own[k], left_in[0, k])

            @pl.when(z == 3)
            def _():
                right(0, k).wait_recv()
                kv[k, 0] = choose(is_mine, own[k], right_in[0, k])

            @pl.when(z == 1)
            def _():
                came = left_in[0, k]
                if lanes > 1:
                    came = choose(in_lane_1, left_in[1, k], came)
                came = choose(from_left, right_in[0, k], came)
                kv[k, 0] = choose(is_mine, own[k], came)

            @pl.when(z == 2)
            def _():
                came = right_in[0, k]
                if lanes > 1:
                    came = choose(in_lane_1, right_in[1, k], came)
                came = choose(from_left, came, left_in[0, k])
                kv[k, 0] = choose(is_mine, own[k], came)

            cross(k).start()

        @pl.when(i < mine)
        def _():
            attend_suffix(0, i)

        h_far = i - 5

        @pl.when((x == 1) & (h_far == 0))
        def _():
            seg_cross().wait_recv()
            set_bias(1)

        @pl.when((x == 1) & (h_far >= 0) & (h_far < mine))
        def _():
            suffix_cross(h_far).wait_recv()
            attend_suffix(1, h_far)

        part = i - depth - lag

        @pl.when((part >= 0) & (part < chunks))
        def _():
            @pl.when(lax.rem(part, 2) == 0)
            def _():
                cross(part).wait_recv()
                cross(part + 1).wait_recv()

            attend_prefix(part)

        return carry

    lax.fori_loop(0, chunks + depth + lag, step, 0)

    for h in range(mine):
        out_copy(h).wait_recv()
        out_copy(h).wait_send()
        suffix_copy(h).wait_send()
    seg_copy().wait_send()
    query_copy().wait_send()

    @pl.when(x == 0)
    def _():
        seg_cross().wait_send()
        for h in range(mine):
            suffix_cross(h).wait_send()

    @pl.loop(0, mine * half)
    def _(e):
        mate_copy(e).wait_send()

    @pl.when((z == 0) | (z == 3))
    def _():
        want_copy(jnp.where(z == 0, 1, 2)).wait_send()

    @pl.loop(0, chunks)
    def _(k):
        cross(k).wait_send()

        @pl.when(z < 3)
        def _():
            right(0, k).wait_send()

        @pl.when(z > 0)
        def _():
            left(0, k).wait_send()

        if lanes > 1:
            @pl.when(z == 1)
            def _():
                right(1, k).wait_send()

            @pl.when(z == 2)
            def _():
                left(1, k).wait_send()


def fused(lanes, owner, group_of, pages, queries, suffix, seg_row, pool):
    tokens, width = queries.shape
    heads = suffix.shape[1] // (2 * HEAD)
    mine = heads // 2
    q_heads = width // HEAD
    chunks = 2 * pages.shape[1] * pool.shape[1] // tokens * mine
    piece = (tokens, 2 * HEAD)
    count = 4 * tokens
    vmem, smem = pl.BlockSpec(memory_space=pltpu.VMEM), pl.BlockSpec(memory_space=pltpu.SMEM)
    far = pl.BlockSpec(memory_space=pl.ANY)
    dma = pltpu.SemaphoreType.DMA
    bf16, f32, i32 = jnp.bfloat16, jnp.float32, jnp.int32
    return pl.pallas_call(
        functools.partial(fused_kernel, lanes, heads, q_heads // heads),
        out_shape=jax.ShapeDtypeStruct((tokens, width), bf16),
        in_specs=[smem] * 3 + [far, far, vmem, far],
        out_specs=vmem,
        scratch_shapes=[
            pltpu.VMEM((chunks,) + piece, bf16),
            pltpu.VMEM((chunks // 2,) + piece, bf16),
            pltpu.VMEM((2, 2, 8, tokens), i32),
            pltpu.VMEM((2, tokens, HEAD), i32),
            pltpu.VMEM((8, HEAD), i32),
            pltpu.VMEM((8, HEAD), i32),
        ]
        + [pltpu.VMEM((lanes, chunks) + piece, bf16)] * 4
        + [
            pltpu.VMEM((chunks, 2) + piece, bf16),
            pltpu.VMEM((2, mine, 2) + piece, bf16),
            pltpu.VMEM((2, tokens, width // 2), bf16),
            pltpu.VMEM((2, tokens, 2 * tokens), f32),
        ]
        + [pltpu.VMEM((tokens, count), f32)] * 2
        + [pltpu.VMEM((tokens, count), bf16)] * 2
        + [pltpu.VMEM((tokens, HEAD), f32)] * 2
        + [pltpu.VMEM((q_heads, tokens, HEAD), f32)] * 3
        + [
            pltpu.VMEM((mine, tokens, width // heads), bf16),
        ]
        + [pltpu.VMEM(pool.shape[:2] + (2 * HEAD,), bf16)] * heads
        + [dma((3 * mine + 1,))]
        + [dma((lanes, chunks))] * 4
        + [dma((chunks,))] * 2
        + [dma((chunks // 2,))] * 2
        + [dma] * 2
        + [dma((mine,))] * 4
        + [dma((2,))] * 2
        + [dma] * 2
        + [dma((mine,))] * 2,
        compiler_params=pltpu.CompilerParams(
            collective_id=lanes, has_side_effects=True, vmem_limit_bytes=58 << 20
        ),
    )(owner, group_of, pages, queries, suffix, seg_row, pool)


def pipeline(tiles, count, query, block, mask, place, state, buffers, init):
    m_ref, l_ref, acc = state
    scores, weights, factors = buffers
    rows = factors[0].shape[0]

    def multiply(t):
        scores[t % 2][:, :count] = lax.dot_general(
            query(tiles[t]), block(tiles[t])[:, :HEAD],
            (((1,), (1,)), ((), ())), preferred_element_type=jnp.float32,
        )

    def soften(t):
        sc = scores[t % 2][:, :count]
        if mask is not None:
            sc = jnp.minimum(sc, mask(tiles[t]))
        at = place(tiles[t])
        top = jnp.broadcast_to(jnp.max(sc, axis=1, keepdims=True), (rows, HEAD))
        if not init:
            old = m_ref[at]
            top = jnp.maximum(old, top)
            factors[t % 2][...] = jnp.exp2((old - top) * EXP2_SCALE)
        m_ref[at] = top
        w = jnp.exp2((sc - top[:, :1]) * EXP2_SCALE)
        weights[t % 2][:, :count] = w.astype(jnp.bfloat16)

    def gather(t):
        at = place(tiles[t])
        values = jnp.concatenate(
            [block(tiles[t])[:, HEAD:], jnp.ones((count, HEAD), jnp.bfloat16)], axis=1
        )
        add = jnp.dot(weights[t % 2][:, :count], values, preferred_element_type=jnp.float32)
        if init:
            acc[at] = add[:, :HEAD]
            l_ref[at] = add[:, HEAD:]
        else:
            factor = factors[t % 2][...]
            acc[at] = acc[at] * factor + add[:, :HEAD]
            l_ref[at] = l_ref[at] * factor + add[:, HEAD:]

    multiply(0)
    for t in range(len(tiles)):
        if t + 1 < len(tiles):
            multiply(t + 1)
        if t > 0:
            gather(t - 1)
        soften(t)
    gather(len(tiles) - 1)


def moved_kernel(
    flip, heads, group_size,
    owner, group_of, pages, queries, suffix, seg_row, pool,
    out,
    kv, mate, sg, qseg, wants, wanted, skv, qs, bias,
    down_in, down_out, up_q, slots, made, up_in, up_out, back, fin,
    made_ml, up_in_ml, up_out_ml, back_ml, fin_ml,
    score_0, score_1, weight_0, weight_1, factor_0, factor_1,
    m_ref, l_ref, acc, m_job, l_job, acc_job, spare,
    pages_0, pages_1, pages_2, pages_3, sem_load,
    sem_x_s, sem_x_r, sem_mate_s, sem_mate_r, sem_q_s, sem_q_r, sem_skv_s, sem_skv_r,
    sem_xskv_s, sem_xskv_r, sem_sg_s, sem_sg_r, sem_want_s, sem_want_r,
    sem_out_s, sem_out_r, sem_down_s, sem_down_r, sem_upq_s, sem_upq_r,
    sem_up_s, sem_up_r, sem_upml_s, sem_upml_r, sem_back_s, sem_back_r,
    sem_backml_s, sem_backml_r,
):
    z = lax.axis_index("group")
    s = lax.axis_index("seq")
    x = s // 2
    c = lax.rem(s, 2)
    p = 3 - z if flip else z
    toward = -1 if flip else 1
    up = lax.rem(z + toward + 4, 4)
    down = lax.rem(z - toward + 4, 4)
    serves = p < 2
    chunks = kv.shape[1]
    rows = kv.shape[2]
    mine = heads // 2
    tokens = queries.shape[0]
    wide = group_size * HEAD
    pair = 2 * HEAD
    partner = s + 1 - 2 * c
    across = lax.rem(s + 2, 4)
    per_head = chunks // mine
    half = per_head // 2
    jobs = 4 * mine

    owner_0, owner_1, want = owner[0], owner[1], group_of[0]

    pages_in = (pages_0, pages_1, pages_2, pages_3)
    barrier = pltpu.get_barrier_semaphore()
    for there in (partner, across):
        pl.semaphore_signal(barrier, inc=1, device_id={"seq": there}, device_id_type=MESH)
    for k in range(1, 4):
        pl.semaphore_signal(
            barrier, inc=1, device_id={"group": lax.rem(z + k, 4)}, device_id_type=MESH
        )

    wants[...] = jnp.broadcast_to(want, wants.shape)
    wanted[z] = jnp.broadcast_to(want, wants.shape)
    sg[0, c] = jnp.broadcast_to(seg_row[...], sg.shape[2:])

    def query_columns(core, h):
        return pl.ds(pl.multiple_of((core * mine + h) * wide, HEAD), wide)

    def columns(core, h):
        return pl.ds(pl.multiple_of((core * mine + h) * pair, pair), pair)

    def load_pages(e):
        core = c if e < mine else 1 - c
        return pltpu.make_async_copy(
            pool.at[:, :, columns(core, e % mine)], pages_in[e], sem_load.at[e]
        )

    def load_suffix(h):
        return pltpu.make_async_copy(
            suffix.at[:, columns(c, h)], skv.at[0, h, c], sem_load.at[2 * mine + h]
        )

    def load_queries(h):
        return pltpu.make_async_copy(
            queries.at[:, query_columns(c, h)], qs.at[h * 2 + c], sem_load.at[3 * mine + h]
        )

    @pl.when(serves)
    def _():
        load_pages(0).start()

    for h in range(mine):
        load_queries(h).start()
    for h in range(mine):
        load_suffix(h).start()

    @pl.when(serves)
    def _():
        for h in range(mine):
            load_pages(mine + h).start()
            if h + 1 < mine:
                load_pages(h + 1).start()

    owned = jnp.where(owner_1 == z, 1, 0)
    page = pool.shape[1]
    in_part = rows // page

    def place_pages(e):
        load_pages(e).wait()

        @pl.loop(0, pages.shape[1])
        def _(j):
            place = pl.ds(pl.multiple_of(lax.rem(j, in_part) * page, page), page)
            rows_now = pages_in[e][pages[owned, j]]
            if e < mine:
                kv[0, e * per_head + j // in_part, place, :] = rows_now
            else:
                mate[(e - mine) * half + j // in_part, place, :] = rows_now

    @pl.when(serves)
    def _():
        place_pages(0)

    pl.semaphore_wait(barrier, 5)

    def move(src, dst, send, recv, axis, there):
        return pltpu.make_async_remote_copy(
            src_ref=src, dst_ref=dst, send_sem=send, recv_sem=recv,
            device_id={axis: there}, device_id_type=MESH,
        )

    def cross(k):
        return move(kv.at[0, k], kv.at[1, k], sem_x_s.at[k], sem_x_r.at[k], "seq", across)

    def mate_copy(e):
        to = e // half * per_head + half + lax.rem(e, half)
        return move(
            mate.at[e], kv.at[0, to], sem_mate_s.at[e], sem_mate_r.at[e], "seq", partner
        )

    def query_copy(h):
        return move(
            queries.at[:, query_columns(1 - c, h)], qs.at[h * 2 + c],
            sem_q_s.at[h], sem_q_r.at[h], "seq", partner,
        )

    def suffix_copy(h):
        return move(
            suffix.at[:, columns(1 - c, h)], skv.at[0, h, c],
            sem_skv_s.at[h], sem_skv_r.at[h], "seq", partner,
        )

    def suffix_cross(h):
        return move(
            skv.at[0, h], skv.at[1, h], sem_xskv_s.at[h], sem_xskv_r.at[h], "seq", across
        )

    def seg_copy():
        return move(sg.at[0, c], sg.at[0, c], sem_sg_s.at[0], sem_sg_r.at[0], "seq", partner)

    def seg_cross():
        return move(sg.at[0], sg.at[1], sem_sg_s.at[1], sem_sg_r.at[1], "seq", across)

    def want_copy(k, origin):
        return move(
            wants, wanted.at[origin], sem_want_s.at[k - 1], sem_want_r.at[origin],
            "group", lax.rem(z + k, 4),
        )

    def out_copy(h):
        return move(
            spare.at[h], out.at[:, query_columns(c, h)],
            sem_out_s.at[h], sem_out_r.at[h], "seq", partner,
        )

    def send_down(lane, e, src):
        return move(
            src, down_in.at[lane, e], sem_down_s.at[lane, e], sem_down_r.at[lane, e],
            "group", down,
        )

    def send_up_q(e):
        return move(qs.at[e], up_q.at[e], sem_upq_s.at[e], sem_upq_r.at[e], "group", up)

    def send_up(lane, f, src):
        return move(
            src.at[lane, f], up_in.at[lane, f], sem_up_s.at[lane, f], sem_up_r.at[lane, f],
            "group", up,
        )

    def send_up_ml(lane, e, src):
        return move(
            src.at[lane, e], up_in_ml.at[lane, e], sem_upml_s.at[lane, e],
            sem_upml_r.at[lane, e], "group", up,
        )

    def send_back(f):
        return move(made.at[0, f], back.at[f], sem_back_s.at[f], sem_back_r.at[f], "group", down)

    def send_back_ml(e):
        return move(
            made_ml.at[0, e], back_ml.at[e], sem_backml_s.at[e], sem_backml_r.at[e],
            "group", down,
        )

    for k in range(1, 4):
        want_copy(k, z).start()
    seg_copy().start()
    for h in range(mine):
        query_copy(h).start()
    for h in range(mine):
        suffix_copy(h).start()

    @pl.when(serves)
    def _():
        @pl.loop(0, half)
        def _(k):
            cross(k).start()

        for h in range(mine):
            place_pages(mine + h)

            @pl.loop(h * half, (h + 1) * half)
            def _(e):
                mate_copy(e).start()

        for h in range(1, mine):
            place_pages(h)

    for h in range(mine):
        load_queries(h).wait()
        query_copy(h).wait_recv()

    @pl.when(p == 3)
    def _():
        for e in range(2 * mine):
            send_down(1, e, qs.at[e]).start()

    @pl.when(p == 2)
    def _():
        for e in range(2):
            send_down(0, e, qs.at[e]).start()

    @pl.when(p == 0)
    def _():
        for e in range(2 * mine):
            send_up_q(e).start()

    seg_copy().wait_recv()
    for h in range(mine):
        load_suffix(h).wait()
        suffix_copy(h).wait_recv()

    @pl.when(serves)
    def _():
        @pl.loop(0, mine * half)
        def _(e):
            mate_copy(e).wait_recv()

        @pl.loop(half, chunks)
        def _(k):
            cross(k).start()

    @pl.when(x == 0)
    def _():
        seg_cross().start()
        for h in range(mine):
            suffix_cross(h).start()

    for a in range(2):
        qseg[a] = jnp.broadcast_to(sg[0, a, :1, :], (HEAD, tokens)).T

    for k in range(1, 4):
        want_copy(k, lax.rem(z + k, 4)).wait_recv()
    at_0, at_1 = (3 - owner_0, 3 - owner_1) if flip else (owner_0, owner_1)
    served = [
        jnp.where(jnp.max(wanted[3 - q if flip else q]) == 1, at_1, at_0) for q in range(4)
    ]

    def by(server, q):
        return (served[q] == server).astype(jnp.int32)

    split = (served[2] != served[3]).astype(jnp.int32)

    buffers = ((score_0, score_1), (weight_0, weight_1), (factor_0, factor_1))

    def set_bias(side):
        for a in range(2):
            k_seg = jnp.concatenate([sg[side, b, :1, :] for b in range(2)], axis=1)
            seen = k_seg == qseg[a][:, :1]
            if side == 0:
                q_off = a * tokens + lax.broadcasted_iota(jnp.int32, seen.shape, 0)
                seen = seen & (lax.broadcasted_iota(jnp.int32, seen.shape, 1) <= q_off)
            bias[a] = jnp.where(seen, jnp.inf, NEG_FILL)

    def attend_suffix(side, h):
        pipeline(
            [(a, i) for a in range(2) for i in range(group_size)], 2 * tokens,
            lambda t: qs[h * 2 + t[0], :, t[1] * HEAD : (t[1] + 1) * HEAD],
            lambda t: skv[side, h].reshape(2 * tokens, pair),
            lambda t: bias[t[0]],
            lambda t: (h * 2 + t[0]) * group_size + t[1],
            (m_ref, l_ref, acc), buffers, side == 0,
        )

    def event_1(b):
        e = b // 4 * 2 + lax.rem(b, 2)

        @pl.when(lax.rem(b // 2, 2) == 0)
        def _():
            send_down(0, e, down_out.at[0, e]).wait_recv()
            send_up_q(e).wait_recv()
            down_out[0, e] = choose(by(0, 1), qs[e], down_in[0, e])
            send_down(0, e, down_out.at[0, e]).start()
            rest = choose(by(1, 1), qs[e], down_in[0, e])
            slots[0, e] = choose(by(1, 0), up_q[e], rest)

        @pl.when(lax.rem(b // 2, 2) == 1)
        def _():
            send_down(1, e, down_out.at[1, e]).wait_recv()
            rest = choose(by(0, 2), down_in[0, e], qs[e])
            down_out[1, e] = choose(by(0, 3), down_in[1, e], rest)
            send_down(1, e, down_out.at[1, e]).start()
            rest = choose(by(1, 2), down_in[0, e], qs[e])
            slots[1, e] = choose(by(1, 3), down_in[1, e], rest)

    def event_0(b):
        e = b // 4 * 2 + lax.rem(b, 2)

        @pl.when(lax.rem(b // 2, 2) == 0)
        def _():
            send_down(0, e, down_out.at[0, e]).wait_recv()
            slots[0, e] = choose(by(0, 0), qs[e], down_in[0, e])

        @pl.when(lax.rem(b // 2, 2) == 1)
        def _():
            send_down(1, e, down_out.at[1, e]).wait_recv()
            slots[1, e] = down_in[1, e]

    def relay_q(e):
        send_down(1, e, down_in.at[1, e]).wait_recv()
        send_down(1, e, down_in.at[1, e]).start()

    def relay_1(e):
        for f in range(2):
            send_up(0, 2 * e + f, up_out).wait_recv()
        send_up_ml(0, e, up_out_ml).wait_recv()
        for f in range(2):
            rest = choose(by(1, 2), made[0, 2 * e + f], up_in[0, 2 * e + f])
            up_out[0, 2 * e + f] = choose(split, made[1, 2 * e + f], rest)
            send_up(0, 2 * e + f, up_out).start()
        rest = choose(by(1, 2), made_ml[0, e], up_in_ml[0, e])
        up_out_ml[0, e] = choose(split, made_ml[1, e], rest)
        send_up_ml(0, e, up_out_ml).start()

    local_3 = (1 - split) * by(1, 3)

    def relay_2(e):
        for f in range(2):
            send_up(1, 2 * e + f, up_out).wait_recv()
            up_out[1, 2 * e + f] = choose(local_3, made[1, 2 * e + f], up_in[1, 2 * e + f])
            send_up(1, 2 * e + f, up_out).start()
        send_up_ml(1, e, up_out_ml).wait_recv()
        up_out_ml[1, e] = choose(local_3, made_ml[1, e], up_in_ml[1, e])
        send_up_ml(1, e, up_out_ml).start()

    def finish(b, h, j, a):
        e = h * 2 + a
        lane = lax.broadcasted_iota(jnp.int32, (tokens, HEAD), 1)
        packed = jnp.zeros((tokens, HEAD), jnp.float32)
        for i in range(group_size):
            at = i % 2 * HEAD
            tile = a * group_size + i
            ratio = acc_job[tile] / l_job[tile]
            made[j, 2 * e + i // 2, :, at : at + HEAD] = ratio.astype(made.dtype)
            packed = jnp.where(lane == i, m_job[tile], packed)
            packed = jnp.where(lane == group_size + i, l_job[tile], packed)
        made_ml[j, e] = packed.T[:8]

        @pl.when(p == 0)
        def _():
            for f in range(2):
                send_up(j, 2 * e + f, made).start()
            send_up_ml(j, e, made_ml).start()

        @pl.when((p == 1) & (j == 0))
        def _():
            for f in range(2):
                send_back(2 * e + f).start()
            send_back_ml(e).start()

        @pl.when((p == 1) & (j == 1))
        def _():
            relay_1(e)

        @pl.when((p == 1) & (h == 1) & (j == 0))
        def _():
            relay_2(a)

    def serve(n, carry):
        h, r = n // 8, lax.rem(n, 8)
        j = r // 4
        early = (h == 0) & (j == 0)
        a = jnp.where(early, lax.rem(r, 2), lax.rem(r // 2, 2))
        v = jnp.where(early, r // 2, lax.rem(r, 2))
        e = h * 2 + a
        b = h * 4 + j * 2 + a

        @pl.when((p == 0) & (v == 0))
        def _():
            event_0(b)

        for at, due in ((1, 1), (2, 2), (3, 3), (5, 4), (6, 5), (8, 6), (9, 7)):
            @pl.when((p == 1) & (n == at))
            def _():
                event_1(jnp.int32(due))

        @pl.when((v == 1) & (j == 0) & (a == 0))
        def _():
            for k in range(per_head):
                cross(h * per_head + k).wait_recv()

        own_tiles = pl.ds(a * group_size, group_size)

        @pl.when(v == 0)
        def _():
            shape = (group_size,) + m_job.shape[1:]
            m_job[own_tiles] = jnp.full(shape, NEG_FILL, jnp.float32)
            l_job[own_tiles] = jnp.zeros(shape, jnp.float32)
            acc_job[own_tiles] = jnp.zeros(shape, jnp.float32)

        pipeline(
            [(g, i) for g in range(2) for i in range(group_size)], half * rows,
            lambda t: slots[j, e, :, t[1] * HEAD : (t[1] + 1) * HEAD],
            lambda t: kv[v, pl.ds(h * per_head + t[0] * half, half)].reshape(half * rows, pair),
            None, lambda t: a * group_size + t[1], (m_job, l_job, acc_job), buffers, False,
        )

        @pl.when(v == 1)
        def _():
            finish(b, h, j, a)

        return carry

    def merge(e):
        h, a = e // 2, e % 2
        ml = jnp.concatenate([fin_ml[e]] * (HEAD // 8), axis=0).T

        def ratio(i):
            at = e * group_size + i
            lane = i % 2 * HEAD
            near = m_ref[at]
            far = jnp.broadcast_to(ml[:, i : i + 1], (tokens, HEAD))
            top = jnp.maximum(near, far)
            keep = jnp.exp2((near - top) * EXP2_SCALE)
            total = jnp.broadcast_to(
                ml[:, group_size + i : group_size + i + 1], (tokens, HEAD)
            ) * jnp.exp2((far - top) * EXP2_SCALE)
            context = fin[2 * e + i // 2, :, lane : lane + HEAD].astype(jnp.float32)
            both = context * total + acc[at] * keep
            return (both / (total + l_ref[at] * keep)).astype(out.dtype)

        @pl.when(a != c)
        def _():
            for i in range(group_size):
                spare[h, :, i * HEAD : (i + 1) * HEAD] = ratio(i)
            out_copy(h).start()

        @pl.when(a == c)
        def _():
            for i in range(group_size):
                col = ((c * mine + h) * group_size + i) * HEAD
                out[:, pl.ds(pl.multiple_of(col, HEAD), HEAD)] = ratio(i)

    set_bias(0)

    @pl.loop(0, mine)
    def _(h):
        attend_suffix(0, h)

        @pl.when(p == 2)
        def _():
            relay_q(h)

    @pl.when(p == 2)
    def _():
        for e in range(2, 2 * mine):
            send_down(0, e, qs.at[e]).start()

    @pl.when(p == 1)
    def _():
        event_1(jnp.int32(0))

    lax.fori_loop(0, jnp.where(serves, 2 * jobs, 0), serve, 0)

    @pl.when(p == 1)
    def _():
        relay_2(2)

    @pl.when(x == 1)
    def _():
        seg_cross().wait_recv()
        set_bias(1)

    @pl.loop(0, mine)
    def _(h):
        @pl.when(x == 1)
        def _():
            suffix_cross(h).wait_recv()
            attend_suffix(1, h)

        @pl.when(p == 2)
        def _():
            relay_q(2 + h)

    @pl.when(p == 1)
    def _():
        relay_2(3)

    for e in range(2 * mine):
        both = (2 * e, 2 * e + 1)

        @pl.when(p == 0)
        def _():
            for f in both:
                send_back(f).wait_recv()
                fin[f] = choose(by(0, 0), made[0, f], back[f])
            send_back_ml(e).wait_recv()
            fin_ml[e] = choose(by(0, 0), made_ml[0, e], back_ml[e])

        @pl.when(p == 1)
        def _():
            def pick(have, came, at):
                here = choose(by(1, 0), have[1, at], have[0, at])
                there = choose(by(0, 0), came[1, at], came[0, at])
                return choose(by(1, 1), here, there)

            for f in both:
                fin[f] = pick(made, up_in, f)
            fin_ml[e] = pick(made_ml, up_in_ml, e)

        @pl.when(p == 2)
        def _():
            late_2 = split * by(0, 2)
            early_3 = split * by(1, 3)
            for f in both:
                send_up(0, f, up_out).wait_recv()
                send_up(1, f, up_out).wait_recv()
                up_out[1, f] = choose(early_3, up_in[0, f], up_in[1, f])
                send_up(1, f, up_out).start()
                fin[f] = choose(late_2, up_in[1, f], up_in[0, f])
            send_up_ml(0, e, up_out_ml).wait_recv()
            send_up_ml(1, e, up_out_ml).wait_recv()
            up_out_ml[1, e] = choose(early_3, up_in_ml[0, e], up_in_ml[1, e])
            send_up_ml(1, e, up_out_ml).start()
            fin_ml[e] = choose(late_2, up_in_ml[1, e], up_in_ml[0, e])

        @pl.when(p == 3)
        def _():
            for f in both:
                send_up(1, f, up_out).wait_recv()
                fin[f] = up_in[1, f]
            send_up_ml(1, e, up_out_ml).wait_recv()
            fin_ml[e] = up_in_ml[1, e]

        merge(e)

    for k in range(1, 4):
        want_copy(k, z).wait_send()
    for h in range(mine):
        out_copy(h).wait_recv()
        out_copy(h).wait_send()
        suffix_copy(h).wait_send()
        query_copy(h).wait_send()
    seg_copy().wait_send()

    @pl.when(x == 0)
    def _():
        seg_cross().wait_send()
        for h in range(mine):
            suffix_cross(h).wait_send()

    @pl.when(serves)
    def _():
        @pl.loop(0, mine * half)
        def _(e):
            mate_copy(e).wait_send()

        @pl.loop(0, chunks)
        def _(k):
            cross(k).wait_send()

    for e in range(2 * mine):
        @pl.when((p == 1) | (p == 2))
        def _():
            send_down(0, e, qs.at[e]).wait_send()

        @pl.when(p > 0)
        def _():
            send_down(1, e, qs.at[e]).wait_send()

        @pl.when(p < 2)
        def _():
            send_up_ml(0, e, up_out_ml).wait_send()
            for f in range(2):
                send_up(0, 2 * e + f, up_out).wait_send()

        @pl.when(p < 3)
        def _():
            send_up_ml(1, e, up_out_ml).wait_send()
            for f in range(2):
                send_up(1, 2 * e + f, up_out).wait_send()

        @pl.when(p == 0)
        def _():
            send_up_q(e).wait_send()

        @pl.when(p == 1)
        def _():
            send_back_ml(e).wait_send()
            for f in range(2):
                send_back(2 * e + f).wait_send()


def moved(flip, owner, group_of, pages, queries, suffix, seg_row, pool):
    tokens, width = queries.shape
    heads = suffix.shape[1] // (2 * HEAD)
    mine = heads // 2
    q_heads = width // HEAD
    group_size = q_heads // heads
    chunks = 2 * pages.shape[1] * pool.shape[1] // tokens * mine
    piece = (tokens, 2 * HEAD)
    query = (tokens, group_size * HEAD)
    count = 4 * tokens
    vmem, smem = pl.BlockSpec(memory_space=pltpu.VMEM), pl.BlockSpec(memory_space=pltpu.SMEM)
    far = pl.BlockSpec(memory_space=pl.ANY)
    dma = pltpu.SemaphoreType.DMA
    bf16, f32, i32 = jnp.bfloat16, jnp.float32, jnp.int32
    parts = 2 * mine
    return pl.pallas_call(
        functools.partial(moved_kernel, flip, heads, group_size),
        out_shape=jax.ShapeDtypeStruct((tokens, width), bf16),
        in_specs=[smem] * 3 + [far, far, vmem, far],
        out_specs=vmem,
        scratch_shapes=[
            pltpu.VMEM((2, chunks) + piece, bf16),
            pltpu.VMEM((chunks // 2,) + piece, bf16),
            pltpu.VMEM((2, 2, 8, tokens), i32),
            pltpu.VMEM((2, tokens, HEAD), i32),
            pltpu.VMEM((8, HEAD), i32),
            pltpu.VMEM((4, 8, HEAD), i32),
            pltpu.VMEM((2, mine, 2) + piece, bf16),
            pltpu.VMEM((parts,) + query, bf16),
            pltpu.VMEM((2, tokens, 2 * tokens), f32),
        ]
        + [pltpu.VMEM((2, parts) + query, bf16)] * 2
        + [
            pltpu.VMEM((parts,) + query, bf16),
            pltpu.VMEM((2, parts) + query, bf16),
        ]
        + [pltpu.VMEM((2, 2 * parts) + piece, bf16)] * 3
        + [pltpu.VMEM((2 * parts,) + piece, bf16)] * 2
        + [pltpu.VMEM((2, parts, 8, tokens), f32)] * 3
        + [pltpu.VMEM((parts, 8, tokens), f32)] * 2
        + [pltpu.VMEM((tokens, count), f32)] * 2
        + [pltpu.VMEM((tokens, count), bf16)] * 2
        + [pltpu.VMEM((tokens, HEAD), f32)] * 2
        + [pltpu.VMEM((q_heads, tokens, HEAD), f32)] * 3
        + [pltpu.VMEM((2 * group_size, tokens, HEAD), f32)] * 3
        + [
            pltpu.VMEM((mine,) + query, bf16),
        ]
        + [pltpu.VMEM(pool.shape[:2] + (2 * HEAD,), bf16)] * heads
        + [dma((4 * mine,))]
        + [dma((chunks,))] * 2
        + [dma((chunks // 2,))] * 2
        + [dma((mine,))] * 6
        + [dma((2,))] * 2
        + [dma((3,)), dma((4,))]
        + [dma((mine,))] * 2
        + [dma((2, parts))] * 2
        + [dma((parts,))] * 2
        + [dma((2, 2 * parts))] * 2
        + [dma((2, parts))] * 2
        + [dma((2 * parts,))] * 2
        + [dma((parts,))] * 2,
        compiler_params=pltpu.CompilerParams(
            collective_id=2 + flip, has_side_effects=True, vmem_limit_bytes=58 << 20
        ),
    )(owner, group_of, pages, queries, suffix, seg_row, pool)


def local_fused(queries, suffix_kv, suffix_seg, prefix_pool, page_table, owner, group_of):
    args = (owner, group_of, page_table, queries[0], suffix_kv[0], suffix_seg, prefix_pool[0])
    low = (owner < 2).astype(jnp.int32)
    plans = [
        functools.partial(moved, 1), functools.partial(fused, 1), functools.partial(moved, 0)
    ]
    return lax.switch(low[0] + low[1], plans, *args)[None]


def fits(mesh):
    return dict(mesh.shape) == {"group": 4, "seq": 4, "tensor": 2}


def solution(mesh):
    return jax.shard_map(
        local_fused if fits(mesh) else local,
        mesh=mesh,
        in_specs=(
            P("group", "seq", "tensor"),
            P("group", "seq", "tensor"),
            P("group", "seq"),
            P("group", "seq", None, "tensor"),
            P(None, "seq"),
            P(),
            P("group"),
        ),
        out_specs=P("group", "seq", "tensor"),
        check_vma=False,
    )
```

```python
import functools
import math

import jax
import jax.numpy as jnp
from jax import lax
from jax.experimental import pallas as pl
from jax.experimental.pallas import tpu as pltpu
from jax.sharding import PartitionSpec as P

HEAD = 128


NEG_FILL = -1e30


def broadcast(value, axis, root):
    mine = lax.axis_index(axis) == root
    return lax.psum(jnp.where(mine, value, jnp.zeros_like(value)), axis)


def absorb(carried, query_rows, key_block, valid):
    running_max, running_sum, accumulator = carried
    scale = 1.0 / math.sqrt(HEAD)
    key_rows = key_block[:, :, 0, :]
    value_rows = key_block[:, :, 1, :]
    scores = (
        jnp.einsum("thgd,khd->htgk", query_rows, key_rows, preferred_element_type=jnp.float32)
        * scale
    )
    if valid is not None:
        scores = jnp.where(valid[None, :, None, :], scores, NEG_FILL)
    new_max = jnp.maximum(running_max, jnp.max(scores, axis=-1, keepdims=True))
    weight = jnp.exp(scores - new_max)
    if valid is not None:
        weight = jnp.where(valid[None, :, None, :], weight, 0.0)
    factor = jnp.exp(running_max - new_max)
    running_sum = running_sum * factor + jnp.sum(weight, axis=-1, keepdims=True)
    accumulator = accumulator * factor + jnp.einsum(
        "htgk,khd->htgd",
        weight.astype(jnp.bfloat16),
        value_rows,
        preferred_element_type=jnp.float32,
    )
    return (new_max, running_sum, accumulator)


def sweep(carried, query_rows, kv_rows, mask_for):
    row_count = kv_rows.shape[0]
    block_rows = math.gcd(row_count, 1024)
    head_count = kv_rows.shape[1] // (2 * HEAD)

    def absorb_block(block_index, state_now):
        offset = block_index * block_rows
        key_block = lax.dynamic_slice_in_dim(kv_rows, offset, block_rows, 0).reshape(
            block_rows, head_count, 2, HEAD
        )
        return absorb(state_now, query_rows, key_block, mask_for(offset, block_rows))

    if row_count == block_rows:
        return absorb_block(0, carried)
    return lax.fori_loop(0, row_count // block_rows, absorb_block, carried)


def combine(earlier, later):
    new_max = jnp.maximum(earlier[0], later[0])
    scale_first = jnp.exp(earlier[0] - new_max)
    scale_second = jnp.exp(later[0] - new_max)
    return (
        new_max,
        earlier[1] * scale_first + later[1] * scale_second,
        earlier[2] * scale_first + later[2] * scale_second,
    )


def no_mask(offset, block_rows):
    return None


def local(queries, suffix_kv, suffix_seg, prefix_pool, page_table, owner, group_of):
    tokens = queries.shape[1]
    row_width = suffix_kv.shape[-1]
    head_count = row_width // (2 * HEAD)
    group_size = queries.shape[-1] // (head_count * HEAD)
    query_rows = queries[0].reshape(tokens, head_count, group_size, HEAD)
    page_pool = prefix_pool[0]
    my_group = group_of[0]
    held_shape = (page_table.shape[1] * page_pool.shape[1], row_width)

    def compact(slot_ids):
        def put(j, rows):
            page = lax.dynamic_slice_in_dim(page_pool, slot_ids[j], 1, 0)
            return lax.dynamic_update_slice_in_dim(rows, page, j, 0)

        count = slot_ids.shape[0]
        rows = jnp.zeros((count,) + page_pool.shape[1:], page_pool.dtype)
        return lax.fori_loop(0, count, put, rows).reshape(-1, row_width)

    def visit_group(request, held_pages):
        moved_pages = broadcast(compact(page_table[request]), "group", owner[request])
        return jnp.where(request == my_group, moved_pages, held_pages)

    prefix_rows = lax.fori_loop(
        0, page_table.shape[0], visit_group, jnp.zeros(held_shape, jnp.bfloat16)
    )
    fresh_state = (
        jnp.full((head_count, tokens, group_size, 1), NEG_FILL, jnp.float32),
        jnp.zeros((head_count, tokens, group_size, 1), jnp.float32),
        jnp.zeros((head_count, tokens, group_size, HEAD), jnp.float32),
    )
    before = sweep(
        fresh_state, query_rows, lax.all_gather(prefix_rows, "seq", axis=0, tiled=True), no_mask
    )
    first_row = lax.axis_index("seq") * tokens
    query_pos = first_row + jnp.arange(tokens, dtype=jnp.int32)
    query_seg = suffix_seg[0]
    first_index = jnp.int32(0)
    kv_rows = lax.all_gather(suffix_kv[0], "seq", axis=0, tiled=True)
    key_segments = lax.all_gather(suffix_seg[0], "seq", axis=0, tiled=True)

    def mask_for(offset, block_rows):
        block_seg = lax.dynamic_slice_in_dim(key_segments, offset, block_rows, 0)
        key_pos = first_index + offset + jnp.arange(block_rows, dtype=jnp.int32)
        return (block_seg[None, :] == query_seg[:, None]) & (key_pos[None, :] <= query_pos[:, None])

    combined = sweep(fresh_state, query_rows, kv_rows, mask_for)
    final_state = combine(before, combined)
    outcome = final_state[2] / final_state[1]
    return outcome.transpose(1, 0, 2, 3).reshape(1, tokens, -1).astype(jnp.bfloat16)

MESH = pl.DeviceIdType.MESH
SKEW = 2
EXP2_SCALE = math.log2(math.e) / math.sqrt(HEAD)


def choose(flag, first, second):
    return lax.select(flag != 0, first, second)


def fused_kernel(
    lanes, heads, group_size,
    owner, group_of, pages, queries, suffix, seg_row, pool,
    out,
    own, mate, sg, qseg, wants, wanted,
    right_in, left_in, right_out, left_out, kv, skv, qs, bias,
    score_0, score_1, weight_0, weight_1, factor_0, factor_1,
    m_ref, l_ref, acc, spare,
    pages_0, pages_1, pages_2, pages_3, sem_load,
    sem_right_s, sem_right_r, sem_left_s, sem_left_r, sem_x_s, sem_x_r,
    sem_mate_s, sem_mate_r, sem_q_s, sem_q_r, sem_skv_s, sem_skv_r,
    sem_xskv_s, sem_xskv_r, sem_sg_s, sem_sg_r, sem_want_s, sem_want_r,
    sem_out_s, sem_out_r,
):
    z = lax.axis_index("group")
    s = lax.axis_index("seq")
    x = s // 2
    c = lax.rem(s, 2)
    chunks, rows = own.shape[:2]
    mine = heads // 2
    tokens = queries.shape[0]
    width = mine * group_size * HEAD
    pair = 2 * HEAD
    partner = s + 1 - 2 * c
    across = lax.rem(s + 2, 4)
    mid = (z == 1) | (z == 2)
    per_head = chunks // mine
    half = per_head // 2

    owner_0, owner_1, want = owner[0], owner[1], group_of[0]
    owner_mine = jnp.where(want == 1, owner_1, owner_0)

    wanted[...] = jnp.zeros_like(wanted)
    pages_in = (pages_0, pages_1, pages_2, pages_3)
    barrier = pltpu.get_barrier_semaphore()
    for there in (partner, across):
        pl.semaphore_signal(barrier, inc=1, device_id={"seq": there}, device_id_type=MESH)

    @pl.when(z > 0)
    def _():
        pl.semaphore_signal(barrier, inc=1, device_id={"group": z - 1}, device_id_type=MESH)

    @pl.when(z < 3)
    def _():
        pl.semaphore_signal(barrier, inc=1, device_id={"group": z + 1}, device_id_type=MESH)

    wants[...] = jnp.broadcast_to(want, wants.shape)
    sg[0, c] = jnp.broadcast_to(seg_row[...], sg.shape[2:])

    owned = jnp.where(owner_1 == z, 1, 0)
    page = pool.shape[1]
    in_part = rows // page

    def columns(core, h):
        return pl.ds(pl.multiple_of((core * mine + h) * pair, pair), pair)

    def load_pages(e):
        core = c if e < mine else 1 - c
        return pltpu.make_async_copy(
            pool.at[:, :, columns(core, e % mine)], pages_in[e], sem_load.at[e]
        )

    def load_suffix(h):
        return pltpu.make_async_copy(
            suffix.at[:, columns(c, h)], skv.at[0, h, c], sem_load.at[2 * mine + h]
        )

    def load_queries():
        cols = pl.ds(pl.multiple_of(c * width, HEAD), width)
        return pltpu.make_async_copy(queries.at[:, cols], qs.at[c], sem_load.at[3 * mine])

    def place_pages(e):
        load_pages(e).wait()
        first = e * per_head if e < mine else (e - mine) * half
        into = own if e < mine else mate

        @pl.loop(0, pages.shape[1])
        def _(j):
            place = pl.ds(pl.multiple_of(lax.rem(j, in_part) * page, page), page)
            into[first + j // in_part, place, :] = pages_in[e][pages[owned, j]]

    load_pages(0).start()
    for h in range(mine):
        load_suffix(h).start()
    load_queries().start()
    for h in range(mine):
        load_pages(mine + h).start()
        if h + 1 < mine:
            load_pages(h + 1).start()
    place_pages(0)

    pl.semaphore_wait(barrier, jnp.where(mid, 4, 3))

    def move(src, dst, send, recv, axis, there):
        return pltpu.make_async_remote_copy(
            src_ref=src, dst_ref=dst, send_sem=send, recv_sem=recv,
            device_id={axis: there}, device_id_type=MESH,
        )

    def right(lane, k, src=None):
        return move(
            right_out.at[lane, k] if src is None else src, right_in.at[lane, k],
            sem_right_s.at[lane, k], sem_right_r.at[lane, k], "group", lax.rem(z + 1, 4),
        )

    def left(lane, k, src=None):
        return move(
            left_out.at[lane, k] if src is None else src, left_in.at[lane, k],
            sem_left_s.at[lane, k], sem_left_r.at[lane, k], "group", lax.rem(z + 3, 4),
        )

    def cross(k):
        return move(kv.at[k, 0], kv.at[k, 1], sem_x_s.at[k], sem_x_r.at[k], "seq", across)

    def mate_copy(e):
        to = e // half * per_head + half + lax.rem(e, half)
        return move(
            mate.at[e], own.at[to], sem_mate_s.at[e], sem_mate_r.at[e], "seq", partner
        )

    def query_copy():
        cols = pl.ds(pl.multiple_of((1 - c) * width, HEAD), width)
        return move(queries.at[:, cols], qs.at[c], sem_q_s, sem_q_r, "seq", partner)

    def suffix_copy(h):
        return move(
            suffix.at[:, columns(1 - c, h)], skv.at[0, h, c],
            sem_skv_s.at[h], sem_skv_r.at[h], "seq", partner,
        )

    def suffix_cross(h):
        return move(
            skv.at[0, h], skv.at[1, h], sem_xskv_s.at[h], sem_xskv_r.at[h], "seq", across
        )

    def seg_copy():
        return move(sg.at[0, c], sg.at[0, c], sem_sg_s.at[0], sem_sg_r.at[0], "seq", partner)

    def seg_cross():
        return move(sg.at[0], sg.at[1], sem_sg_s.at[1], sem_sg_r.at[1], "seq", across)

    def want_copy(there):
        return move(wants, wanted, sem_want_s, sem_want_r, "group", there)

    def out_copy(h):
        cols = pl.ds(
            pl.multiple_of((c * mine + h) * group_size * HEAD, HEAD), group_size * HEAD
        )
        return move(
            spare.at[h], out.at[:, cols], sem_out_s.at[h], sem_out_r.at[h], "seq", partner
        )

    def from_edge(first, last):
        @pl.when(z == 0)
        def _():
            @pl.loop(first, last)
            def _(k):
                right(0, k, own.at[k]).start()

        @pl.when(z == 3)
        def _():
            @pl.loop(first, last)
            def _(k):
                left(0, k, own.at[k]).start()

    @pl.when((z == 0) | (z == 3))
    def _():
        want_copy(jnp.where(z == 0, 1, 2)).start()

    from_edge(0, half)
    seg_copy().start()
    for h in range(mine):
        suffix_copy(h).start()
    query_copy().start()

    for h in range(mine):
        place_pages(mine + h)

        @pl.loop(h * half, (h + 1) * half)
        def _(e):
            mate_copy(e).start()

    seg_copy().wait_recv()
    for h in range(mine):
        load_suffix(h).wait()
        suffix_copy(h).wait_recv()

    @pl.when(x == 0)
    def _():
        seg_cross().start()
        for h in range(mine):
            suffix_cross(h).start()

    for h in range(1, mine):
        place_pages(h)

    @pl.loop(0, mine * half)
    def _(e):
        mate_copy(e).wait_recv()

    from_edge(half, chunks)
    for a in range(2):
        qseg[a] = jnp.broadcast_to(sg[0, a, :1, :], (HEAD, tokens)).T
    load_queries().wait()
    query_copy().wait_recv()

    scores, weights, factors = (
        (score_0, score_1), (weight_0, weight_1), (factor_0, factor_1)
    )

    def attend(h, tiles, count, block, init, masks):
        def place(tile):
            return (h * 2 + tile[0]) * group_size + tile[1]

        def multiply(t):
            a, i = tiles[t]
            col = pl.multiple_of((h * group_size + i) * HEAD, HEAD)
            scores[t % 2][:, :count] = lax.dot_general(
                qs[a, :, pl.ds(col, HEAD)], block()[:, :HEAD],
                (((1,), (1,)), ((), ())), preferred_element_type=jnp.float32,
            )

        def soften(t):
            sc = scores[t % 2][:, :count]
            if masks is not None:
                sc = jnp.minimum(sc, masks[tiles[t][0]])
            at = place(tiles[t])
            top = jnp.broadcast_to(jnp.max(sc, axis=1, keepdims=True), (tokens, HEAD))
            if not init:
                old = m_ref[at]
                top = jnp.maximum(old, top)
                factors[t % 2][...] = jnp.exp2((old - top) * EXP2_SCALE)
            m_ref[at] = top
            w = jnp.exp2((sc - top[:, :1]) * EXP2_SCALE)
            weights[t % 2][:, :count] = w.astype(jnp.bfloat16)

        def gather(t):
            at = place(tiles[t])
            values = jnp.concatenate(
                [block()[:, HEAD:], jnp.ones((count, HEAD), jnp.bfloat16)], axis=1
            )
            add = jnp.dot(
                weights[t % 2][:, :count], values, preferred_element_type=jnp.float32
            )
            if init:
                acc[at] = add[:, :HEAD]
                l_ref[at] = add[:, HEAD:]
            else:
                factor = factors[t % 2][...]
                acc[at] = acc[at] * factor + add[:, :HEAD]
                l_ref[at] = l_ref[at] * factor + add[:, HEAD:]

        multiply(0)
        for t in range(len(tiles)):
            if t + 1 < len(tiles):
                multiply(t + 1)
            if t > 0:
                gather(t - 1)
            soften(t)
        gather(len(tiles) - 1)

    def set_bias(side):
        for a in range(2):
            k_seg = jnp.concatenate([sg[side, b, :1, :] for b in range(2)], axis=1)
            seen = k_seg == qseg[a][:, :1]
            if side == 0:
                q_off = a * tokens + lax.broadcasted_iota(jnp.int32, seen.shape, 0)
                seen = seen & (lax.broadcasted_iota(jnp.int32, seen.shape, 1) <= q_off)
            bias[a] = jnp.where(seen, jnp.inf, NEG_FILL)

    def attend_suffix(side, h):
        attend(
            h, [(a, i) for a in range(2) for i in range(group_size)], 2 * tokens,
            lambda: skv[side, h].reshape(2 * tokens, pair), side == 0, (bias[0], bias[1]),
        )

    def attend_prefix(part):
        unit = part // 2
        h = unit // (per_head // 2)
        a = lax.rem(part + 1 + c, 2)
        attend(
            h, [(a, i) for i in range(group_size)], 4 * rows,
            lambda: kv[pl.ds(2 * unit, 2)].reshape(4 * rows, pair), False, None,
        )

        @pl.when(lax.rem(unit, per_head // 2) == per_head // 2 - 1)
        def _():
            def ratio(i):
                at = (h * 2 + a) * group_size + i
                return (acc[at] / l_ref[at]).astype(out.dtype)

            @pl.when(a != c)
            def _():
                for i in range(group_size):
                    spare[h, :, i * HEAD : (i + 1) * HEAD] = ratio(i)
                out_copy(h).start()

            @pl.when(a == c)
            def _():
                for i in range(group_size):
                    col = ((c * mine + h) * group_size + i) * HEAD
                    out[:, pl.ds(pl.multiple_of(col, HEAD), HEAD)] = ratio(i)

    depth = SKEW * jnp.maximum(z, 3 - z)
    lag = 2 + 2 * x
    is_mine = (owner_mine == z).astype(jnp.int32)
    from_left = (owner_mine < z).astype(jnp.int32)
    in_lane_1 = (want == 1).astype(jnp.int32)

    def sent_on(lane):
        if lanes == 1:
            return ((owner_0 == z) | (owner_1 == z)).astype(jnp.int32)
        return ((owner_0, owner_1)[lane] == z).astype(jnp.int32)

    @pl.when(mid)
    def _():
        want_copy(jnp.where(z == 1, 0, 3)).wait_recv()

    edge_want = jnp.max(wanted[...])
    edge_owned = (jnp.where(edge_want == 1, owner_1, owner_0) == z).astype(jnp.int32)

    set_bias(0)

    def step(i, carry):
        k_right = i - SKEW * z

        @pl.when(mid & (k_right >= 0) & (k_right < chunks))
        def _():
            k = k_right

            @pl.when(z == 1)
            def _():
                right(0, k).wait_recv()
                for lane in range(lanes):
                    right_out[lane, k] = choose(sent_on(lane), own[k], right_in[0, k])
                    right(lane, k).start()

            @pl.when(z == 2)
            def _():
                for lane in range(lanes):
                    right(lane, k).wait_recv()
                got = right_in[0, k]
                if lanes > 1:
                    got = choose(edge_want, right_in[1, k], got)
                right_out[0, k] = choose(edge_owned, own[k], got)
                right(0, k).start()

        k_left = i - SKEW * (3 - z)

        @pl.when(mid & (k_left >= 0) & (k_left < chunks))
        def _():
            k = k_left

            @pl.when(z == 2)
            def _():
                left(0, k).wait_recv()
                for lane in range(lanes):
                    left_out[lane, k] = choose(sent_on(lane), own[k], left_in[0, k])
                    left(lane, k).start()

            @pl.when(z == 1)
            def _():
                for lane in range(lanes):
                    left(lane, k).wait_recv()
                got = left_in[0, k]
                if lanes > 1:
                    got = choose(edge_want, left_in[1, k], got)
                left_out[0, k] = choose(edge_owned, own[k], got)
                left(0, k).start()

        k_mine = i - depth

        @pl.when((k_mine >= 0) & (k_mine < chunks))
        def _():
            k = k_mine

            @pl.when(z == 0)
            def _():
                left(0, k).wait_recv()
                kv[k, 0] = choose(is_mine, own[k], left_in[0, k])

            @pl.when(z == 3)
            def _():
                right(0, k).wait_recv()
                kv[k, 0] = choose(is_mine, own[k], right_in[0, k])

            @pl.when(z == 1)
            def _():
                came = left_in[0, k]
                if lanes > 1:
                    came = choose(in_lane_1, left_in[1, k], came)
                came = choose(from_left, right_in[0, k], came)
                kv[k, 0] = choose(is_mine, own[k], came)

            @pl.when(z == 2)
            def _():
                came = right_in[0, k]
                if lanes > 1:
                    came = choose(in_lane_1, right_in[1, k], came)
                came = choose(from_left, came, left_in[0, k])
                kv[k, 0] = choose(is_mine, own[k], came)

            cross(k).start()

        h_near = i - SKEW

        @pl.when((h_near >= 0) & (h_near < mine))
        def _():
            attend_suffix(0, h_near)

        h_far = i - 5

        @pl.when((x == 1) & (h_far == 0))
        def _():
            seg_cross().wait_recv()
            set_bias(1)

        @pl.when((x == 1) & (h_far >= 0) & (h_far < mine))
        def _():
            suffix_cross(h_far).wait_recv()
            attend_suffix(1, h_far)

        part = i - depth - lag

        @pl.when((part >= 0) & (part < chunks))
        def _():
            @pl.when(lax.rem(part, 2) == 0)
            def _():
                cross(part).wait_recv()
                cross(part + 1).wait_recv()

            attend_prefix(part)

        return carry

    lax.fori_loop(0, chunks + depth + lag, step, 0)

    for h in range(mine):
        out_copy(h).wait_recv()
        out_copy(h).wait_send()
        suffix_copy(h).wait_send()
    seg_copy().wait_send()
    query_copy().wait_send()

    @pl.when(x == 0)
    def _():
        seg_cross().wait_send()
        for h in range(mine):
            suffix_cross(h).wait_send()

    @pl.loop(0, mine * half)
    def _(e):
        mate_copy(e).wait_send()

    @pl.when((z == 0) | (z == 3))
    def _():
        want_copy(jnp.where(z == 0, 1, 2)).wait_send()

    @pl.loop(0, chunks)
    def _(k):
        cross(k).wait_send()

        @pl.when(z < 3)
        def _():
            right(0, k).wait_send()

        @pl.when(z > 0)
        def _():
            left(0, k).wait_send()

        if lanes > 1:
            @pl.when(z == 1)
            def _():
                right(1, k).wait_send()

            @pl.when(z == 2)
            def _():
                left(1, k).wait_send()


def fused(lanes, owner, group_of, pages, queries, suffix, seg_row, pool):
    tokens, width = queries.shape
    heads = suffix.shape[1] // (2 * HEAD)
    mine = heads // 2
    q_heads = width // HEAD
    chunks = 2 * pages.shape[1] * pool.shape[1] // tokens * mine
    piece = (tokens, 2 * HEAD)
    count = 4 * tokens
    vmem, smem = pl.BlockSpec(memory_space=pltpu.VMEM), pl.BlockSpec(memory_space=pltpu.SMEM)
    far = pl.BlockSpec(memory_space=pl.ANY)
    dma = pltpu.SemaphoreType.DMA
    bf16, f32, i32 = jnp.bfloat16, jnp.float32, jnp.int32
    return pl.pallas_call(
        functools.partial(fused_kernel, lanes, heads, q_heads // heads),
        out_shape=jax.ShapeDtypeStruct((tokens, width), bf16),
        in_specs=[smem] * 3 + [far, far, vmem, far],
        out_specs=vmem,
        scratch_shapes=[
            pltpu.VMEM((chunks,) + piece, bf16),
            pltpu.VMEM((chunks // 2,) + piece, bf16),
            pltpu.VMEM((2, 2, 8, tokens), i32),
            pltpu.VMEM((2, tokens, HEAD), i32),
            pltpu.VMEM((8, HEAD), i32),
            pltpu.VMEM((8, HEAD), i32),
        ]
        + [pltpu.VMEM((lanes, chunks) + piece, bf16)] * 4
        + [
            pltpu.VMEM((chunks, 2) + piece, bf16),
            pltpu.VMEM((2, mine, 2) + piece, bf16),
            pltpu.VMEM((2, tokens, width // 2), bf16),
            pltpu.VMEM((2, tokens, 2 * tokens), f32),
        ]
        + [pltpu.VMEM((tokens, count), f32)] * 2
        + [pltpu.VMEM((tokens, count), bf16)] * 2
        + [pltpu.VMEM((tokens, HEAD), f32)] * 2
        + [pltpu.VMEM((q_heads, tokens, HEAD), f32)] * 3
        + [
            pltpu.VMEM((mine, tokens, width // heads), bf16),
        ]
        + [pltpu.VMEM(pool.shape[:2] + (2 * HEAD,), bf16)] * heads
        + [dma((3 * mine + 1,))]
        + [dma((lanes, chunks))] * 4
        + [dma((chunks,))] * 2
        + [dma((chunks // 2,))] * 2
        + [dma] * 2
        + [dma((mine,))] * 4
        + [dma((2,))] * 2
        + [dma] * 2
        + [dma((mine,))] * 2,
        compiler_params=pltpu.CompilerParams(
            collective_id=lanes, has_side_effects=True, vmem_limit_bytes=58 << 20
        ),
    )(owner, group_of, pages, queries, suffix, seg_row, pool)


def pipeline(tiles, count, query, block, mask, place, state, buffers, init):
    m_ref, l_ref, acc = state
    scores, weights, factors = buffers
    rows = factors[0].shape[0]

    def multiply(t):
        scores[t % 2][:, :count] = lax.dot_general(
            query(tiles[t]), block(tiles[t])[:, :HEAD],
            (((1,), (1,)), ((), ())), preferred_element_type=jnp.float32,
        )

    def soften(t):
        sc = scores[t % 2][:, :count]
        if mask is not None:
            sc = jnp.minimum(sc, mask(tiles[t]))
        at = place(tiles[t])
        top = jnp.broadcast_to(jnp.max(sc, axis=1, keepdims=True), (rows, HEAD))
        if not init:
            old = m_ref[at]
            top = jnp.maximum(old, top)
            factors[t % 2][...] = jnp.exp2((old - top) * EXP2_SCALE)
        m_ref[at] = top
        w = jnp.exp2((sc - top[:, :1]) * EXP2_SCALE)
        weights[t % 2][:, :count] = w.astype(jnp.bfloat16)

    def gather(t):
        at = place(tiles[t])
        values = jnp.concatenate(
            [block(tiles[t])[:, HEAD:], jnp.ones((count, HEAD), jnp.bfloat16)], axis=1
        )
        add = jnp.dot(weights[t % 2][:, :count], values, preferred_element_type=jnp.float32)
        if init:
            acc[at] = add[:, :HEAD]
            l_ref[at] = add[:, HEAD:]
        else:
            factor = factors[t % 2][...]
            acc[at] = acc[at] * factor + add[:, :HEAD]
            l_ref[at] = l_ref[at] * factor + add[:, HEAD:]

    multiply(0)
    for t in range(len(tiles)):
        if t + 1 < len(tiles):
            multiply(t + 1)
        if t > 0:
            gather(t - 1)
        soften(t)
    gather(len(tiles) - 1)


def moved_kernel(
    flip, heads, group_size,
    owner, group_of, pages, queries, suffix, seg_row, pool,
    out,
    kv, mate, sg, qseg, wants, wanted, skv, qs, bias,
    down_in, down_out, up_q, slots, made, up_in, up_out, back, fin,
    made_ml, up_in_ml, up_out_ml, back_ml, fin_ml,
    score_0, score_1, weight_0, weight_1, factor_0, factor_1,
    m_ref, l_ref, acc, m_job, l_job, acc_job, spare,
    pages_0, pages_1, pages_2, pages_3, sem_load,
    sem_x_s, sem_x_r, sem_mate_s, sem_mate_r, sem_q_s, sem_q_r, sem_skv_s, sem_skv_r,
    sem_xskv_s, sem_xskv_r, sem_sg_s, sem_sg_r, sem_want_s, sem_want_r,
    sem_out_s, sem_out_r, sem_down_s, sem_down_r, sem_upq_s, sem_upq_r,
    sem_up_s, sem_up_r, sem_upml_s, sem_upml_r, sem_back_s, sem_back_r,
    sem_backml_s, sem_backml_r,
):
    z = lax.axis_index("group")
    s = lax.axis_index("seq")
    x = s // 2
    c = lax.rem(s, 2)
    p = 3 - z if flip else z
    toward = -1 if flip else 1
    up = lax.rem(z + toward + 4, 4)
    down = lax.rem(z - toward + 4, 4)
    serves = p < 2
    chunks = kv.shape[1]
    rows = kv.shape[2]
    mine = heads // 2
    tokens = queries.shape[0]
    wide = group_size * HEAD
    pair = 2 * HEAD
    partner = s + 1 - 2 * c
    across = lax.rem(s + 2, 4)
    per_head = chunks // mine
    half = per_head // 2
    jobs = 4 * mine

    owner_0, owner_1, want = owner[0], owner[1], group_of[0]

    pages_in = (pages_0, pages_1, pages_2, pages_3)
    barrier = pltpu.get_barrier_semaphore()
    for there in (partner, across):
        pl.semaphore_signal(barrier, inc=1, device_id={"seq": there}, device_id_type=MESH)
    for k in range(1, 4):
        pl.semaphore_signal(
            barrier, inc=1, device_id={"group": lax.rem(z + k, 4)}, device_id_type=MESH
        )

    wants[...] = jnp.broadcast_to(want, wants.shape)
    wanted[z] = jnp.broadcast_to(want, wants.shape)
    sg[0, c] = jnp.broadcast_to(seg_row[...], sg.shape[2:])

    def query_columns(core, h):
        return pl.ds(pl.multiple_of((core * mine + h) * wide, HEAD), wide)

    def columns(core, h):
        return pl.ds(pl.multiple_of((core * mine + h) * pair, pair), pair)

    def load_pages(e):
        core = c if e < mine else 1 - c
        return pltpu.make_async_copy(
            pool.at[:, :, columns(core, e % mine)], pages_in[e], sem_load.at[e]
        )

    def load_suffix(h):
        return pltpu.make_async_copy(
            suffix.at[:, columns(c, h)], skv.at[0, h, c], sem_load.at[2 * mine + h]
        )

    def load_queries(h):
        return pltpu.make_async_copy(
            queries.at[:, query_columns(c, h)], qs.at[h * 2 + c], sem_load.at[3 * mine + h]
        )

    @pl.when(serves)
    def _():
        load_pages(0).start()

    for h in range(mine):
        load_queries(h).start()
    for h in range(mine):
        load_suffix(h).start()

    @pl.when(serves)
    def _():
        for h in range(mine):
            load_pages(mine + h).start()
            if h + 1 < mine:
                load_pages(h + 1).start()

    owned = jnp.where(owner_1 == z, 1, 0)
    page = pool.shape[1]
    in_part = rows // page

    def place_pages(e):
        load_pages(e).wait()

        @pl.loop(0, pages.shape[1])
        def _(j):
            place = pl.ds(pl.multiple_of(lax.rem(j, in_part) * page, page), page)
            rows_now = pages_in[e][pages[owned, j]]
            if e < mine:
                kv[0, e * per_head + j // in_part, place, :] = rows_now
            else:
                mate[(e - mine) * half + j // in_part, place, :] = rows_now

    @pl.when(serves)
    def _():
        place_pages(0)

    pl.semaphore_wait(barrier, 5)

    def move(src, dst, send, recv, axis, there):
        return pltpu.make_async_remote_copy(
            src_ref=src, dst_ref=dst, send_sem=send, recv_sem=recv,
            device_id={axis: there}, device_id_type=MESH,
        )

    def cross(k):
        return move(kv.at[0, k], kv.at[1, k], sem_x_s.at[k], sem_x_r.at[k], "seq", across)

    def mate_copy(e):
        to = e // half * per_head + half + lax.rem(e, half)
        return move(
            mate.at[e], kv.at[0, to], sem_mate_s.at[e], sem_mate_r.at[e], "seq", partner
        )

    def query_copy(h):
        return move(
            queries.at[:, query_columns(1 - c, h)], qs.at[h * 2 + c],
            sem_q_s.at[h], sem_q_r.at[h], "seq", partner,
        )

    def suffix_copy(h):
        return move(
            suffix.at[:, columns(1 - c, h)], skv.at[0, h, c],
            sem_skv_s.at[h], sem_skv_r.at[h], "seq", partner,
        )

    def suffix_cross(h):
        return move(
            skv.at[0, h], skv.at[1, h], sem_xskv_s.at[h], sem_xskv_r.at[h], "seq", across
        )

    def seg_copy():
        return move(sg.at[0, c], sg.at[0, c], sem_sg_s.at[0], sem_sg_r.at[0], "seq", partner)

    def seg_cross():
        return move(sg.at[0], sg.at[1], sem_sg_s.at[1], sem_sg_r.at[1], "seq", across)

    def want_copy(k, origin):
        return move(
            wants, wanted.at[origin], sem_want_s.at[k - 1], sem_want_r.at[origin],
            "group", lax.rem(z + k, 4),
        )

    def out_copy(h):
        return move(
            spare.at[h], out.at[:, query_columns(c, h)],
            sem_out_s.at[h], sem_out_r.at[h], "seq", partner,
        )

    def send_down(lane, e, src):
        return move(
            src, down_in.at[lane, e], sem_down_s.at[lane, e], sem_down_r.at[lane, e],
            "group", down,
        )

    def send_up_q(e):
        return move(qs.at[e], up_q.at[e], sem_upq_s.at[e], sem_upq_r.at[e], "group", up)

    def send_up(lane, f, src):
        return move(
            src.at[lane, f], up_in.at[lane, f], sem_up_s.at[lane, f], sem_up_r.at[lane, f],
            "group", up,
        )

    def send_up_ml(lane, e, src):
        return move(
            src.at[lane, e], up_in_ml.at[lane, e], sem_upml_s.at[lane, e],
            sem_upml_r.at[lane, e], "group", up,
        )

    def send_back(f):
        return move(made.at[0, f], back.at[f], sem_back_s.at[f], sem_back_r.at[f], "group", down)

    def send_back_ml(e):
        return move(
            made_ml.at[0, e], back_ml.at[e], sem_backml_s.at[e], sem_backml_r.at[e],
            "group", down,
        )

    for k in range(1, 4):
        want_copy(k, z).start()
    seg_copy().start()
    for h in range(mine):
        query_copy(h).start()
    for h in range(mine):
        suffix_copy(h).start()

    @pl.when(serves)
    def _():
        @pl.loop(0, half)
        def _(k):
            cross(k).start()

        for h in range(mine):
            place_pages(mine + h)

            @pl.loop(h * half, (h + 1) * half)
            def _(e):
                mate_copy(e).start()

        for h in range(1, mine):
            place_pages(h)

    for h in range(mine):
        load_queries(h).wait()
        query_copy(h).wait_recv()

    @pl.when(p == 3)
    def _():
        for e in range(2 * mine):
            send_down(1, e, qs.at[e]).start()

    @pl.when(p == 2)
    def _():
        for e in range(2):
            send_down(0, e, qs.at[e]).start()

    @pl.when(p == 0)
    def _():
        for e in range(2 * mine):
            send_up_q(e).start()

    seg_copy().wait_recv()
    for h in range(mine):
        load_suffix(h).wait()
        suffix_copy(h).wait_recv()

    @pl.when(serves)
    def _():
        @pl.loop(0, mine * half)
        def _(e):
            mate_copy(e).wait_recv()

        @pl.loop(half, chunks)
        def _(k):
            cross(k).start()

    @pl.when(x == 0)
    def _():
        seg_cross().start()
        for h in range(mine):
            suffix_cross(h).start()

    for a in range(2):
        qseg[a] = jnp.broadcast_to(sg[0, a, :1, :], (HEAD, tokens)).T

    for k in range(1, 4):
        want_copy(k, lax.rem(z + k, 4)).wait_recv()
    at_0, at_1 = (3 - owner_0, 3 - owner_1) if flip else (owner_0, owner_1)
    served = [
        jnp.where(jnp.max(wanted[3 - q if flip else q]) == 1, at_1, at_0) for q in range(4)
    ]

    def by(server, q):
        return (served[q] == server).astype(jnp.int32)

    split = (served[2] != served[3]).astype(jnp.int32)

    buffers = ((score_0, score_1), (weight_0, weight_1), (factor_0, factor_1))

    def set_bias(side):
        for a in range(2):
            k_seg = jnp.concatenate([sg[side, b, :1, :] for b in range(2)], axis=1)
            seen = k_seg == qseg[a][:, :1]
            if side == 0:
                q_off = a * tokens + lax.broadcasted_iota(jnp.int32, seen.shape, 0)
                seen = seen & (lax.broadcasted_iota(jnp.int32, seen.shape, 1) <= q_off)
            bias[a] = jnp.where(seen, jnp.inf, NEG_FILL)

    def attend_suffix(side, h):
        pipeline(
            [(a, i) for a in range(2) for i in range(group_size)], 2 * tokens,
            lambda t: qs[h * 2 + t[0], :, t[1] * HEAD : (t[1] + 1) * HEAD],
            lambda t: skv[side, h].reshape(2 * tokens, pair),
            lambda t: bias[t[0]],
            lambda t: (h * 2 + t[0]) * group_size + t[1],
            (m_ref, l_ref, acc), buffers, side == 0,
        )

    def event_1(b):
        e = b // 4 * 2 + lax.rem(b, 2)

        @pl.when(lax.rem(b // 2, 2) == 0)
        def _():
            send_down(0, e, down_out.at[0, e]).wait_recv()
            send_up_q(e).wait_recv()
            down_out[0, e] = choose(by(0, 1), qs[e], down_in[0, e])
            send_down(0, e, down_out.at[0, e]).start()
            rest = choose(by(1, 1), qs[e], down_in[0, e])
            slots[0, e] = choose(by(1, 0), up_q[e], rest)

        @pl.when(lax.rem(b // 2, 2) == 1)
        def _():
            send_down(1, e, down_out.at[1, e]).wait_recv()
            rest = choose(by(0, 2), down_in[0, e], qs[e])
            down_out[1, e] = choose(by(0, 3), down_in[1, e], rest)
            send_down(1, e, down_out.at[1, e]).start()
            rest = choose(by(1, 2), down_in[0, e], qs[e])
            slots[1, e] = choose(by(1, 3), down_in[1, e], rest)

    def event_0(b):
        e = b // 4 * 2 + lax.rem(b, 2)

        @pl.when(lax.rem(b // 2, 2) == 0)
        def _():
            send_down(0, e, down_out.at[0, e]).wait_recv()
            slots[0, e] = choose(by(0, 0), qs[e], down_in[0, e])

        @pl.when(lax.rem(b // 2, 2) == 1)
        def _():
            send_down(1, e, down_out.at[1, e]).wait_recv()
            slots[1, e] = down_in[1, e]

    def relay_q(e):
        send_down(1, e, down_in.at[1, e]).wait_recv()
        send_down(1, e, down_in.at[1, e]).start()

    def relay_1(e):
        for f in range(2):
            send_up(0, 2 * e + f, up_out).wait_recv()
        send_up_ml(0, e, up_out_ml).wait_recv()
        for f in range(2):
            rest = choose(by(1, 2), made[0, 2 * e + f], up_in[0, 2 * e + f])
            up_out[0, 2 * e + f] = choose(split, made[1, 2 * e + f], rest)
            send_up(0, 2 * e + f, up_out).start()
        rest = choose(by(1, 2), made_ml[0, e], up_in_ml[0, e])
        up_out_ml[0, e] = choose(split, made_ml[1, e], rest)
        send_up_ml(0, e, up_out_ml).start()

    local_3 = (1 - split) * by(1, 3)

    def relay_2(e):
        for f in range(2):
            send_up(1, 2 * e + f, up_out).wait_recv()
            up_out[1, 2 * e + f] = choose(local_3, made[1, 2 * e + f], up_in[1, 2 * e + f])
            send_up(1, 2 * e + f, up_out).start()
        send_up_ml(1, e, up_out_ml).wait_recv()
        up_out_ml[1, e] = choose(local_3, made_ml[1, e], up_in_ml[1, e])
        send_up_ml(1, e, up_out_ml).start()

    def finish(b, h, j, a):
        e = h * 2 + a
        lane = lax.broadcasted_iota(jnp.int32, (tokens, HEAD), 1)
        packed = jnp.zeros((tokens, HEAD), jnp.float32)
        for i in range(group_size):
            at = i % 2 * HEAD
            tile = a * group_size + i
            ratio = acc_job[tile] / l_job[tile]
            made[j, 2 * e + i // 2, :, at : at + HEAD] = ratio.astype(made.dtype)
            packed = jnp.where(lane == i, m_job[tile], packed)
            packed = jnp.where(lane == group_size + i, l_job[tile], packed)
        made_ml[j, e] = packed.T[:8]

        @pl.when(p == 0)
        def _():
            for f in range(2):
                send_up(j, 2 * e + f, made).start()
            send_up_ml(j, e, made_ml).start()

        @pl.when((p == 1) & (j == 0))
        def _():
            for f in range(2):
                send_back(2 * e + f).start()
            send_back_ml(e).start()

        @pl.when((p == 1) & (j == 1))
        def _():
            relay_1(e)

        @pl.when((p == 1) & (h == 1) & (j == 0))
        def _():
            relay_2(a)

    def serve(n, carry):
        h, r = n // 8, lax.rem(n, 8)
        j = r // 4
        early = (h == 0) & (j == 0)
        a = jnp.where(early, lax.rem(r, 2), lax.rem(r // 2, 2))
        v = jnp.where(early, r // 2, lax.rem(r, 2))
        e = h * 2 + a
        b = h * 4 + j * 2 + a

        @pl.when((p == 0) & (v == 0))
        def _():
            event_0(b)

        for at, due in ((1, 1), (2, 2), (3, 3), (5, 4), (6, 5), (8, 6), (9, 7)):
            @pl.when((p == 1) & (n == at))
            def _():
                event_1(jnp.int32(due))

        @pl.when((v == 1) & (j == 0) & (a == 0))
        def _():
            for k in range(per_head):
                cross(h * per_head + k).wait_recv()

        own_tiles = pl.ds(a * group_size, group_size)

        @pl.when(v == 0)
        def _():
            shape = (group_size,) + m_job.shape[1:]
            m_job[own_tiles] = jnp.full(shape, NEG_FILL, jnp.float32)
            l_job[own_tiles] = jnp.zeros(shape, jnp.float32)
            acc_job[own_tiles] = jnp.zeros(shape, jnp.float32)

        pipeline(
            [(g, i) for g in range(2) for i in range(group_size)], half * rows,
            lambda t: slots[j, e, :, t[1] * HEAD : (t[1] + 1) * HEAD],
            lambda t: kv[v, pl.ds(h * per_head + t[0] * half, half)].reshape(half * rows, pair),
            None, lambda t: a * group_size + t[1], (m_job, l_job, acc_job), buffers, False,
        )

        @pl.when(v == 1)
        def _():
            finish(b, h, j, a)

        return carry

    def merge(e):
        h, a = e // 2, e % 2
        ml = jnp.concatenate([fin_ml[e]] * (HEAD // 8), axis=0).T

        def ratio(i):
            at = e * group_size + i
            lane = i % 2 * HEAD
            near = m_ref[at]
            far = jnp.broadcast_to(ml[:, i : i + 1], (tokens, HEAD))
            top = jnp.maximum(near, far)
            keep = jnp.exp2((near - top) * EXP2_SCALE)
            total = jnp.broadcast_to(
                ml[:, group_size + i : group_size + i + 1], (tokens, HEAD)
            ) * jnp.exp2((far - top) * EXP2_SCALE)
            context = fin[2 * e + i // 2, :, lane : lane + HEAD].astype(jnp.float32)
            both = context * total + acc[at] * keep
            return (both / (total + l_ref[at] * keep)).astype(out.dtype)

        @pl.when(a != c)
        def _():
            for i in range(group_size):
                spare[h, :, i * HEAD : (i + 1) * HEAD] = ratio(i)
            out_copy(h).start()

        @pl.when(a == c)
        def _():
            for i in range(group_size):
                col = ((c * mine + h) * group_size + i) * HEAD
                out[:, pl.ds(pl.multiple_of(col, HEAD), HEAD)] = ratio(i)

    set_bias(0)

    @pl.loop(0, mine)
    def _(h):
        attend_suffix(0, h)

        @pl.when(p == 2)
        def _():
            relay_q(h)

    @pl.when(p == 2)
    def _():
        for e in range(2, 2 * mine):
            send_down(0, e, qs.at[e]).start()

    @pl.when(p == 1)
    def _():
        event_1(jnp.int32(0))

    lax.fori_loop(0, jnp.where(serves, 2 * jobs, 0), serve, 0)

    @pl.when(p == 1)
    def _():
        relay_2(2)

    @pl.when(x == 1)
    def _():
        seg_cross().wait_recv()
        set_bias(1)

    @pl.loop(0, mine)
    def _(h):
        @pl.when(x == 1)
        def _():
            suffix_cross(h).wait_recv()
            attend_suffix(1, h)

        @pl.when(p == 2)
        def _():
            relay_q(2 + h)

    @pl.when(p == 1)
    def _():
        relay_2(3)

    for e in range(2 * mine):
        both = (2 * e, 2 * e + 1)

        @pl.when(p == 0)
        def _():
            for f in both:
                send_back(f).wait_recv()
                fin[f] = choose(by(0, 0), made[0, f], back[f])
            send_back_ml(e).wait_recv()
            fin_ml[e] = choose(by(0, 0), made_ml[0, e], back_ml[e])

        @pl.when(p == 1)
        def _():
            def pick(have, came, at):
                here = choose(by(1, 0), have[1, at], have[0, at])
                there = choose(by(0, 0), came[1, at], came[0, at])
                return choose(by(1, 1), here, there)

            for f in both:
                fin[f] = pick(made, up_in, f)
            fin_ml[e] = pick(made_ml, up_in_ml, e)

        @pl.when(p == 2)
        def _():
            late_2 = split * by(0, 2)
            early_3 = split * by(1, 3)
            for f in both:
                send_up(0, f, up_out).wait_recv()
                send_up(1, f, up_out).wait_recv()
                up_out[1, f] = choose(early_3, up_in[0, f], up_in[1, f])
                send_up(1, f, up_out).start()
                fin[f] = choose(late_2, up_in[1, f], up_in[0, f])
            send_up_ml(0, e, up_out_ml).wait_recv()
            send_up_ml(1, e, up_out_ml).wait_recv()
            up_out_ml[1, e] = choose(early_3, up_in_ml[0, e], up_in_ml[1, e])
            send_up_ml(1, e, up_out_ml).start()
            fin_ml[e] = choose(late_2, up_in_ml[1, e], up_in_ml[0, e])

        @pl.when(p == 3)
        def _():
            for f in both:
                send_up(1, f, up_out).wait_recv()
                fin[f] = up_in[1, f]
            send_up_ml(1, e, up_out_ml).wait_recv()
            fin_ml[e] = up_in_ml[1, e]

        merge(e)

    for k in range(1, 4):
        want_copy(k, z).wait_send()
    for h in range(mine):
        out_copy(h).wait_recv()
        out_copy(h).wait_send()
        suffix_copy(h).wait_send()
        query_copy(h).wait_send()
    seg_copy().wait_send()

    @pl.when(x == 0)
    def _():
        seg_cross().wait_send()
        for h in range(mine):
            suffix_cross(h).wait_send()

    @pl.when(serves)
    def _():
        @pl.loop(0, mine * half)
        def _(e):
            mate_copy(e).wait_send()

        @pl.loop(0, chunks)
        def _(k):
            cross(k).wait_send()

    for e in range(2 * mine):
        @pl.when((p == 1) | (p == 2))
        def _():
            send_down(0, e, qs.at[e]).wait_send()

        @pl.when(p > 0)
        def _():
            send_down(1, e, qs.at[e]).wait_send()

        @pl.when(p < 2)
        def _():
            send_up_ml(0, e, up_out_ml).wait_send()
            for f in range(2):
                send_up(0, 2 * e + f, up_out).wait_send()

        @pl.when(p < 3)
        def _():
            send_up_ml(1, e, up_out_ml).wait_send()
            for f in range(2):
                send_up(1, 2 * e + f, up_out).wait_send()

        @pl.when(p == 0)
        def _():
            send_up_q(e).wait_send()

        @pl.when(p == 1)
        def _():
            send_back_ml(e).wait_send()
            for f in range(2):
                send_back(2 * e + f).wait_send()


def moved(flip, owner, group_of, pages, queries, suffix, seg_row, pool):
    tokens, width = queries.shape
    heads = suffix.shape[1] // (2 * HEAD)
    mine = heads // 2
    q_heads = width // HEAD
    group_size = q_heads // heads
    chunks = 2 * pages.shape[1] * pool.shape[1] // tokens * mine
    piece = (tokens, 2 * HEAD)
    query = (tokens, group_size * HEAD)
    count = 4 * tokens
    vmem, smem = pl.BlockSpec(memory_space=pltpu.VMEM), pl.BlockSpec(memory_space=pltpu.SMEM)
    far = pl.BlockSpec(memory_space=pl.ANY)
    dma = pltpu.SemaphoreType.DMA
    bf16, f32, i32 = jnp.bfloat16, jnp.float32, jnp.int32
    parts = 2 * mine
    return pl.pallas_call(
        functools.partial(moved_kernel, flip, heads, group_size),
        out_shape=jax.ShapeDtypeStruct((tokens, width), bf16),
        in_specs=[smem] * 3 + [far, far, vmem, far],
        out_specs=vmem,
        scratch_shapes=[
            pltpu.VMEM((2, chunks) + piece, bf16),
            pltpu.VMEM((chunks // 2,) + piece, bf16),
            pltpu.VMEM((2, 2, 8, tokens), i32),
            pltpu.VMEM((2, tokens, HEAD), i32),
            pltpu.VMEM((8, HEAD), i32),
            pltpu.VMEM((4, 8, HEAD), i32),
            pltpu.VMEM((2, mine, 2) + piece, bf16),
            pltpu.VMEM((parts,) + query, bf16),
            pltpu.VMEM((2, tokens, 2 * tokens), f32),
        ]
        + [pltpu.VMEM((2, parts) + query, bf16)] * 2
        + [
            pltpu.VMEM((parts,) + query, bf16),
            pltpu.VMEM((2, parts) + query, bf16),
        ]
        + [pltpu.VMEM((2, 2 * parts) + piece, bf16)] * 3
        + [pltpu.VMEM((2 * parts,) + piece, bf16)] * 2
        + [pltpu.VMEM((2, parts, 8, tokens), f32)] * 3
        + [pltpu.VMEM((parts, 8, tokens), f32)] * 2
        + [pltpu.VMEM((tokens, count), f32)] * 2
        + [pltpu.VMEM((tokens, count), bf16)] * 2
        + [pltpu.VMEM((tokens, HEAD), f32)] * 2
        + [pltpu.VMEM((q_heads, tokens, HEAD), f32)] * 3
        + [pltpu.VMEM((2 * group_size, tokens, HEAD), f32)] * 3
        + [
            pltpu.VMEM((mine,) + query, bf16),
        ]
        + [pltpu.VMEM(pool.shape[:2] + (2 * HEAD,), bf16)] * heads
        + [dma((4 * mine,))]
        + [dma((chunks,))] * 2
        + [dma((chunks // 2,))] * 2
        + [dma((mine,))] * 6
        + [dma((2,))] * 2
        + [dma((3,)), dma((4,))]
        + [dma((mine,))] * 2
        + [dma((2, parts))] * 2
        + [dma((parts,))] * 2
        + [dma((2, 2 * parts))] * 2
        + [dma((2, parts))] * 2
        + [dma((2 * parts,))] * 2
        + [dma((parts,))] * 2,
        compiler_params=pltpu.CompilerParams(
            collective_id=2 + flip, has_side_effects=True, vmem_limit_bytes=58 << 20
        ),
    )(owner, group_of, pages, queries, suffix, seg_row, pool)


def local_fused(queries, suffix_kv, suffix_seg, prefix_pool, page_table, owner, group_of):
    args = (owner, group_of, page_table, queries[0], suffix_kv[0], suffix_seg, prefix_pool[0])
    low = (owner < 2).astype(jnp.int32)
    plans = [
        functools.partial(moved, 1), functools.partial(fused, 1), functools.partial(moved, 0)
    ]
    return lax.switch(low[0] + low[1], plans, *args)[None]


def fits(mesh):
    return dict(mesh.shape) == {"group": 4, "seq": 4, "tensor": 2}


def solution(mesh):
    return jax.shard_map(
        local_fused if fits(mesh) else local,
        mesh=mesh,
        in_specs=(
            P("group", "seq", "tensor"),
            P("group", "seq", "tensor"),
            P("group", "seq"),
            P("group", "seq", None, "tensor"),
            P(None, "seq"),
            P(),
            P("group"),
        ),
        out_specs=P("group", "seq", "tensor"),
        check_vma=False,
    )
```

```python
import functools
import math

import jax
import jax.numpy as jnp
from jax import lax
from jax.experimental import pallas as pl
from jax.experimental.pallas import tpu as pltpu
from jax.sharding import PartitionSpec as P

HEAD = 128


NEG_FILL = -1e30


def broadcast(value, axis, root):
    mine = lax.axis_index(axis) == root
    return lax.psum(jnp.where(mine, value, jnp.zeros_like(value)), axis)


def absorb(carried, query_rows, key_block, valid):
    running_max, running_sum, accumulator = carried
    scale = 1.0 / math.sqrt(HEAD)
    key_rows = key_block[:, :, 0, :]
    value_rows = key_block[:, :, 1, :]
    scores = (
        jnp.einsum("thgd,khd->htgk", query_rows, key_rows, preferred_element_type=jnp.float32)
        * scale
    )
    if valid is not None:
        scores = jnp.where(valid[None, :, None, :], scores, NEG_FILL)
    new_max = jnp.maximum(running_max, jnp.max(scores, axis=-1, keepdims=True))
    weight = jnp.exp(scores - new_max)
    if valid is not None:
        weight = jnp.where(valid[None, :, None, :], weight, 0.0)
    factor = jnp.exp(running_max - new_max)
    running_sum = running_sum * factor + jnp.sum(weight, axis=-1, keepdims=True)
    accumulator = accumulator * factor + jnp.einsum(
        "htgk,khd->htgd",
        weight.astype(jnp.bfloat16),
        value_rows,
        preferred_element_type=jnp.float32,
    )
    return (new_max, running_sum, accumulator)


def sweep(carried, query_rows, kv_rows, mask_for):
    row_count = kv_rows.shape[0]
    block_rows = math.gcd(row_count, 1024)
    head_count = kv_rows.shape[1] // (2 * HEAD)

    def absorb_block(block_index, state_now):
        offset = block_index * block_rows
        key_block = lax.dynamic_slice_in_dim(kv_rows, offset, block_rows, 0).reshape(
            block_rows, head_count, 2, HEAD
        )
        return absorb(state_now, query_rows, key_block, mask_for(offset, block_rows))

    if row_count == block_rows:
        return absorb_block(0, carried)
    return lax.fori_loop(0, row_count // block_rows, absorb_block, carried)


def combine(earlier, later):
    new_max = jnp.maximum(earlier[0], later[0])
    scale_first = jnp.exp(earlier[0] - new_max)
    scale_second = jnp.exp(later[0] - new_max)
    return (
        new_max,
        earlier[1] * scale_first + later[1] * scale_second,
        earlier[2] * scale_first + later[2] * scale_second,
    )


def no_mask(offset, block_rows):
    return None


def local(queries, suffix_kv, suffix_seg, prefix_pool, page_table, owner, group_of):
    tokens = queries.shape[1]
    row_width = suffix_kv.shape[-1]
    head_count = row_width // (2 * HEAD)
    group_size = queries.shape[-1] // (head_count * HEAD)
    query_rows = queries[0].reshape(tokens, head_count, group_size, HEAD)
    page_pool = prefix_pool[0]
    my_group = group_of[0]
    held_shape = (page_table.shape[1] * page_pool.shape[1], row_width)

    def compact(slot_ids):
        def put(j, rows):
            page = lax.dynamic_slice_in_dim(page_pool, slot_ids[j], 1, 0)
            return lax.dynamic_update_slice_in_dim(rows, page, j, 0)

        count = slot_ids.shape[0]
        rows = jnp.zeros((count,) + page_pool.shape[1:], page_pool.dtype)
        return lax.fori_loop(0, count, put, rows).reshape(-1, row_width)

    def visit_group(request, held_pages):
        moved_pages = broadcast(compact(page_table[request]), "group", owner[request])
        return jnp.where(request == my_group, moved_pages, held_pages)

    prefix_rows = lax.fori_loop(
        0, page_table.shape[0], visit_group, jnp.zeros(held_shape, jnp.bfloat16)
    )
    fresh_state = (
        jnp.full((head_count, tokens, group_size, 1), NEG_FILL, jnp.float32),
        jnp.zeros((head_count, tokens, group_size, 1), jnp.float32),
        jnp.zeros((head_count, tokens, group_size, HEAD), jnp.float32),
    )
    before = sweep(
        fresh_state, query_rows, lax.all_gather(prefix_rows, "seq", axis=0, tiled=True), no_mask
    )
    first_row = lax.axis_index("seq") * tokens
    query_pos = first_row + jnp.arange(tokens, dtype=jnp.int32)
    query_seg = suffix_seg[0]
    first_index = jnp.int32(0)
    kv_rows = lax.all_gather(suffix_kv[0], "seq", axis=0, tiled=True)
    key_segments = lax.all_gather(suffix_seg[0], "seq", axis=0, tiled=True)

    def mask_for(offset, block_rows):
        block_seg = lax.dynamic_slice_in_dim(key_segments, offset, block_rows, 0)
        key_pos = first_index + offset + jnp.arange(block_rows, dtype=jnp.int32)
        return (block_seg[None, :] == query_seg[:, None]) & (key_pos[None, :] <= query_pos[:, None])

    combined = sweep(fresh_state, query_rows, kv_rows, mask_for)
    final_state = combine(before, combined)
    outcome = final_state[2] / final_state[1]
    return outcome.transpose(1, 0, 2, 3).reshape(1, tokens, -1).astype(jnp.bfloat16)

MESH = pl.DeviceIdType.MESH
SKEW = 2
EXP2_SCALE = math.log2(math.e) / math.sqrt(HEAD)


def choose(flag, first, second):
    return lax.select(flag != 0, first, second)


def fused_kernel(
    lanes, heads, group_size,
    owner, group_of, pages, queries, suffix, seg_row, pool,
    out,
    own, mate, sg, qseg, wants, wanted,
    right_in, left_in, right_out, left_out, kv, skv, qs, bias,
    score_0, score_1, weight_0, weight_1, factor_0, factor_1,
    m_ref, l_ref, acc, spare,
    pages_0, pages_1, pages_2, pages_3, sem_load,
    sem_right_s, sem_right_r, sem_left_s, sem_left_r, sem_x_s, sem_x_r,
    sem_mate_s, sem_mate_r, sem_q_s, sem_q_r, sem_skv_s, sem_skv_r,
    sem_xskv_s, sem_xskv_r, sem_sg_s, sem_sg_r, sem_want_s, sem_want_r,
    sem_out_s, sem_out_r,
):
    z = lax.axis_index("group")
    s = lax.axis_index("seq")
    x = s // 2
    c = lax.rem(s, 2)
    chunks, rows = own.shape[:2]
    mine = heads // 2
    tokens = queries.shape[0]
    width = mine * group_size * HEAD
    pair = 2 * HEAD
    partner = s + 1 - 2 * c
    across = lax.rem(s + 2, 4)
    mid = (z == 1) | (z == 2)
    per_head = chunks // mine
    half = per_head // 2

    owner_0, owner_1, want = owner[0], owner[1], group_of[0]
    owner_mine = jnp.where(want == 1, owner_1, owner_0)

    wanted[...] = jnp.zeros_like(wanted)
    pages_in = (pages_0, pages_1, pages_2, pages_3)
    barrier = pltpu.get_barrier_semaphore()
    for there in (partner, across):
        pl.semaphore_signal(barrier, inc=1, device_id={"seq": there}, device_id_type=MESH)

    @pl.when(z > 0)
    def _():
        pl.semaphore_signal(barrier, inc=1, device_id={"group": z - 1}, device_id_type=MESH)

    @pl.when(z < 3)
    def _():
        pl.semaphore_signal(barrier, inc=1, device_id={"group": z + 1}, device_id_type=MESH)

    wants[...] = jnp.broadcast_to(want, wants.shape)
    sg[0, c] = jnp.broadcast_to(seg_row[...], sg.shape[2:])

    owned = jnp.where(owner_1 == z, 1, 0)
    page = pool.shape[1]
    in_part = rows // page

    def columns(core, h):
        return pl.ds(pl.multiple_of((core * mine + h) * pair, pair), pair)

    def load_pages(e):
        core = c if e < mine else 1 - c
        return pltpu.make_async_copy(
            pool.at[:, :, columns(core, e % mine)], pages_in[e], sem_load.at[e]
        )

    def load_suffix(h):
        return pltpu.make_async_copy(
            suffix.at[:, columns(c, h)], skv.at[0, h, c], sem_load.at[2 * mine + h]
        )

    def load_queries():
        cols = pl.ds(pl.multiple_of(c * width, HEAD), width)
        return pltpu.make_async_copy(queries.at[:, cols], qs.at[c], sem_load.at[3 * mine])

    def place_pages(e):
        load_pages(e).wait()
        first = e * per_head if e < mine else (e - mine) * half
        into = own if e < mine else mate

        @pl.loop(0, pages.shape[1])
        def _(j):
            place = pl.ds(pl.multiple_of(lax.rem(j, in_part) * page, page), page)
            into[first + j // in_part, place, :] = pages_in[e][pages[owned, j]]

    load_pages(0).start()
    for h in range(mine):
        load_suffix(h).start()
    load_queries().start()
    for h in range(mine):
        load_pages(mine + h).start()
        if h + 1 < mine:
            load_pages(h + 1).start()
    place_pages(0)

    pl.semaphore_wait(barrier, jnp.where(mid, 4, 3))

    def move(src, dst, send, recv, axis, there):
        return pltpu.make_async_remote_copy(
            src_ref=src, dst_ref=dst, send_sem=send, recv_sem=recv,
            device_id={axis: there}, device_id_type=MESH,
        )

    def right(lane, k, src=None):
        return move(
            right_out.at[lane, k] if src is None else src, right_in.at[lane, k],
            sem_right_s.at[lane, k], sem_right_r.at[lane, k], "group", lax.rem(z + 1, 4),
        )

    def left(lane, k, src=None):
        return move(
            left_out.at[lane, k] if src is None else src, left_in.at[lane, k],
            sem_left_s.at[lane, k], sem_left_r.at[lane, k], "group", lax.rem(z + 3, 4),
        )

    def cross(k):
        return move(kv.at[k, 0], kv.at[k, 1], sem_x_s.at[k], sem_x_r.at[k], "seq", across)

    def mate_copy(e):
        to = e // half * per_head + half + lax.rem(e, half)
        return move(
            mate.at[e], own.at[to], sem_mate_s.at[e], sem_mate_r.at[e], "seq", partner
        )

    def query_copy():
        cols = pl.ds(pl.multiple_of((1 - c) * width, HEAD), width)
        return move(queries.at[:, cols], qs.at[c], sem_q_s, sem_q_r, "seq", partner)

    def suffix_copy(h):
        return move(
            suffix.at[:, columns(1 - c, h)], skv.at[0, h, c],
            sem_skv_s.at[h], sem_skv_r.at[h], "seq", partner,
        )

    def suffix_cross(h):
        return move(
            skv.at[0, h], skv.at[1, h], sem_xskv_s.at[h], sem_xskv_r.at[h], "seq", across
        )

    def seg_copy():
        return move(sg.at[0, c], sg.at[0, c], sem_sg_s.at[0], sem_sg_r.at[0], "seq", partner)

    def seg_cross():
        return move(sg.at[0], sg.at[1], sem_sg_s.at[1], sem_sg_r.at[1], "seq", across)

    def want_copy(there):
        return move(wants, wanted, sem_want_s, sem_want_r, "group", there)

    def out_copy(h):
        cols = pl.ds(
            pl.multiple_of((c * mine + h) * group_size * HEAD, HEAD), group_size * HEAD
        )
        return move(
            spare.at[h], out.at[:, cols], sem_out_s.at[h], sem_out_r.at[h], "seq", partner
        )

    def from_edge(first, last):
        @pl.when(z == 0)
        def _():
            @pl.loop(first, last)
            def _(k):
                right(0, k, own.at[k]).start()

        @pl.when(z == 3)
        def _():
            @pl.loop(first, last)
            def _(k):
                left(0, k, own.at[k]).start()

    @pl.when((z == 0) | (z == 3))
    def _():
        want_copy(jnp.where(z == 0, 1, 2)).start()

    from_edge(0, half)
    seg_copy().start()
    for h in range(mine):
        suffix_copy(h).start()
    query_copy().start()

    for h in range(mine):
        place_pages(mine + h)

        @pl.loop(h * half, (h + 1) * half)
        def _(e):
            mate_copy(e).start()

    seg_copy().wait_recv()
    for h in range(mine):
        load_suffix(h).wait()
        suffix_copy(h).wait_recv()

    @pl.when(x == 0)
    def _():
        seg_cross().start()
        for h in range(mine):
            suffix_cross(h).start()

    for h in range(1, mine):
        place_pages(h)

    @pl.loop(0, mine * half)
    def _(e):
        mate_copy(e).wait_recv()

    from_edge(half, chunks)
    for a in range(2):
        qseg[a] = jnp.broadcast_to(sg[0, a, :1, :], (HEAD, tokens)).T
    load_queries().wait()
    query_copy().wait_recv()

    scores, weights, factors = (
        (score_0, score_1), (weight_0, weight_1), (factor_0, factor_1)
    )

    def attend(h, tiles, count, block, init, masks):
        def place(tile):
            return (h * 2 + tile[0]) * group_size + tile[1]

        def multiply(t):
            a, i = tiles[t]
            col = pl.multiple_of((h * group_size + i) * HEAD, HEAD)
            scores[t % 2][:, :count] = lax.dot_general(
                qs[a, :, pl.ds(col, HEAD)], block()[:, :HEAD],
                (((1,), (1,)), ((), ())), preferred_element_type=jnp.float32,
            )

        def soften(t):
            sc = scores[t % 2][:, :count]
            if masks is not None:
                sc = jnp.minimum(sc, masks[tiles[t][0]])
            at = place(tiles[t])
            top = jnp.broadcast_to(jnp.max(sc, axis=1, keepdims=True), (tokens, HEAD))
            if not init:
                old = m_ref[at]
                top = jnp.maximum(old, top)
                factors[t % 2][...] = jnp.exp2((old - top) * EXP2_SCALE)
            m_ref[at] = top
            w = jnp.exp2((sc - top[:, :1]) * EXP2_SCALE)
            weights[t % 2][:, :count] = w.astype(jnp.bfloat16)

        def gather(t):
            at = place(tiles[t])
            values = jnp.concatenate(
                [block()[:, HEAD:], jnp.ones((count, HEAD), jnp.bfloat16)], axis=1
            )
            add = jnp.dot(
                weights[t % 2][:, :count], values, preferred_element_type=jnp.float32
            )
            if init:
                acc[at] = add[:, :HEAD]
                l_ref[at] = add[:, HEAD:]
            else:
                factor = factors[t % 2][...]
                acc[at] = acc[at] * factor + add[:, :HEAD]
                l_ref[at] = l_ref[at] * factor + add[:, HEAD:]

        multiply(0)
        for t in range(len(tiles)):
            if t + 1 < len(tiles):
                multiply(t + 1)
            if t > 0:
                gather(t - 1)
            soften(t)
        gather(len(tiles) - 1)

    def set_bias(side):
        for a in range(2):
            k_seg = jnp.concatenate([sg[side, b, :1, :] for b in range(2)], axis=1)
            seen = k_seg == qseg[a][:, :1]
            if side == 0:
                q_off = a * tokens + lax.broadcasted_iota(jnp.int32, seen.shape, 0)
                seen = seen & (lax.broadcasted_iota(jnp.int32, seen.shape, 1) <= q_off)
            bias[a] = jnp.where(seen, jnp.inf, NEG_FILL)

    def attend_suffix(side, h):
        attend(
            h, [(a, i) for a in range(2) for i in range(group_size)], 2 * tokens,
            lambda: skv[side, h].reshape(2 * tokens, pair), side == 0, (bias[0], bias[1]),
        )

    def attend_prefix(part):
        unit = part // 2
        h = unit // (per_head // 2)
        a = lax.rem(part + 1 + c, 2)
        attend(
            h, [(a, i) for i in range(group_size)], 4 * rows,
            lambda: kv[pl.ds(2 * unit, 2)].reshape(4 * rows, pair), False, None,
        )

        @pl.when(lax.rem(unit, per_head // 2) == per_head // 2 - 1)
        def _():
            def ratio(i):
                at = (h * 2 + a) * group_size + i
                return (acc[at] / l_ref[at]).astype(out.dtype)

            @pl.when(a != c)
            def _():
                for i in range(group_size):
                    spare[h, :, i * HEAD : (i + 1) * HEAD] = ratio(i)
                out_copy(h).start()

            @pl.when(a == c)
            def _():
                for i in range(group_size):
                    col = ((c * mine + h) * group_size + i) * HEAD
                    out[:, pl.ds(pl.multiple_of(col, HEAD), HEAD)] = ratio(i)

    depth = SKEW * jnp.maximum(z, 3 - z)
    lag = 2 + 2 * x
    is_mine = (owner_mine == z).astype(jnp.int32)
    from_left = (owner_mine < z).astype(jnp.int32)
    in_lane_1 = (want == 1).astype(jnp.int32)

    def sent_on(lane):
        if lanes == 1:
            return ((owner_0 == z) | (owner_1 == z)).astype(jnp.int32)
        return ((owner_0, owner_1)[lane] == z).astype(jnp.int32)

    @pl.when(mid)
    def _():
        want_copy(jnp.where(z == 1, 0, 3)).wait_recv()

    edge_want = jnp.max(wanted[...])
    edge_owned = (jnp.where(edge_want == 1, owner_1, owner_0) == z).astype(jnp.int32)

    set_bias(0)

    def step(i, carry):
        k_right = i - SKEW * z

        @pl.when(mid & (k_right >= 0) & (k_right < chunks))
        def _():
            k = k_right

            @pl.when(z == 1)
            def _():
                right(0, k).wait_recv()
                for lane in range(lanes):
                    right_out[lane, k] = choose(sent_on(lane), own[k], right_in[0, k])
                    right(lane, k).start()

            @pl.when(z == 2)
            def _():
                for lane in range(lanes):
                    right(lane, k).wait_recv()
                got = right_in[0, k]
                if lanes > 1:
                    got = choose(edge_want, right_in[1, k], got)
                right_out[0, k] = choose(edge_owned, own[k], got)
                right(0, k).start()

        k_left = i - SKEW * (3 - z)

        @pl.when(mid & (k_left >= 0) & (k_left < chunks))
        def _():
            k = k_left

            @pl.when(z == 2)
            def _():
                left(0, k).wait_recv()
                for lane in range(lanes):
                    left_out[lane, k] = choose(sent_on(lane), own[k], left_in[0, k])
                    left(lane, k).start()

            @pl.when(z == 1)
            def _():
                for lane in range(lanes):
                    left(lane, k).wait_recv()
                got = left_in[0, k]
                if lanes > 1:
                    got = choose(edge_want, left_in[1, k], got)
                left_out[0, k] = choose(edge_owned, own[k], got)
                left(0, k).start()

        k_mine = i - depth

        @pl.when((k_mine >= 0) & (k_mine < chunks))
        def _():
            k = k_mine

            @pl.when(z == 0)
            def _():
                left(0, k).wait_recv()
                kv[k, 0] = choose(is_mine, own[k], left_in[0, k])

            @pl.when(z == 3)
            def _():
                right(0, k).wait_recv()
                kv[k, 0] = choose(is_mine, own[k], right_in[0, k])

            @pl.when(z == 1)
            def _():
                came = left_in[0, k]
                if lanes > 1:
                    came = choose(in_lane_1, left_in[1, k], came)
                came = choose(from_left, right_in[0, k], came)
                kv[k, 0] = choose(is_mine, own[k], came)

            @pl.when(z == 2)
            def _():
                came = right_in[0, k]
                if lanes > 1:
                    came = choose(in_lane_1, right_in[1, k], came)
                came = choose(from_left, came, left_in[0, k])
                kv[k, 0] = choose(is_mine, own[k], came)

            cross(k).start()

        h_near = i - SKEW

        @pl.when((h_near >= 0) & (h_near < mine))
        def _():
            attend_suffix(0, h_near)

        h_far = i - 5

        @pl.when((x == 1) & (h_far == 0))
        def _():
            seg_cross().wait_recv()
            set_bias(1)

        @pl.when((x == 1) & (h_far >= 0) & (h_far < mine))
        def _():
            suffix_cross(h_far).wait_recv()
            attend_suffix(1, h_far)

        part = i - depth - lag

        @pl.when((part >= 0) & (part < chunks))
        def _():
            @pl.when(lax.rem(part, 2) == 0)
            def _():
                cross(part).wait_recv()
                cross(part + 1).wait_recv()

            attend_prefix(part)

        return carry

    lax.fori_loop(0, chunks + depth + lag, step, 0)

    for h in range(mine):
        out_copy(h).wait_recv()
        out_copy(h).wait_send()
        suffix_copy(h).wait_send()
    seg_copy().wait_send()
    query_copy().wait_send()

    @pl.when(x == 0)
    def _():
        seg_cross().wait_send()
        for h in range(mine):
            suffix_cross(h).wait_send()

    @pl.loop(0, mine * half)
    def _(e):
        mate_copy(e).wait_send()

    @pl.when((z == 0) | (z == 3))
    def _():
        want_copy(jnp.where(z == 0, 1, 2)).wait_send()

    @pl.loop(0, chunks)
    def _(k):
        cross(k).wait_send()

        @pl.when(z < 3)
        def _():
            right(0, k).wait_send()

        @pl.when(z > 0)
        def _():
            left(0, k).wait_send()

        if lanes > 1:
            @pl.when(z == 1)
            def _():
                right(1, k).wait_send()

            @pl.when(z == 2)
            def _():
                left(1, k).wait_send()


def fused(lanes, owner, group_of, pages, queries, suffix, seg_row, pool):
    tokens, width = queries.shape
    heads = suffix.shape[1] // (2 * HEAD)
    mine = heads // 2
    q_heads = width // HEAD
    chunks = 2 * pages.shape[1] * pool.shape[1] // tokens * mine
    piece = (tokens, 2 * HEAD)
    count = 4 * tokens
    vmem, smem = pl.BlockSpec(memory_space=pltpu.VMEM), pl.BlockSpec(memory_space=pltpu.SMEM)
    far = pl.BlockSpec(memory_space=pl.ANY)
    dma = pltpu.SemaphoreType.DMA
    bf16, f32, i32 = jnp.bfloat16, jnp.float32, jnp.int32
    return pl.pallas_call(
        functools.partial(fused_kernel, lanes, heads, q_heads // heads),
        out_shape=jax.ShapeDtypeStruct((tokens, width), bf16),
        in_specs=[smem] * 3 + [far, far, vmem, far],
        out_specs=vmem,
        scratch_shapes=[
            pltpu.VMEM((chunks,) + piece, bf16),
            pltpu.VMEM((chunks // 2,) + piece, bf16),
            pltpu.VMEM((2, 2, 8, tokens), i32),
            pltpu.VMEM((2, tokens, HEAD), i32),
            pltpu.VMEM((8, HEAD), i32),
            pltpu.VMEM((8, HEAD), i32),
        ]
        + [pltpu.VMEM((lanes, chunks) + piece, bf16)] * 4
        + [
            pltpu.VMEM((chunks, 2) + piece, bf16),
            pltpu.VMEM((2, mine, 2) + piece, bf16),
            pltpu.VMEM((2, tokens, width // 2), bf16),
            pltpu.VMEM((2, tokens, 2 * tokens), f32),
        ]
        + [pltpu.VMEM((tokens, count), f32)] * 2
        + [pltpu.VMEM((tokens, count), bf16)] * 2
        + [pltpu.VMEM((tokens, HEAD), f32)] * 2
        + [pltpu.VMEM((q_heads, tokens, HEAD), f32)] * 3
        + [
            pltpu.VMEM((mine, tokens, width // heads), bf16),
        ]
        + [pltpu.VMEM(pool.shape[:2] + (2 * HEAD,), bf16)] * heads
        + [dma((3 * mine + 1,))]
        + [dma((lanes, chunks))] * 4
        + [dma((chunks,))] * 2
        + [dma((chunks // 2,))] * 2
        + [dma] * 2
        + [dma((mine,))] * 4
        + [dma((2,))] * 2
        + [dma] * 2
        + [dma((mine,))] * 2,
        compiler_params=pltpu.CompilerParams(
            collective_id=lanes, has_side_effects=True, vmem_limit_bytes=58 << 20
        ),
    )(owner, group_of, pages, queries, suffix, seg_row, pool)


def pipeline(tiles, count, query, block, mask, place, state, buffers, init):
    m_ref, l_ref, acc = state
    scores, weights, factors = buffers
    rows = factors[0].shape[0]

    def multiply(t):
        scores[t % 2][:, :count] = lax.dot_general(
            query(tiles[t]), block(tiles[t])[:, :HEAD],
            (((1,), (1,)), ((), ())), preferred_element_type=jnp.float32,
        )

    def soften(t):
        sc = scores[t % 2][:, :count]
        if mask is not None:
            sc = jnp.minimum(sc, mask(tiles[t]))
        at = place(tiles[t])
        top = jnp.broadcast_to(jnp.max(sc, axis=1, keepdims=True), (rows, HEAD))
        if not init:
            old = m_ref[at]
            top = jnp.maximum(old, top)
            factors[t % 2][...] = jnp.exp2((old - top) * EXP2_SCALE)
        m_ref[at] = top
        w = jnp.exp2((sc - top[:, :1]) * EXP2_SCALE)
        weights[t % 2][:, :count] = w.astype(jnp.bfloat16)

    def gather(t):
        at = place(tiles[t])
        values = jnp.concatenate(
            [block(tiles[t])[:, HEAD:], jnp.ones((count, HEAD), jnp.bfloat16)], axis=1
        )
        add = jnp.dot(weights[t % 2][:, :count], values, preferred_element_type=jnp.float32)
        if init:
            acc[at] = add[:, :HEAD]
            l_ref[at] = add[:, HEAD:]
        else:
            factor = factors[t % 2][...]
            acc[at] = acc[at] * factor + add[:, :HEAD]
            l_ref[at] = l_ref[at] * factor + add[:, HEAD:]

    multiply(0)
    for t in range(len(tiles)):
        if t + 1 < len(tiles):
            multiply(t + 1)
        if t > 0:
            gather(t - 1)
        soften(t)
    gather(len(tiles) - 1)


def moved_kernel(
    flip, heads, group_size,
    owner, group_of, pages, queries, suffix, seg_row, pool,
    out,
    kv, mate, sg, qseg, wants, wanted, skv, qs, bias,
    down_in, down_out, up_q, slots, made, up_in, up_out, back, fin,
    made_ml, up_in_ml, up_out_ml, back_ml, fin_ml,
    score_0, score_1, weight_0, weight_1, factor_0, factor_1,
    m_ref, l_ref, acc, m_job, l_job, acc_job, spare,
    pages_0, pages_1, pages_2, pages_3, sem_load,
    sem_x_s, sem_x_r, sem_mate_s, sem_mate_r, sem_q_s, sem_q_r, sem_skv_s, sem_skv_r,
    sem_xskv_s, sem_xskv_r, sem_sg_s, sem_sg_r, sem_want_s, sem_want_r,
    sem_out_s, sem_out_r, sem_down_s, sem_down_r, sem_upq_s, sem_upq_r,
    sem_up_s, sem_up_r, sem_upml_s, sem_upml_r, sem_back_s, sem_back_r,
    sem_backml_s, sem_backml_r,
):
    z = lax.axis_index("group")
    s = lax.axis_index("seq")
    x = s // 2
    c = lax.rem(s, 2)
    p = 3 - z if flip else z
    toward = -1 if flip else 1
    up = lax.rem(z + toward + 4, 4)
    down = lax.rem(z - toward + 4, 4)
    serves = p < 2
    chunks = kv.shape[1]
    rows = kv.shape[2]
    mine = heads // 2
    tokens = queries.shape[0]
    wide = group_size * HEAD
    pair = 2 * HEAD
    partner = s + 1 - 2 * c
    across = lax.rem(s + 2, 4)
    per_head = chunks // mine
    half = per_head // 2
    jobs = 4 * mine

    owner_0, owner_1, want = owner[0], owner[1], group_of[0]

    pages_in = (pages_0, pages_1, pages_2, pages_3)
    barrier = pltpu.get_barrier_semaphore()
    for there in (partner, across):
        pl.semaphore_signal(barrier, inc=1, device_id={"seq": there}, device_id_type=MESH)
    for k in range(1, 4):
        pl.semaphore_signal(
            barrier, inc=1, device_id={"group": lax.rem(z + k, 4)}, device_id_type=MESH
        )

    wants[...] = jnp.broadcast_to(want, wants.shape)
    wanted[z] = jnp.broadcast_to(want, wants.shape)
    sg[0, c] = jnp.broadcast_to(seg_row[...], sg.shape[2:])

    def query_columns(core, h):
        return pl.ds(pl.multiple_of((core * mine + h) * wide, HEAD), wide)

    def columns(core, h):
        return pl.ds(pl.multiple_of((core * mine + h) * pair, pair), pair)

    def load_pages(e):
        core = c if e < mine else 1 - c
        return pltpu.make_async_copy(
            pool.at[:, :, columns(core, e % mine)], pages_in[e], sem_load.at[e]
        )

    def load_suffix(h):
        return pltpu.make_async_copy(
            suffix.at[:, columns(c, h)], skv.at[0, h, c], sem_load.at[2 * mine + h]
        )

    def load_queries(h):
        return pltpu.make_async_copy(
            queries.at[:, query_columns(c, h)], qs.at[h * 2 + c], sem_load.at[3 * mine + h]
        )

    @pl.when(serves)
    def _():
        load_pages(0).start()

    for h in range(mine):
        load_queries(h).start()
    for h in range(mine):
        load_suffix(h).start()

    @pl.when(serves)
    def _():
        for h in range(mine):
            load_pages(mine + h).start()
            if h + 1 < mine:
                load_pages(h + 1).start()

    owned = jnp.where(owner_1 == z, 1, 0)
    page = pool.shape[1]
    in_part = rows // page

    def place_pages(e):
        load_pages(e).wait()

        @pl.loop(0, pages.shape[1])
        def _(j):
            place = pl.ds(pl.multiple_of(lax.rem(j, in_part) * page, page), page)
            rows_now = pages_in[e][pages[owned, j]]
            if e < mine:
                kv[0, e * per_head + j // in_part, place, :] = rows_now
            else:
                mate[(e - mine) * half + j // in_part, place, :] = rows_now

    @pl.when(serves)
    def _():
        place_pages(0)

    pl.semaphore_wait(barrier, 5)

    def move(src, dst, send, recv, axis, there):
        return pltpu.make_async_remote_copy(
            src_ref=src, dst_ref=dst, send_sem=send, recv_sem=recv,
            device_id={axis: there}, device_id_type=MESH,
        )

    def cross(k):
        return move(kv.at[0, k], kv.at[1, k], sem_x_s.at[k], sem_x_r.at[k], "seq", across)

    def mate_copy(e):
        to = e // half * per_head + half + lax.rem(e, half)
        return move(
            mate.at[e], kv.at[0, to], sem_mate_s.at[e], sem_mate_r.at[e], "seq", partner
        )

    def query_copy(h):
        return move(
            queries.at[:, query_columns(1 - c, h)], qs.at[h * 2 + c],
            sem_q_s.at[h], sem_q_r.at[h], "seq", partner,
        )

    def suffix_copy(h):
        return move(
            suffix.at[:, columns(1 - c, h)], skv.at[0, h, c],
            sem_skv_s.at[h], sem_skv_r.at[h], "seq", partner,
        )

    def suffix_cross(h):
        return move(
            skv.at[0, h], skv.at[1, h], sem_xskv_s.at[h], sem_xskv_r.at[h], "seq", across
        )

    def seg_copy():
        return move(sg.at[0, c], sg.at[0, c], sem_sg_s.at[0], sem_sg_r.at[0], "seq", partner)

    def seg_cross():
        return move(sg.at[0], sg.at[1], sem_sg_s.at[1], sem_sg_r.at[1], "seq", across)

    def want_copy(k, origin):
        return move(
            wants, wanted.at[origin], sem_want_s.at[k - 1], sem_want_r.at[origin],
            "group", lax.rem(z + k, 4),
        )

    def out_copy(h):
        return move(
            spare.at[h], out.at[:, query_columns(c, h)],
            sem_out_s.at[h], sem_out_r.at[h], "seq", partner,
        )

    def send_down(lane, e, src):
        return move(
            src, down_in.at[lane, e], sem_down_s.at[lane, e], sem_down_r.at[lane, e],
            "group", down,
        )

    def send_up_q(e):
        return move(qs.at[e], up_q.at[e], sem_upq_s.at[e], sem_upq_r.at[e], "group", up)

    def send_up(lane, f, src):
        return move(
            src.at[lane, f], up_in.at[lane, f], sem_up_s.at[lane, f], sem_up_r.at[lane, f],
            "group", up,
        )

    def send_up_ml(lane, e, src):
        return move(
            src.at[lane, e], up_in_ml.at[lane, e], sem_upml_s.at[lane, e],
            sem_upml_r.at[lane, e], "group", up,
        )

    def send_back(f):
        return move(made.at[0, f], back.at[f], sem_back_s.at[f], sem_back_r.at[f], "group", down)

    def send_back_ml(e):
        return move(
            made_ml.at[0, e], back_ml.at[e], sem_backml_s.at[e], sem_backml_r.at[e],
            "group", down,
        )

    for k in range(1, 4):
        want_copy(k, z).start()
    seg_copy().start()
    for h in range(mine):
        query_copy(h).start()
    for h in range(mine):
        suffix_copy(h).start()

    @pl.when(serves)
    def _():
        @pl.loop(0, half)
        def _(k):
            cross(k).start()

        for h in range(mine):
            place_pages(mine + h)

            @pl.loop(h * half, (h + 1) * half)
            def _(e):
                mate_copy(e).start()

        for h in range(1, mine):
            place_pages(h)

    for h in range(mine):
        load_queries(h).wait()
        query_copy(h).wait_recv()

    @pl.when(p == 3)
    def _():
        for e in range(2 * mine):
            send_down(1, e, qs.at[e]).start()

    @pl.when(p == 2)
    def _():
        for e in range(2):
            send_down(0, e, qs.at[e]).start()

    @pl.when(p == 0)
    def _():
        for e in range(2 * mine):
            send_up_q(e).start()

    seg_copy().wait_recv()
    for h in range(mine):
        load_suffix(h).wait()
        suffix_copy(h).wait_recv()

    @pl.when(serves)
    def _():
        @pl.loop(0, mine * half)
        def _(e):
            mate_copy(e).wait_recv()

        @pl.loop(half, chunks)
        def _(k):
            cross(k).start()

    @pl.when(x == 0)
    def _():
        seg_cross().start()
        for h in range(mine):
            suffix_cross(h).start()

    for a in range(2):
        qseg[a] = jnp.broadcast_to(sg[0, a, :1, :], (HEAD, tokens)).T

    for k in range(1, 4):
        want_copy(k, lax.rem(z + k, 4)).wait_recv()
    at_0, at_1 = (3 - owner_0, 3 - owner_1) if flip else (owner_0, owner_1)
    served = [
        jnp.where(jnp.max(wanted[3 - q if flip else q]) == 1, at_1, at_0) for q in range(4)
    ]

    def by(server, q):
        return (served[q] == server).astype(jnp.int32)

    split = (served[2] != served[3]).astype(jnp.int32)

    buffers = ((score_0, score_1), (weight_0, weight_1), (factor_0, factor_1))

    def set_bias(side):
        for a in range(2):
            k_seg = jnp.concatenate([sg[side, b, :1, :] for b in range(2)], axis=1)
            seen = k_seg == qseg[a][:, :1]
            if side == 0:
                q_off = a * tokens + lax.broadcasted_iota(jnp.int32, seen.shape, 0)
                seen = seen & (lax.broadcasted_iota(jnp.int32, seen.shape, 1) <= q_off)
            bias[a] = jnp.where(seen, jnp.inf, NEG_FILL)

    def attend_suffix(side, h):
        pipeline(
            [(a, i) for a in range(2) for i in range(group_size)], 2 * tokens,
            lambda t: qs[h * 2 + t[0], :, t[1] * HEAD : (t[1] + 1) * HEAD],
            lambda t: skv[side, h].reshape(2 * tokens, pair),
            lambda t: bias[t[0]],
            lambda t: (h * 2 + t[0]) * group_size + t[1],
            (m_ref, l_ref, acc), buffers, side == 0,
        )

    def event_1(b):
        e = b // 4 * 2 + lax.rem(b, 2)

        @pl.when(lax.rem(b // 2, 2) == 0)
        def _():
            send_down(0, e, down_out.at[0, e]).wait_recv()
            send_up_q(e).wait_recv()
            down_out[0, e] = choose(by(0, 1), qs[e], down_in[0, e])
            send_down(0, e, down_out.at[0, e]).start()
            rest = choose(by(1, 1), qs[e], down_in[0, e])
            slots[0, e] = choose(by(1, 0), up_q[e], rest)

        @pl.when(lax.rem(b // 2, 2) == 1)
        def _():
            send_down(1, e, down_out.at[1, e]).wait_recv()
            rest = choose(by(0, 2), down_in[0, e], qs[e])
            down_out[1, e] = choose(by(0, 3), down_in[1, e], rest)
            send_down(1, e, down_out.at[1, e]).start()
            rest = choose(by(1, 2), down_in[0, e], qs[e])
            slots[1, e] = choose(by(1, 3), down_in[1, e], rest)

    def event_0(b):
        e = b // 4 * 2 + lax.rem(b, 2)

        @pl.when(lax.rem(b // 2, 2) == 0)
        def _():
            send_down(0, e, down_out.at[0, e]).wait_recv()
            slots[0, e] = choose(by(0, 0), qs[e], down_in[0, e])

        @pl.when(lax.rem(b // 2, 2) == 1)
        def _():
            send_down(1, e, down_out.at[1, e]).wait_recv()
            slots[1, e] = down_in[1, e]

    def relay_q(e):
        send_down(1, e, down_in.at[1, e]).wait_recv()
        send_down(1, e, down_in.at[1, e]).start()

    def relay_1(e):
        for f in range(2):
            send_up(0, 2 * e + f, up_out).wait_recv()
        send_up_ml(0, e, up_out_ml).wait_recv()
        for f in range(2):
            rest = choose(by(1, 2), made[0, 2 * e + f], up_in[0, 2 * e + f])
            up_out[0, 2 * e + f] = choose(split, made[1, 2 * e + f], rest)
            send_up(0, 2 * e + f, up_out).start()
        rest = choose(by(1, 2), made_ml[0, e], up_in_ml[0, e])
        up_out_ml[0, e] = choose(split, made_ml[1, e], rest)
        send_up_ml(0, e, up_out_ml).start()

    local_3 = (1 - split) * by(1, 3)

    def relay_2(e):
        for f in range(2):
            send_up(1, 2 * e + f, up_out).wait_recv()
            up_out[1, 2 * e + f] = choose(local_3, made[1, 2 * e + f], up_in[1, 2 * e + f])
            send_up(1, 2 * e + f, up_out).start()
        send_up_ml(1, e, up_out_ml).wait_recv()
        up_out_ml[1, e] = choose(local_3, made_ml[1, e], up_in_ml[1, e])
        send_up_ml(1, e, up_out_ml).start()

    def finish(b, h, j, a):
        e = h * 2 + a
        lane = lax.broadcasted_iota(jnp.int32, (tokens, HEAD), 1)
        packed = jnp.zeros((tokens, HEAD), jnp.float32)
        for i in range(group_size):
            at = i % 2 * HEAD
            tile = a * group_size + i
            ratio = acc_job[tile] / l_job[tile]
            made[j, 2 * e + i // 2, :, at : at + HEAD] = ratio.astype(made.dtype)
            packed = jnp.where(lane == i, m_job[tile], packed)
            packed = jnp.where(lane == group_size + i, l_job[tile], packed)
        made_ml[j, e] = packed.T[:8]

        @pl.when(p == 0)
        def _():
            for f in range(2):
                send_up(j, 2 * e + f, made).start()
            send_up_ml(j, e, made_ml).start()

        @pl.when((p == 1) & (j == 0))
        def _():
            for f in range(2):
                send_back(2 * e + f).start()
            send_back_ml(e).start()

        @pl.when((p == 1) & (j == 1))
        def _():
            relay_1(e)

        @pl.when((p == 1) & (h == 1) & (j == 0))
        def _():
            relay_2(a)

    def serve(n, carry):
        h, r = n // 8, lax.rem(n, 8)
        j = r // 4
        early = (h == 0) & (j == 0)
        a = jnp.where(early, lax.rem(r, 2), lax.rem(r // 2, 2))
        v = jnp.where(early, r // 2, lax.rem(r, 2))
        e = h * 2 + a
        b = h * 4 + j * 2 + a

        @pl.when((p == 0) & (v == 0))
        def _():
            event_0(b)

        for at, due in ((1, 1), (2, 2), (3, 3), (5, 4), (6, 5), (8, 6), (9, 7)):
            @pl.when((p == 1) & (n == at))
            def _():
                event_1(jnp.int32(due))

        @pl.when((v == 1) & (j == 0) & (a == 0))
        def _():
            for k in range(per_head):
                cross(h * per_head + k).wait_recv()

        own_tiles = pl.ds(a * group_size, group_size)

        @pl.when(v == 0)
        def _():
            shape = (group_size,) + m_job.shape[1:]
            m_job[own_tiles] = jnp.full(shape, NEG_FILL, jnp.float32)
            l_job[own_tiles] = jnp.zeros(shape, jnp.float32)
            acc_job[own_tiles] = jnp.zeros(shape, jnp.float32)

        pipeline(
            [(g, i) for g in range(2) for i in range(group_size)], half * rows,
            lambda t: slots[j, e, :, t[1] * HEAD : (t[1] + 1) * HEAD],
            lambda t: kv[v, pl.ds(h * per_head + t[0] * half, half)].reshape(half * rows, pair),
            None, lambda t: a * group_size + t[1], (m_job, l_job, acc_job), buffers, False,
        )

        @pl.when(v == 1)
        def _():
            finish(b, h, j, a)

        return carry

    def merge(e):
        h, a = e // 2, e % 2
        ml = jnp.concatenate([fin_ml[e]] * (HEAD // 8), axis=0).T

        def ratio(i):
            at = e * group_size + i
            lane = i % 2 * HEAD
            near = m_ref[at]
            far = jnp.broadcast_to(ml[:, i : i + 1], (tokens, HEAD))
            top = jnp.maximum(near, far)
            keep = jnp.exp2((near - top) * EXP2_SCALE)
            total = jnp.broadcast_to(
                ml[:, group_size + i : group_size + i + 1], (tokens, HEAD)
            ) * jnp.exp2((far - top) * EXP2_SCALE)
            context = fin[2 * e + i // 2, :, lane : lane + HEAD].astype(jnp.float32)
            both = context * total + acc[at] * keep
            return (both / (total + l_ref[at] * keep)).astype(out.dtype)

        @pl.when(a != c)
        def _():
            for i in range(group_size):
                spare[h, :, i * HEAD : (i + 1) * HEAD] = ratio(i)
            out_copy(h).start()

        @pl.when(a == c)
        def _():
            for i in range(group_size):
                col = ((c * mine + h) * group_size + i) * HEAD
                out[:, pl.ds(pl.multiple_of(col, HEAD), HEAD)] = ratio(i)

    set_bias(0)

    @pl.loop(0, mine)
    def _(h):
        attend_suffix(0, h)

        @pl.when(p == 2)
        def _():
            relay_q(h)

    @pl.when(p == 2)
    def _():
        for e in range(2, 2 * mine):
            send_down(0, e, qs.at[e]).start()

    @pl.when(p == 1)
    def _():
        event_1(jnp.int32(0))

    lax.fori_loop(0, jnp.where(serves, 2 * jobs, 0), serve, 0)

    @pl.when(p == 1)
    def _():
        relay_2(2)

    @pl.when(x == 1)
    def _():
        seg_cross().wait_recv()
        set_bias(1)

    @pl.loop(0, mine)
    def _(h):
        @pl.when(x == 1)
        def _():
            suffix_cross(h).wait_recv()
            attend_suffix(1, h)

        @pl.when(p == 2)
        def _():
            relay_q(2 + h)

    @pl.when(p == 1)
    def _():
        relay_2(3)

    for e in range(2 * mine):
        both = (2 * e, 2 * e + 1)

        @pl.when(p == 0)
        def _():
            for f in both:
                send_back(f).wait_recv()
                fin[f] = choose(by(0, 0), made[0, f], back[f])
            send_back_ml(e).wait_recv()
            fin_ml[e] = choose(by(0, 0), made_ml[0, e], back_ml[e])

        @pl.when(p == 1)
        def _():
            def pick(have, came, at):
                here = choose(by(1, 0), have[1, at], have[0, at])
                there = choose(by(0, 0), came[1, at], came[0, at])
                return choose(by(1, 1), here, there)

            for f in both:
                fin[f] = pick(made, up_in, f)
            fin_ml[e] = pick(made_ml, up_in_ml, e)

        @pl.when(p == 2)
        def _():
            late_2 = split * by(0, 2)
            early_3 = split * by(1, 3)
            for f in both:
                send_up(0, f, up_out).wait_recv()
                send_up(1, f, up_out).wait_recv()
                up_out[1, f] = choose(early_3, up_in[0, f], up_in[1, f])
                send_up(1, f, up_out).start()
                fin[f] = choose(late_2, up_in[1, f], up_in[0, f])
            send_up_ml(0, e, up_out_ml).wait_recv()
            send_up_ml(1, e, up_out_ml).wait_recv()
            up_out_ml[1, e] = choose(early_3, up_in_ml[0, e], up_in_ml[1, e])
            send_up_ml(1, e, up_out_ml).start()
            fin_ml[e] = choose(late_2, up_in_ml[1, e], up_in_ml[0, e])

        @pl.when(p == 3)
        def _():
            for f in both:
                send_up(1, f, up_out).wait_recv()
                fin[f] = up_in[1, f]
            send_up_ml(1, e, up_out_ml).wait_recv()
            fin_ml[e] = up_in_ml[1, e]

        merge(e)

    for k in range(1, 4):
        want_copy(k, z).wait_send()
    for h in range(mine):
        out_copy(h).wait_recv()
        out_copy(h).wait_send()
        suffix_copy(h).wait_send()
        query_copy(h).wait_send()
    seg_copy().wait_send()

    @pl.when(x == 0)
    def _():
        seg_cross().wait_send()
        for h in range(mine):
            suffix_cross(h).wait_send()

    @pl.when(serves)
    def _():
        @pl.loop(0, mine * half)
        def _(e):
            mate_copy(e).wait_send()

        @pl.loop(0, chunks)
        def _(k):
            cross(k).wait_send()

    for e in range(2 * mine):
        @pl.when((p == 1) | (p == 2))
        def _():
            send_down(0, e, qs.at[e]).wait_send()

        @pl.when(p > 0)
        def _():
            send_down(1, e, qs.at[e]).wait_send()

        @pl.when(p < 2)
        def _():
            send_up_ml(0, e, up_out_ml).wait_send()
            for f in range(2):
                send_up(0, 2 * e + f, up_out).wait_send()

        @pl.when(p < 3)
        def _():
            send_up_ml(1, e, up_out_ml).wait_send()
            for f in range(2):
                send_up(1, 2 * e + f, up_out).wait_send()

        @pl.when(p == 0)
        def _():
            send_up_q(e).wait_send()

        @pl.when(p == 1)
        def _():
            send_back_ml(e).wait_send()
            for f in range(2):
                send_back(2 * e + f).wait_send()


def moved(flip, owner, group_of, pages, queries, suffix, seg_row, pool):
    tokens, width = queries.shape
    heads = suffix.shape[1] // (2 * HEAD)
    mine = heads // 2
    q_heads = width // HEAD
    group_size = q_heads // heads
    chunks = 2 * pages.shape[1] * pool.shape[1] // tokens * mine
    piece = (tokens, 2 * HEAD)
    query = (tokens, group_size * HEAD)
    count = 4 * tokens
    vmem, smem = pl.BlockSpec(memory_space=pltpu.VMEM), pl.BlockSpec(memory_space=pltpu.SMEM)
    far = pl.BlockSpec(memory_space=pl.ANY)
    dma = pltpu.SemaphoreType.DMA
    bf16, f32, i32 = jnp.bfloat16, jnp.float32, jnp.int32
    parts = 2 * mine
    return pl.pallas_call(
        functools.partial(moved_kernel, flip, heads, group_size),
        out_shape=jax.ShapeDtypeStruct((tokens, width), bf16),
        in_specs=[smem] * 3 + [far, far, vmem, far],
        out_specs=vmem,
        scratch_shapes=[
            pltpu.VMEM((2, chunks) + piece, bf16),
            pltpu.VMEM((chunks // 2,) + piece, bf16),
            pltpu.VMEM((2, 2, 8, tokens), i32),
            pltpu.VMEM((2, tokens, HEAD), i32),
            pltpu.VMEM((8, HEAD), i32),
            pltpu.VMEM((4, 8, HEAD), i32),
            pltpu.VMEM((2, mine, 2) + piece, bf16),
            pltpu.VMEM((parts,) + query, bf16),
            pltpu.VMEM((2, tokens, 2 * tokens), f32),
        ]
        + [pltpu.VMEM((2, parts) + query, bf16)] * 2
        + [
            pltpu.VMEM((parts,) + query, bf16),
            pltpu.VMEM((2, parts) + query, bf16),
        ]
        + [pltpu.VMEM((2, 2 * parts) + piece, bf16)] * 3
        + [pltpu.VMEM((2 * parts,) + piece, bf16)] * 2
        + [pltpu.VMEM((2, parts, 8, tokens), f32)] * 3
        + [pltpu.VMEM((parts, 8, tokens), f32)] * 2
        + [pltpu.VMEM((tokens, count), f32)] * 2
        + [pltpu.VMEM((tokens, count), bf16)] * 2
        + [pltpu.VMEM((tokens, HEAD), f32)] * 2
        + [pltpu.VMEM((q_heads, tokens, HEAD), f32)] * 3
        + [pltpu.VMEM((2 * group_size, tokens, HEAD), f32)] * 3
        + [
            pltpu.VMEM((mine,) + query, bf16),
        ]
        + [pltpu.VMEM(pool.shape[:2] + (2 * HEAD,), bf16)] * heads
        + [dma((4 * mine,))]
        + [dma((chunks,))] * 2
        + [dma((chunks // 2,))] * 2
        + [dma((mine,))] * 6
        + [dma((2,))] * 2
        + [dma((3,)), dma((4,))]
        + [dma((mine,))] * 2
        + [dma((2, parts))] * 2
        + [dma((parts,))] * 2
        + [dma((2, 2 * parts))] * 2
        + [dma((2, parts))] * 2
        + [dma((2 * parts,))] * 2
        + [dma((parts,))] * 2,
        compiler_params=pltpu.CompilerParams(
            collective_id=2 + flip, has_side_effects=True, vmem_limit_bytes=58 << 20
        ),
    )(owner, group_of, pages, queries, suffix, seg_row, pool)


def local_fused(queries, suffix_kv, suffix_seg, prefix_pool, page_table, owner, group_of):
    args = (owner, group_of, page_table, queries[0], suffix_kv[0], suffix_seg, prefix_pool[0])
    low = (owner < 2).astype(jnp.int32)
    plans = [
        functools.partial(moved, 1), functools.partial(fused, 1), functools.partial(moved, 0)
    ]
    return lax.switch(jnp.sum(low), plans, *args)[None]


def fits(mesh):
    return dict(mesh.shape) == {"group": 4, "seq": 4, "tensor": 2}


def solution(mesh):
    return jax.shard_map(
        local_fused if fits(mesh) else local,
        mesh=mesh,
        in_specs=(
            P("group", "seq", "tensor"),
            P("group", "seq", "tensor"),
            P("group", "seq"),
            P("group", "seq", None, "tensor"),
            P(None, "seq"),
            P(),
            P("group"),
        ),
        out_specs=P("group", "seq", "tensor"),
        check_vma=False,
    )
```
